32 devices in a mesh: groups: 1, row: 32 (over z, y, x, core), col: 1.
Axes of the slice: x: 2, y: 2, z: 4, core: 2. Of those that a mesh axis runs over, the one named last changes fastest.
Arguments:
- pair: bfloat16 [128, 128, 128], P(('groups', 'row'), 'col'), may hold values from -6 to 6
- token_mask: int32 [128], P('groups'), may hold values 0 or 1
- tri_in_weight: bfloat16 [128, 512], replicated, may hold values from -0.5 to 0.5
- tri_gate_weight: bfloat16 [128, 128], replicated, may hold values from -0.5 to 0.5
- tri_out_weight: bfloat16 [128, 128], replicated, may hold values from -0.5 to 0.5
- atom_act: bfloat16 [2048, 128], P(('groups', 'row')), may hold values from -6 to 6
- atom_cond: bfloat16 [2048, 128], P(('groups', 'row')), may hold values from -60 to 60
- atom_token: int32 [2048], P(('groups', 'row')), may hold values from 0 to 127, as said below
- atom_mask: int32 [2048], P(('groups', 'row')), may hold values from 0 to 1, as said below
- ada_weight: bfloat16 [128, 256], replicated, may hold values from -0.5 to 0.5
- qkv_weight: bfloat16 [128, 384], replicated, may hold values from -0.5 to 0.5
- bias_weight: bfloat16 [128, 4], replicated, may hold values from -0.5 to 0.5
- attn_out_weight: bfloat16 [128, 128], replicated, may hold values from -0.5 to 0.5
- ffn_in_weight: bfloat16 [128, 512], replicated, may hold values from -0.5 to 0.5
- ffn_out_weight: bfloat16 [256, 128], replicated, may hold values from -0.375 to 0.375
- agg_weight: bfloat16 [128, 384], replicated, may hold values from -0.5 to 0.5
Outputs:
- pair_out: bfloat16 [128, 128, 128], P(('groups', 'row'), 'col')
- atom_out: bfloat16 [2048, 128], P(('groups', 'row'))
- token_out: bfloat16 [128, 384], P(('groups', 'row'))
The draws below stay inside these ranges and needn't reach their ends.
Inputs may be any that keep to these rules, and one draw needn't show every extreme that they name: `atom_token`: Nondecreasing; slots r * 64 to (r + 1) * 64 - 1 hold the atoms of tokens r * 4 to (r + 1) * 4 - 1 followed by padding slots that name the last of those tokens; every token has 1 to 24 atoms. `atom_mask`: in each slab of 64 slots the atoms come first and at most 31 padding slots follow.
All inputs are finite; a program needn't handle non-finite values.
Results may differ from the reference program's by a relative error of at most 0.012.
The reference program's roundings to bfloat16 on the way count: a program that leaves them out, or rounds other values in their place, can miss the bound.
Values may be sent and summed in bfloat16 or wider, within the bound.
No kernel may reach another device: no remote copies, remote signals or barrier semaphores. Data moves between devices by JAX's collectives and lax.ppermute only.
A program may use at most 64 MiB of HBM per device.

```python
import math
import jax
import jax.numpy as jnp
from jax import lax

PAIR_CH = 128
ATOM_CH = 128
SINGLE_CH = 384
HEADS = 4
FFA = 256
QUERY_WINDOW = 32
KEYS = 128
MAXAT = 24
TOK_ROW = 4
N_TOK = 128
ATOM_ROW = 64
ATOMS = 2048
N_ROW = 32


def slab_layout(key):
    devices = ATOMS // ATOM_ROW
    first, second, third, fourth = jax.random.split(jax.random.fold_in(key, 11), 4)
    lowest = ATOM_ROW - QUERY_WINDOW + 1
    totals = jax.random.randint(first, (devices,), lowest, ATOM_ROW + 1)
    fullest = jax.random.randint(second, (), 0, devices)
    totals = jnp.where(jnp.arange(devices) == fullest, ATOM_ROW, totals)
    spare = MAXAT - 1
    slots = TOK_ROW * spare
    owners = jnp.arange(slots) // spare
    favored = jax.random.randint(third, (devices, 1), 0, TOK_ROW)
    noise = jax.random.randint(fourth, (devices, slots), 1, 1 << 20)
    logit_scores = jnp.where(owners[None, :] == favored, 0, noise) * slots + jnp.arange(slots)[None, :]
    ranks = jnp.argsort(jnp.argsort(logit_scores, axis=1), axis=1)
    extra = (totals - TOK_ROW)[:, None]
    chosen = (ranks < extra).astype(jnp.int32)
    counts = 1 + jnp.sum(chosen.reshape(devices, TOK_ROW, spare), axis=2)
    bounds = jnp.cumsum(counts, axis=1)
    position = jnp.arange(ATOM_ROW)
    local = jnp.sum((position[None, :, None] >= bounds[:, None, :]).astype(jnp.int32), axis=2)
    local = jnp.minimum(local, TOK_ROW - 1)
    owner_tokens = jnp.arange(devices)[:, None] * TOK_ROW + local
    live = (position[None, :] < totals[:, None]).astype(jnp.int32)
    return (owner_tokens.reshape(-1).astype(jnp.int32), live.reshape(-1).astype(jnp.int32))


def draw_atom_token(key, part):
    return slab_layout(key)[0]


def draw_atom_mask(key, part):
    return slab_layout(key)[1]


def draw_atom_cond(key, part):
    first = jax.random.fold_in(jax.random.fold_in(key, 23), 0)
    shape = (ATOMS, ATOM_CH)
    values = jax.random.normal(first, shape, jnp.float32)
    return jnp.clip(values, -60.0, 60.0).astype(jnp.bfloat16)


def touch_ends(values, rng, smallest, largest):
    place = [jax.random.randint(jax.random.fold_in(rng, axis), (), 0, length) for axis, length in enumerate(values.shape)]
    main_axis = values.shape.index(max(values.shape))
    neighbour = place[:main_axis] + [(place[main_axis] + 1) % values.shape[main_axis]] + place[main_axis + 1:]
    return values.at[tuple(place)].set(smallest).at[tuple(neighbour)].set(largest)


def shard_levels(key, dims, cuts, low, top_value):
    loudness = 1.0
    for dim, parts in cuts:
        draws = jax.random.uniform(jax.random.fold_in(jax.random.fold_in(key, 6), dim), (parts,), jnp.float32, low / len(cuts), top_value / len(cuts))
        loudness = loudness * jnp.repeat(jnp.exp(draws), dims[dim] // parts).reshape((-1,) + (1,) * (len(dims) - 1 - dim))
    return loudness


def bell_draw(rng, extent, scale, most, pieces=(), kind=jnp.bfloat16):
    drawn = scale * jax.random.normal(rng, extent, jnp.float32)
    if pieces:
        drawn = drawn * shard_levels(rng, extent, pieces, -0.22, 0.18)
    return jnp.clip(drawn, -most, most).astype(kind)


def setup_inputs(seed: int = 0, part: int = 0) -> dict:
    key_of = jax.random.split(jax.random.key(seed), 17)
    own_keys = jax.random.split(jax.random.fold_in(key_of[16], part), 17)
    return {
        "pair": bell_draw(own_keys[0], (N_TOK, N_TOK, PAIR_CH), 1.0, 6.0, ((0, 32),)),
        "token_mask": touch_ends((jax.random.randint(own_keys[1], (N_TOK,), 0, 8) < 7).astype(jnp.int32), jax.random.fold_in(own_keys[1], 1), 0, 1),
        "tri_in_weight": bell_draw(key_of[2], (PAIR_CH, 4 * PAIR_CH), PAIR_CH ** -0.5, 0.5),
        "tri_gate_weight": bell_draw(key_of[3], (PAIR_CH, PAIR_CH), PAIR_CH ** -0.5, 0.5),
        "tri_out_weight": bell_draw(key_of[4], (PAIR_CH, PAIR_CH), PAIR_CH ** -0.5, 0.5),
        "atom_act": bell_draw(own_keys[5], (ATOMS, ATOM_CH), 1.0, 6.0, ((0, 32),)),
        "atom_cond": draw_atom_cond(jax.random.fold_in(jax.random.fold_in(key_of[16], part), 71), part),
        "atom_token": draw_atom_token(jax.random.fold_in(jax.random.fold_in(key_of[16], part), 71), part),
        "atom_mask": draw_atom_mask(jax.random.fold_in(jax.random.fold_in(key_of[16], part), 71), part),
        "ada_weight": bell_draw(key_of[9], (ATOM_CH, 2 * ATOM_CH), ATOM_CH ** -0.5, 0.5),
        "qkv_weight": bell_draw(key_of[10], (ATOM_CH, 3 * ATOM_CH), ATOM_CH ** -0.5, 0.5),
        "bias_weight": bell_draw(key_of[11], (PAIR_CH, HEADS), PAIR_CH ** -0.5, 0.5),
        "attn_out_weight": bell_draw(key_of[12], (ATOM_CH, ATOM_CH), ATOM_CH ** -0.5, 0.5),
        "ffn_in_weight": bell_draw(key_of[13], (ATOM_CH, 2 * FFA), ATOM_CH ** -0.5, 0.5),
        "ffn_out_weight": bell_draw(key_of[14], (FFA, ATOM_CH), FFA ** -0.5, 0.375),
        "agg_weight": bell_draw(key_of[15], (ATOM_CH, SINGLE_CH), ATOM_CH ** -0.5, 0.5),
    }


EPSILON = 1e-05

def layer_norm(values, along):
    average = lax.optimization_barrier(jnp.mean(values, axis=along, keepdims=True))
    centred = values - average
    spread = lax.optimization_barrier(jnp.mean(centred * centred, axis=along, keepdims=True))
    return centred / jnp.sqrt(spread + EPSILON)

def reference(pair, token_mask, tri_in_weight, tri_gate_weight, tri_out_weight, atom_act, atom_cond, atom_token, atom_mask, ada_weight, qkv_weight, bias_weight, attn_out_weight, ffn_in_weight, ffn_out_weight, agg_weight):
    tokens = pair.shape[0]
    channels = pair.shape[2]
    rows = tokens // N_ROW
    token_live = token_mask.astype(jnp.float32)
    in_weight = tri_in_weight.astype(jnp.float32)

    def project_block(index):
        start = index * rows
        block = lax.dynamic_slice_in_dim(pair, start, rows, 0).astype(jnp.float32)
        normed = layer_norm(block, 2).astype(jnp.bfloat16).astype(jnp.float32)
        terms = jnp.einsum('ijd,de->ije', normed, in_weight)
        row_live = lax.dynamic_slice_in_dim(token_live, start, rows, 0)
        both = row_live[:, None, None] * token_live[None, :, None]
        left = (jax.nn.sigmoid(terms[..., channels:2 * channels]) * terms[..., :channels] * both).astype(jnp.bfloat16)
        right = (jax.nn.sigmoid(terms[..., 3 * channels:]) * terms[..., 2 * channels:3 * channels] * both).astype(jnp.bfloat16)
        return (left, right)
    left, right = lax.map(project_block, jnp.arange(N_ROW, dtype=jnp.int32))
    left = left.reshape(tokens, tokens, channels).transpose(2, 0, 1)
    right = right.reshape(tokens, tokens, channels).transpose(2, 0, 1)

    def contract(index):
        return jnp.dot(left[index], right[index].T, preferred_element_type=jnp.float32).astype(jnp.bfloat16)
    product = lax.map(contract, jnp.arange(channels, dtype=jnp.int32))

    def finish_block(index):
        start = index * rows
        block = lax.dynamic_slice_in_dim(pair, start, rows, 0).astype(jnp.float32)
        normed = layer_norm(block, 2).astype(jnp.bfloat16).astype(jnp.float32)
        gate = jax.nn.sigmoid(jnp.einsum('ijd,de->ije', normed, tri_gate_weight.astype(jnp.float32)))
        summed = lax.dynamic_slice_in_dim(product, start, rows, 1).astype(jnp.float32)
        summed_norm = layer_norm(summed, 0).astype(jnp.bfloat16).astype(jnp.float32)
        update = jnp.einsum('dij,de->ije', summed_norm, tri_out_weight.astype(jnp.float32))
        return (block + gate * update).astype(jnp.bfloat16)
    pair_out = lax.map(finish_block, jnp.arange(N_ROW, dtype=jnp.int32)).reshape(tokens, tokens, channels)
    atoms = atom_act.shape[0]
    window_width = atom_act.shape[1]
    head_size = window_width // HEADS
    side = (KEYS - QUERY_WINDOW) // 2
    live = atom_mask.astype(jnp.float32)
    ada = jnp.dot(atom_cond, ada_weight, preferred_element_type=jnp.float32)
    atom_inputs = (jax.nn.sigmoid(ada[:, :window_width]) * layer_norm(atom_act.astype(jnp.float32), 1) + ada[:, window_width:]).astype(jnp.bfloat16)
    projected = jnp.dot(atom_inputs, qkv_weight, preferred_element_type=jnp.float32).astype(jnp.bfloat16)
    queries = projected[:, :window_width]
    padded_keys = jnp.pad(projected[:, window_width:], ((side, side), (0, 0)))
    key_live = jnp.pad(live, (side, side))
    key_token = jnp.pad(atom_token, (side, side))

    def attend(window):
        start = window * QUERY_WINDOW
        query_rows = lax.dynamic_slice_in_dim(queries, start, QUERY_WINDOW, 0).astype(jnp.float32).reshape(QUERY_WINDOW, HEADS, head_size)
        key_rows = lax.dynamic_slice_in_dim(padded_keys, start, KEYS, 0).astype(jnp.float32)
        window_key_rows = key_rows[:, :window_width].reshape(KEYS, HEADS, head_size)
        window_value_rows = key_rows[:, window_width:].reshape(KEYS, HEADS, head_size)
        query_token = lax.dynamic_slice_in_dim(atom_token, start, QUERY_WINDOW, 0)
        keys_token = lax.dynamic_slice_in_dim(key_token, start, KEYS, 0)
        keys_live = lax.dynamic_slice_in_dim(key_live, start, KEYS, 0)
        block = pair_out[query_token][:, keys_token].astype(jnp.float32)
        bias_norm = layer_norm(block, 2).astype(jnp.bfloat16)
        pair_tile_bias = jnp.dot(bias_norm.reshape(QUERY_WINDOW * KEYS, channels), bias_weight, preferred_element_type=jnp.float32).astype(jnp.bfloat16)
        pair_tile_bias = pair_tile_bias.astype(jnp.float32).reshape(QUERY_WINDOW, KEYS, HEADS).transpose(2, 0, 1)
        logit_scores = jnp.einsum('zki,uki->kzu', query_rows, window_key_rows) / math.sqrt(head_size) + pair_tile_bias
        logit_scores = jnp.where(keys_live[None, None, :] > 0, logit_scores, -1e+30)
        softmax_weight = jax.nn.softmax(logit_scores, axis=-1).astype(jnp.bfloat16).astype(jnp.float32)
        head_mixture = jnp.einsum('fkn,nfv->kfv', softmax_weight, window_value_rows).reshape(QUERY_WINDOW, window_width)
        return head_mixture.astype(jnp.bfloat16)
    attended = lax.map(attend, jnp.arange(atoms // QUERY_WINDOW, dtype=jnp.int32)).reshape(atoms, window_width)
    atom_mid = atom_act.astype(jnp.float32) + jnp.dot(attended, attn_out_weight, preferred_element_type=jnp.float32)
    atom_norm = layer_norm(atom_mid, 1).astype(jnp.bfloat16)
    expanded = jnp.dot(atom_norm, ffn_in_weight, preferred_element_type=jnp.float32)
    hidden_width = ffn_out_weight.shape[0]
    inner = (jax.nn.silu(expanded[:, :hidden_width]) * expanded[:, hidden_width:]).astype(jnp.bfloat16)
    atom_out = ((atom_mid + jnp.dot(inner, ffn_out_weight, preferred_element_type=jnp.float32)) * live[:, None]).astype(jnp.bfloat16)
    features = jax.nn.relu(jnp.dot(atom_out, agg_weight, preferred_element_type=jnp.float32)).astype(jnp.bfloat16)
    sums = jax.ops.segment_sum(features.astype(jnp.float32) * live[:, None], atom_token, num_segments=tokens)
    counts = jax.ops.segment_sum(live, atom_token, num_segments=tokens)
    token_out = (sums / counts[:, None]).astype(jnp.bfloat16)
    return (pair_out, atom_out, token_out)
```

```python
import functools
import math

import jax
import jax.numpy as jnp
from jax import lax
from jax.experimental import pallas as pl
from jax.experimental.pallas import tpu as pltpu
from jax.sharding import PartitionSpec as P

QUERY_WINDOW = 32
KEYS = 128


EPSILON = 1e-05


def extended(shard, sides, width):
    for axis, dim in sides:
        size, length = (lax.axis_size(axis), shard.shape[dim])
        up = [(i, (i + 1) % size) for i in range(size - 1)]
        down = [(j, i) for i, j in up]
        last = lax.slice_in_dim(shard, length - width, length, axis=dim)
        first = lax.slice_in_dim(shard, 0, width, axis=dim)
        before = lax.ppermute(last, axis, up)
        after = lax.ppermute(first, axis, down)
        shard = jnp.concatenate([before, shard, after], axis=dim)
    return shard


def layer_norm(values, along):
    average = jnp.mean(values, axis=along, keepdims=True)
    centred = values - average
    spread = jnp.mean(centred * centred, axis=along, keepdims=True)
    return centred / jnp.sqrt(spread + EPSILON)


def per_device(
    pair,
    token_mask,
    tri_in_weight,
    tri_gate_weight,
    tri_out_weight,
    atom_act,
    atom_cond,
    atom_token,
    atom_mask,
    ada_weight,
    qkv_weight,
    bias_weight,
    attn_out_weight,
    ffn_in_weight,
    ffn_out_weight,
    agg_weight,
):
    tok_rows = pair.shape[0]
    col_count = pair.shape[1]
    channels = pair.shape[2]
    row_index = lax.axis_index("row")
    col_index = lax.axis_index("col")
    pair_float = pair.astype(jnp.float32)
    pair_norm = layer_norm(pair_float, 2).astype(jnp.bfloat16)
    row_live = lax.dynamic_slice_in_dim(token_mask, row_index * tok_rows, tok_rows, 0).astype(
        jnp.float32
    )
    col_live = lax.dynamic_slice_in_dim(token_mask, col_index * col_count, col_count, 0).astype(
        jnp.float32
    )
    pair_live = row_live[:, None] * col_live[None, :]
    left_terms = jnp.einsum(
        "ijd,de->eij",
        pair_norm,
        tri_in_weight[:, : 2 * channels],
        preferred_element_type=jnp.float32,
    )
    left = (jax.nn.sigmoid(left_terms[channels:]) * left_terms[:channels] * pair_live).astype(
        jnp.bfloat16
    )
    right_terms = jnp.einsum(
        "ijd,de->eij",
        pair_norm,
        tri_in_weight[:, 2 * channels :],
        preferred_element_type=jnp.float32,
    )
    right = (jax.nn.sigmoid(right_terms[channels:]) * right_terms[:channels] * pair_live).astype(
        jnp.bfloat16
    )
    tri_gate = jax.nn.sigmoid(
        jnp.einsum("ijd,de->ije", pair_norm, tri_gate_weight, preferred_element_type=jnp.float32)
    )
    left_owned, right_owned = (
        lax.all_to_all(left, "row", split_axis=0, concat_axis=1, tiled=True),
        lax.all_to_all(right, "row", split_axis=0, concat_axis=1, tiled=True),
    )
    left_full, right_rows = (
        lax.all_gather(left_owned, "col", axis=2, tiled=True),
        lax.all_gather(right_owned, "col", axis=2, tiled=True),
    )
    right_used = lax.dynamic_slice_in_dim(right_rows, col_index * col_count, col_count, 1)
    tri_sum = jnp.einsum(
        "cik,cjk->cij", left_full, right_used, preferred_element_type=jnp.float32
    ).astype(jnp.bfloat16)
    merged = lax.all_to_all(tri_sum, "row", split_axis=1, concat_axis=0, tiled=True)
    tri_norm = layer_norm(merged.astype(jnp.float32), 0).astype(jnp.bfloat16)
    update = jnp.einsum("dij,de->ije", tri_norm, tri_out_weight, preferred_element_type=jnp.float32)
    pair_out = (pair_float + tri_gate * update).astype(jnp.bfloat16)
    band_width = 3 * tok_rows
    targets = (row_index - 1) * tok_rows + jnp.arange(band_width, dtype=jnp.int32)
    columns = col_index * col_count + jnp.arange(col_count, dtype=jnp.int32)
    selector = (columns[:, None] == targets[None, :]).astype(jnp.bfloat16)
    band_part = jnp.einsum("ijd,jb->ibd", pair_out, selector, preferred_element_type=jnp.float32)
    band = lax.psum(band_part.astype(jnp.bfloat16), "col").astype(jnp.float32)
    band_norm = layer_norm(band, 2).astype(jnp.bfloat16)
    bias_table = jnp.einsum(
        "ibd,dh->ibh", band_norm, bias_weight, preferred_element_type=jnp.float32
    ).astype(jnp.bfloat16)
    slab = atom_act.shape[0]
    window_width = atom_act.shape[1]
    heads = bias_weight.shape[1]
    head_size = window_width // heads
    side = (KEYS - QUERY_WINDOW) // 2
    windows = slab // QUERY_WINDOW
    local_token = atom_token - row_index * tok_rows
    live = atom_mask.astype(jnp.float32)
    token_tag = ((local_token + 1) * atom_mask).astype(jnp.bfloat16)
    ada = jnp.dot(atom_cond, ada_weight, preferred_element_type=jnp.float32)
    atom_inputs = (
        jax.nn.sigmoid(ada[:, :window_width]) * layer_norm(atom_act.astype(jnp.float32), 1)
        + ada[:, window_width:]
    ).astype(jnp.bfloat16)
    projected = jnp.dot(atom_inputs, qkv_weight, preferred_element_type=jnp.float32).astype(
        jnp.bfloat16
    )
    queries = projected[:, :window_width]
    ext_pairs, ext_tag = (
        extended(projected[:, window_width:], (("row", 0),), side),
        extended(token_tag, (("row", 0),), side),
    )
    ext_rows = slab + 2 * side
    ext_position = jnp.arange(ext_rows, dtype=jnp.int32)
    offset = jnp.where(
        ext_position < side, 0, jnp.where(ext_position < side + slab, tok_rows, 2 * tok_rows)
    )
    tag_value = ext_tag.astype(jnp.int32)
    key_valid = tag_value > 0
    band_index = tag_value - 1 + offset
    band_slots = jnp.arange(band_width, dtype=jnp.int32)
    key_onehot = ((band_index[:, None] == band_slots[None, :]) & key_valid[:, None]).astype(
        jnp.bfloat16
    )
    query_onehot = (local_token[:, None] == jnp.arange(tok_rows, dtype=jnp.int32)[None, :]).astype(
        jnp.bfloat16
    )
    query_bias = jnp.einsum(
        "lt,tbh->lbh", query_onehot, bias_table, preferred_element_type=jnp.float32
    ).astype(jnp.bfloat16)
    query_bias = query_bias.reshape(windows, QUERY_WINDOW, band_width, heads)
    key_index = (
        jnp.arange(windows, dtype=jnp.int32)[:, None] * QUERY_WINDOW
        + jnp.arange(KEYS, dtype=jnp.int32)[None, :]
    )
    window_pairs = ext_pairs[key_index]
    window_onehot = key_onehot[key_index]
    window_valid = key_valid[key_index]
    window_bias = jnp.einsum(
        "wlbh,wmb->whlm", query_bias, window_onehot, preferred_element_type=jnp.float32
    )
    query_heads = queries.reshape(windows, QUERY_WINDOW, heads, head_size)
    key_heads = window_pairs[..., :window_width].reshape(windows, KEYS, heads, head_size)
    value_heads = window_pairs[..., window_width:].reshape(windows, KEYS, heads, head_size)
    logit_scores = (
        jnp.einsum("wlhd,wmhd->whlm", query_heads, key_heads, preferred_element_type=jnp.float32)
        / math.sqrt(head_size)
        + window_bias
    )
    logit_scores = jnp.where(window_valid[:, None, None, :], logit_scores, -1e30)
    attn_weights = jax.nn.softmax(logit_scores, axis=-1).astype(jnp.bfloat16)
    attended = (
        jnp.einsum("whlm,wmhd->wlhd", attn_weights, value_heads, preferred_element_type=jnp.float32)
        .reshape(slab, window_width)
        .astype(jnp.bfloat16)
    )
    atom_mid = atom_act.astype(jnp.float32) + jnp.dot(
        attended, attn_out_weight, preferred_element_type=jnp.float32
    )
    atom_norm = layer_norm(atom_mid, 1).astype(jnp.bfloat16)
    expanded = jnp.dot(atom_norm, ffn_in_weight, preferred_element_type=jnp.float32)
    hidden_width = ffn_out_weight.shape[0]
    inner = (jax.nn.silu(expanded[:, :hidden_width]) * expanded[:, hidden_width:]).astype(
        jnp.bfloat16
    )
    atom_out = (
        (atom_mid + jnp.dot(inner, ffn_out_weight, preferred_element_type=jnp.float32))
        * live[:, None]
    ).astype(jnp.bfloat16)
    features = jax.nn.relu(
        jnp.dot(atom_out, agg_weight, preferred_element_type=jnp.float32)
    ).astype(jnp.bfloat16)
    live_onehot = query_onehot * atom_mask.astype(jnp.bfloat16)[:, None]
    token_sums = jnp.einsum("at,ac->tc", live_onehot, features, preferred_element_type=jnp.float32)
    token_counts = jnp.sum(live_onehot.astype(jnp.float32), axis=0)
    token_out = (token_sums / token_counts[:, None]).astype(jnp.bfloat16)
    return (pair_out, atom_out, token_out)


LANES = 128
SUBLANES = 8
SIDE = (KEYS - QUERY_WINDOW) // 2
F32 = jnp.float32
BF16 = jnp.bfloat16
NT = (((1,), (1,)), ((), ()))
TN = (((0,), (0,)), ((), ()))
TT = (((0,), (1,)), ((), ()))


def matmul(a, b, dims=(((1,), (0,)), ((), ()))):
    return lax.dot_general(a, b, dims, preferred_element_type=F32)


def normalize(values, axis):
    average = jnp.mean(values, axis=axis, keepdims=True)
    centred = values - average
    spread = jnp.mean(centred * centred, axis=axis, keepdims=True)
    return centred * lax.rsqrt(spread + EPSILON)


def iota(shape, dim):
    return lax.broadcasted_iota(jnp.int32, shape, dim)


def column_of(row, size):
    eye = iota((size, size), 0) == iota((size, size), 1)
    return jnp.sum(jnp.where(eye, row, 0.0), axis=1, keepdims=True)


def pad_lanes(row):
    return jnp.concatenate([row, jnp.zeros((row.shape[0], LANES - row.shape[1]), row.dtype)], axis=1)


def spread(got_ref, taken):
    for b in range(taken.shape[0]):
        taken[b] = got_ref[:, b * LANES : (b + 1) * LANES].astype(F32)


def send_kernel(
    n_row, pair_ref, mask_ref, in_w_ref, act_ref, cond_ref, token_ref, alive_ref, ada_w_ref, qkv_w_ref,
    out_ref, qkv_ref, staged,
):
    me = lax.axis_index("row")
    rows, cols, channels = pair_ref.shape
    part = channels // n_row
    width = rows * cols
    act = act_ref[...].astype(F32)
    ada = matmul(cond_ref[...], ada_w_ref[...])
    wide = act.shape[1]
    inputs = (jax.nn.sigmoid(ada[:, :wide]) * normalize(act, 1) + ada[:, wide:]).astype(BF16)
    projected = matmul(inputs, qkv_w_ref[...]).astype(BF16)
    qkv_ref[...] = projected
    slab = act.shape[0]
    keys = projected[:, wide : 2 * wide].astype(F32)
    values = projected[:, 2 * wide :].astype(F32)
    rims = (
        jnp.concatenate([keys[slab - SIDE :], values[slab - SIDE :]], axis=0),
        jnp.concatenate([keys[:SIDE], values[:SIDE]], axis=0),
    )
    share = 2 * SIDE // n_row
    blocks = width // LANES
    for d, rim in enumerate(rims):
        for s in range(share):
            staged[blocks, pl.ds(d * share + s, n_row, stride=SUBLANES)] = rim[s * n_row : (s + 1) * n_row]
    tag = ((token_ref[...] - me * rows + 1) * alive_ref[...]).astype(F32)
    tag_rows = jnp.broadcast_to(pad_lanes(tag), (n_row, LANES))
    for s in range(2 * share, SUBLANES):
        staged[blocks, pl.ds(s, n_row, stride=SUBLANES)] = tag_rows
    normed = normalize(pair_ref[...].reshape(width, channels).astype(F32), 1).astype(BF16)
    live = mask_ref[...].astype(F32)
    lane = iota(live.shape, 1)
    both = jnp.concatenate(
        [live * jnp.sum(jnp.where(lane == me * rows + i, live, 0.0), axis=1, keepdims=True) for i in range(rows)],
        axis=1,
    )
    for side in range(2):
        first = 2 * side * channels
        value = matmul(in_w_ref[:, first : first + channels], normed, TT)
        gate = matmul(in_w_ref[:, first + channels : first + 2 * channels], normed, TT)
        term = jax.nn.sigmoid(gate) * value * both
        for q in range(part):
            for b in range(blocks):
                staged[b, pl.ds(side * part + q, n_row, stride=SUBLANES)] = term[
                    q * n_row : (q + 1) * n_row, b * LANES : (b + 1) * LANES
                ]
    for b in range(blocks + 1):
        out_ref[:, b * LANES : (b + 1) * LANES] = staged[b].astype(BF16)


def gate_kernel(pair_ref, gate_w_ref, out_ref):
    rows, cols, channels = pair_ref.shape
    normed = normalize(pair_ref[...].reshape(rows * cols, channels).astype(F32), 1).astype(BF16)
    out_ref[...] = jax.nn.sigmoid(matmul(normed, gate_w_ref[...]))


def triangle_kernel(n_row, rows, got_ref, out_ref, taken, right_terms, staged):
    spread(got_ref, taken)
    cols = n_row * rows
    part = SUBLANES // 2
    half = SUBLANES // rows
    per = part // half
    for q in range(part):
        left = jnp.concatenate(
            [taken[i, pl.ds(q, n_row, stride=SUBLANES)] for i in range(rows)], axis=0
        ).astype(BF16)
        for j in range(rows):
            right_terms[q, pl.ds(j, n_row, stride=rows)] = taken[j, pl.ds(part + q, n_row, stride=SUBLANES)]
        summed = matmul(left, right_terms[q].astype(BF16), NT)
        for i in range(rows):
            staged[q % per, pl.ds((q // per) * rows + i, n_row, stride=SUBLANES)] = summed[
                i * n_row : (i + 1) * n_row
            ]
    rim = taken[rows]
    nothing = jnp.zeros((SUBLANES, LANES), F32)
    from_before = jnp.concatenate([nothing, rim[:-SUBLANES]], axis=0)
    from_after = jnp.concatenate([rim[SUBLANES:], nothing], axis=0)
    share = 2 * SIDE // n_row
    place = iota(rim.shape, 0) % SUBLANES
    is_before = (place < share) | (place == 2 * share)
    for k in range(per):
        out_ref[:, k * LANES : (k + 1) * LANES] = staged[k].astype(BF16)
    out_ref[:, per * LANES :] = jnp.where(is_before, from_before, from_after).astype(BF16)


def finish_kernel(
    n_row, got_ref, pair_ref, gate_ref, out_w_ref, qkv_ref, act_ref, token_ref, alive_ref, bias_w_ref,
    attn_w_ref, ffn_in_ref, ffn_out_ref, agg_ref,
    pair_out_ref, atom_out_ref, token_out_ref, taken, pair_new, sem,
):
    me = lax.axis_index("row")
    rows, cols, channels = pair_ref.shape
    half = SUBLANES // rows
    per = channels // n_row // half
    spread(got_ref, taken)
    out_w = out_w_ref[...]
    band_width = 3 * rows
    band_pad = 2 * SUBLANES
    target = (me - 1) * rows + iota((band_pad, cols), 0)
    select = ((target == iota((band_pad, cols), 1)) & (iota((band_pad, cols), 0) < band_width)).astype(BF16)
    bands = []
    for i in range(rows):
        sums = jnp.concatenate(
            [
                taken[k, pl.ds(h * rows + i, n_row, stride=SUBLANES)]
                for h in range(half)
                for k in range(per)
            ],
            axis=0,
        )
        update = matmul(normalize(sums, 0).astype(BF16), out_w, TN)
        fresh = (pair_ref[i].astype(F32) + gate_ref[i * cols : (i + 1) * cols] * update).astype(BF16)
        pair_new[i] = fresh
        bands.append(matmul(select, fresh))
    copy = pltpu.make_async_copy(pair_new, pair_out_ref, sem)
    copy.start()
    band_norm = normalize(jnp.concatenate(bands, axis=0), 1).astype(BF16)
    heads = bias_w_ref.shape[0]
    bias_rows = matmul(bias_w_ref[...], band_norm, NT).astype(BF16).astype(F32)
    slab = act_ref.shape[0]
    wide = act_ref.shape[1]
    share = 2 * SIDE // n_row
    token = token_ref[...] - me * rows
    alive = alive_ref[...]
    own_tag = pad_lanes(((token + 1) * alive).astype(F32))
    before_tag = taken[per, 2 * share : 2 * share + 1]
    after_tag = taken[per, 2 * share + 1 : 2 * share + 2]
    flat = rows * band_pad
    token_col = column_of(token.astype(F32), slab)
    query_hot = (token_col == (iota((slab, flat), 1) // band_pad).astype(F32)).astype(F32)
    rims = [
        jnp.concatenate(
            [taken[per, pl.ds(d * share + s, n_row, stride=SUBLANES)] for s in range(share)], axis=0
        )
        for d in range(2)
    ]
    own = qkv_ref[...].astype(F32)
    keys_ext = jnp.concatenate([rims[0][:SIDE], own[:, wide : 2 * wide], rims[1][:SIDE]], axis=0)
    values_ext = jnp.concatenate([rims[0][SIDE:], own[:, 2 * wide :], rims[1][SIDE:]], axis=0)
    head_size = wide // heads
    head_of = iota((QUERY_WINDOW, wide), 1) // head_size
    slot = (iota((flat, KEYS), 0) % band_pad).astype(F32)
    lane = iota((1, LANES), 1)
    mixed = []
    for w in range(slab // QUERY_WINDOW):
        start = w * QUERY_WINDOW
        before_end = SIDE - start
        own_end = before_end + slab
        tag = jnp.where(
            lane < before_end,
            pltpu.roll(before_tag, (SIDE - slab - start) % LANES, 1),
            jnp.where(lane < own_end, pltpu.roll(own_tag, before_end % LANES, 1), pltpu.roll(after_tag, own_end % LANES, 1)),
        )
        offset = jnp.where(lane < before_end, 0.0, jnp.where(lane < own_end, 1.0 * rows, 2.0 * rows))
        valid = tag > 0
        key_slot = jnp.where(valid, tag - 1 + offset, -1.0)
        key_hot = (slot == key_slot).astype(BF16)
        hot = query_hot[start : start + QUERY_WINDOW]
        hot_bias = jnp.concatenate([hot * bias_rows[h : h + 1] for h in range(heads)], axis=0).astype(BF16)
        bias = matmul(hot_bias, key_hot)
        query = own[start : start + QUERY_WINDOW, :wide]
        split = jnp.concatenate([jnp.where(head_of == h, query, 0.0) for h in range(heads)], axis=0).astype(BF16)
        scores = matmul(split, keys_ext[start : start + KEYS].astype(BF16), NT) * (1 / math.sqrt(head_size)) + bias
        scores = jnp.where(valid, scores, -1e30)
        powers = jnp.exp(scores - jnp.max(scores, axis=1, keepdims=True))
        weights = (powers / jnp.sum(powers, axis=1, keepdims=True)).astype(BF16)
        blend = matmul(weights, values_ext[start : start + KEYS].astype(BF16))
        total = jnp.zeros((QUERY_WINDOW, wide), F32)
        for h in range(heads):
            total = jnp.where(head_of == h, blend[h * QUERY_WINDOW : (h + 1) * QUERY_WINDOW], total)
        mixed.append(total)
    attended = jnp.concatenate(mixed, axis=0).astype(BF16)
    middle = act_ref[...].astype(F32) + matmul(attended, attn_w_ref[...])
    expanded = matmul(normalize(middle, 1).astype(BF16), ffn_in_ref[...])
    hidden = ffn_out_ref.shape[0]
    inner = (jax.nn.silu(expanded[:, :hidden]) * expanded[:, hidden:]).astype(BF16)
    alive_float = alive.astype(F32)
    final = ((middle + matmul(inner, ffn_out_ref[...])) * column_of(alive_float, slab)).astype(BF16)
    atom_out_ref[...] = final
    features = jnp.maximum(matmul(final, agg_ref[...]), 0.0).astype(BF16)
    member = jnp.where(iota((SUBLANES, slab), 0) == token, alive_float, 0.0)
    sums = matmul(member.astype(BF16), features)
    counts = jnp.maximum(jnp.sum(member, axis=1, keepdims=True), 1.0)
    token_out_ref[...] = (sums / counts).astype(BF16)[:rows]
    copy.wait()


def whole(count):
    return [pl.BlockSpec(memory_space=pltpu.VMEM)] * count


def cost(flops, nbytes, exps=0):
    return pl.CostEstimate(flops=flops, bytes_accessed=nbytes, transcendentals=exps)


def by_kernels(
    pair, token_mask, tri_in_weight, tri_gate_weight, tri_out_weight, atom_act, atom_cond, atom_token, atom_mask,
    ada_weight, qkv_weight, bias_weight, attn_out_weight, ffn_in_weight, ffn_out_weight, agg_weight,
):
    n_row = lax.axis_size("row")
    rows, cols, channels = pair.shape
    slab, wide = atom_act.shape
    width = rows * cols
    per = channels // n_row * rows // SUBLANES
    mask = token_mask.reshape(1, -1)
    token = atom_token.reshape(1, -1)
    alive = atom_mask.reshape(1, -1)
    tile_rows = n_row * SUBLANES
    terms, qkv = pl.pallas_call(
        functools.partial(send_kernel, n_row),
        out_shape=(
            jax.ShapeDtypeStruct((tile_rows, width + LANES), BF16),
            jax.ShapeDtypeStruct((slab, 3 * wide), BF16),
        ),
        in_specs=whole(9),
        out_specs=tuple(whole(2)),
        scratch_shapes=[pltpu.VMEM((width // LANES + 1, tile_rows, LANES), F32)],
        cost_estimate=cost(8 * width * channels * channels, 1 << 20, 2 * width * channels),
        name="send",
    )(pair, mask, tri_in_weight, atom_act, atom_cond, token, alive, ada_weight, qkv_weight)
    terms = terms.reshape(n_row, SUBLANES, width + LANES)
    got = lax.all_to_all(terms, "row", split_axis=0, concat_axis=0, tiled=True).reshape(tile_rows, width + LANES)
    gate = pl.pallas_call(
        gate_kernel,
        out_shape=jax.ShapeDtypeStruct((width, channels), F32),
        in_specs=whole(2),
        out_specs=whole(1)[0],
        cost_estimate=cost(2 * width * channels * channels, 1 << 19, width * channels),
        name="gate",
    )(pair, tri_gate_weight)
    out_width = per * cols + LANES
    sums = pl.pallas_call(
        functools.partial(triangle_kernel, n_row, rows),
        out_shape=jax.ShapeDtypeStruct((tile_rows, out_width), BF16),
        in_specs=whole(1),
        out_specs=whole(1)[0],
        scratch_shapes=[
            pltpu.VMEM((rows + 1, tile_rows, LANES), F32),
            pltpu.VMEM((channels // n_row, cols, cols), F32),
            pltpu.VMEM((per, tile_rows, LANES), F32),
        ],
        cost_estimate=cost(2 * width * width, 1 << 19),
        name="triangle",
    )(got)
    sums = sums.reshape(n_row, SUBLANES, out_width)
    back = lax.all_to_all(sums, "row", split_axis=0, concat_axis=0, tiled=True).reshape(tile_rows, out_width)
    return pl.pallas_call(
        functools.partial(finish_kernel, n_row),
        out_shape=(
            jax.ShapeDtypeStruct(pair.shape, BF16),
            jax.ShapeDtypeStruct(atom_act.shape, BF16),
            jax.ShapeDtypeStruct((rows, agg_weight.shape[1]), BF16),
        ),
        in_specs=whole(13),
        out_specs=(pl.BlockSpec(memory_space=pl.ANY), *whole(2)),
        scratch_shapes=[
            pltpu.VMEM((per + 1, tile_rows, LANES), F32),
            pltpu.VMEM(pair.shape, BF16),
            pltpu.SemaphoreType.DMA,
        ],
        cost_estimate=cost(4 * width * channels * channels, 1 << 20),
        name="finish",
    )(
        back, pair, gate, tri_out_weight, qkv, atom_act, token, alive, bias_weight.T, attn_out_weight,
        ffn_in_weight, ffn_out_weight, agg_weight,
    )


def kernels_fit(mesh, args):
    pair, atom_act, bias_weight = args[0], args[5], args[11]
    n_row = mesh.shape["row"]
    n_group = mesh.shape["groups"]
    cols, channels = pair.shape[1:]
    rows = pair.shape[0] // (n_group * n_row)
    slab = atom_act.shape[0] // (n_group * n_row)
    wide = atom_act.shape[1]
    share = 2 * SIDE // n_row
    return (
        mesh.shape["col"] == 1
        and cols == LANES
        and channels == LANES
        and wide == LANES
        and rows * 2 == SUBLANES
        and 2 * channels == n_row * SUBLANES
        and 2 * SIDE == share * n_row
        and 2 * share + 2 == SUBLANES
        and SIDE <= slab <= LANES
        and slab % QUERY_WINDOW == 0
        and slab + 2 * SIDE - KEYS == slab - QUERY_WINDOW
        and QUERY_WINDOW % (2 * SUBLANES) == 0
        and wide % bias_weight.shape[1] == 0
    )


def solution(mesh):
    in_specs = (
        P(("groups", "row"), "col", None),
        P("groups"),
        P(),
        P(),
        P(),
        P(("groups", "row"), None),
        P(("groups", "row"), None),
        P(("groups", "row")),
        P(("groups", "row")),
        P(),
        P(),
        P(),
        P(),
        P(),
        P(),
        P(),
    )
    out_specs = (
        P(("groups", "row"), "col", None),
        P(("groups", "row"), None),
        P(("groups", "row"), None),
    )

    def layer(*args):
        body = by_kernels if kernels_fit(mesh, args) else per_device
        return jax.shard_map(body, mesh=mesh, in_specs=in_specs, out_specs=out_specs, check_vma=False)(*args)

    return layer
```

```python
import functools
import math

import jax
import jax.numpy as jnp
from jax import lax
from jax.experimental import pallas as pl
from jax.experimental.pallas import tpu as pltpu
from jax.sharding import PartitionSpec as P

QUERY_WINDOW = 32
KEYS = 128


EPSILON = 1e-05


def extended(shard, sides, width):
    for axis, dim in sides:
        size, length = (lax.axis_size(axis), shard.shape[dim])
        up = [(i, (i + 1) % size) for i in range(size - 1)]
        down = [(j, i) for i, j in up]
        last = lax.slice_in_dim(shard, length - width, length, axis=dim)
        first = lax.slice_in_dim(shard, 0, width, axis=dim)
        before = lax.ppermute(last, axis, up)
        after = lax.ppermute(first, axis, down)
        shard = jnp.concatenate([before, shard, after], axis=dim)
    return shard


def layer_norm(values, along):
    average = jnp.mean(values, axis=along, keepdims=True)
    centred = values - average
    spread = jnp.mean(centred * centred, axis=along, keepdims=True)
    return centred / jnp.sqrt(spread + EPSILON)


def per_device(
    pair,
    token_mask,
    tri_in_weight,
    tri_gate_weight,
    tri_out_weight,
    atom_act,
    atom_cond,
    atom_token,
    atom_mask,
    ada_weight,
    qkv_weight,
    bias_weight,
    attn_out_weight,
    ffn_in_weight,
    ffn_out_weight,
    agg_weight,
):
    tok_rows = pair.shape[0]
    col_count = pair.shape[1]
    channels = pair.shape[2]
    row_index = lax.axis_index("row")
    col_index = lax.axis_index("col")
    pair_float = pair.astype(jnp.float32)
    pair_norm = layer_norm(pair_float, 2).astype(jnp.bfloat16)
    row_live = lax.dynamic_slice_in_dim(token_mask, row_index * tok_rows, tok_rows, 0).astype(
        jnp.float32
    )
    col_live = lax.dynamic_slice_in_dim(token_mask, col_index * col_count, col_count, 0).astype(
        jnp.float32
    )
    pair_live = row_live[:, None] * col_live[None, :]
    left_terms = jnp.einsum(
        "ijd,de->eij",
        pair_norm,
        tri_in_weight[:, : 2 * channels],
        preferred_element_type=jnp.float32,
    )
    left = (jax.nn.sigmoid(left_terms[channels:]) * left_terms[:channels] * pair_live).astype(
        jnp.bfloat16
    )
    right_terms = jnp.einsum(
        "ijd,de->eij",
        pair_norm,
        tri_in_weight[:, 2 * channels :],
        preferred_element_type=jnp.float32,
    )
    right = (jax.nn.sigmoid(right_terms[channels:]) * right_terms[:channels] * pair_live).astype(
        jnp.bfloat16
    )
    tri_gate = jax.nn.sigmoid(
        jnp.einsum("ijd,de->ije", pair_norm, tri_gate_weight, preferred_element_type=jnp.float32)
    )
    left_owned, right_owned = (
        lax.all_to_all(left, "row", split_axis=0, concat_axis=1, tiled=True),
        lax.all_to_all(right, "row", split_axis=0, concat_axis=1, tiled=True),
    )
    left_full, right_rows = (
        lax.all_gather(left_owned, "col", axis=2, tiled=True),
        lax.all_gather(right_owned, "col", axis=2, tiled=True),
    )
    right_used = lax.dynamic_slice_in_dim(right_rows, col_index * col_count, col_count, 1)
    tri_sum = jnp.einsum(
        "cik,cjk->cij", left_full, right_used, preferred_element_type=jnp.float32
    ).astype(jnp.bfloat16)
    merged = lax.all_to_all(tri_sum, "row", split_axis=1, concat_axis=0, tiled=True)
    tri_norm = layer_norm(merged.astype(jnp.float32), 0).astype(jnp.bfloat16)
    update = jnp.einsum("dij,de->ije", tri_norm, tri_out_weight, preferred_element_type=jnp.float32)
    pair_out = (pair_float + tri_gate * update).astype(jnp.bfloat16)
    band_width = 3 * tok_rows
    targets = (row_index - 1) * tok_rows + jnp.arange(band_width, dtype=jnp.int32)
    columns = col_index * col_count + jnp.arange(col_count, dtype=jnp.int32)
    selector = (columns[:, None] == targets[None, :]).astype(jnp.bfloat16)
    band_part = jnp.einsum("ijd,jb->ibd", pair_out, selector, preferred_element_type=jnp.float32)
    band = lax.psum(band_part.astype(jnp.bfloat16), "col").astype(jnp.float32)
    band_norm = layer_norm(band, 2).astype(jnp.bfloat16)
    bias_table = jnp.einsum(
        "ibd,dh->ibh", band_norm, bias_weight, preferred_element_type=jnp.float32
    ).astype(jnp.bfloat16)
    slab = atom_act.shape[0]
    window_width = atom_act.shape[1]
    heads = bias_weight.shape[1]
    head_size = window_width // heads
    side = (KEYS - QUERY_WINDOW) // 2
    windows = slab // QUERY_WINDOW
    local_token = atom_token - row_index * tok_rows
    live = atom_mask.astype(jnp.float32)
    token_tag = ((local_token + 1) * atom_mask).astype(jnp.bfloat16)
    ada = jnp.dot(atom_cond, ada_weight, preferred_element_type=jnp.float32)
    atom_inputs = (
        jax.nn.sigmoid(ada[:, :window_width]) * layer_norm(atom_act.astype(jnp.float32), 1)
        + ada[:, window_width:]
    ).astype(jnp.bfloat16)
    projected = jnp.dot(atom_inputs, qkv_weight, preferred_element_type=jnp.float32).astype(
        jnp.bfloat16
    )
    queries = projected[:, :window_width]
    ext_pairs, ext_tag = (
        extended(projected[:, window_width:], (("row", 0),), side),
        extended(token_tag, (("row", 0),), side),
    )
    ext_rows = slab + 2 * side
    ext_position = jnp.arange(ext_rows, dtype=jnp.int32)
    offset = jnp.where(
        ext_position < side, 0, jnp.where(ext_position < side + slab, tok_rows, 2 * tok_rows)
    )
    tag_value = ext_tag.astype(jnp.int32)
    key_valid = tag_value > 0
    band_index = tag_value - 1 + offset
    band_slots = jnp.arange(band_width, dtype=jnp.int32)
    key_onehot = ((band_index[:, None] == band_slots[None, :]) & key_valid[:, None]).astype(
        jnp.bfloat16
    )
    query_onehot = (local_token[:, None] == jnp.arange(tok_rows, dtype=jnp.int32)[None, :]).astype(
        jnp.bfloat16
    )
    query_bias = jnp.einsum(
        "lt,tbh->lbh", query_onehot, bias_table, preferred_element_type=jnp.float32
    ).astype(jnp.bfloat16)
    query_bias = query_bias.reshape(windows, QUERY_WINDOW, band_width, heads)
    key_index = (
        jnp.arange(windows, dtype=jnp.int32)[:, None] * QUERY_WINDOW
        + jnp.arange(KEYS, dtype=jnp.int32)[None, :]
    )
    window_pairs = ext_pairs[key_index]
    window_onehot = key_onehot[key_index]
    window_valid = key_valid[key_index]
    window_bias = jnp.einsum(
        "wlbh,wmb->whlm", query_bias, window_onehot, preferred_element_type=jnp.float32
    )
    query_heads = queries.reshape(windows, QUERY_WINDOW, heads, head_size)
    key_heads = window_pairs[..., :window_width].reshape(windows, KEYS, heads, head_size)
    value_heads = window_pairs[..., window_width:].reshape(windows, KEYS, heads, head_size)
    logit_scores = (
        jnp.einsum("wlhd,wmhd->whlm", query_heads, key_heads, preferred_element_type=jnp.float32)
        / math.sqrt(head_size)
        + window_bias
    )
    logit_scores = jnp.where(window_valid[:, None, None, :], logit_scores, -1e30)
    attn_weights = jax.nn.softmax(logit_scores, axis=-1).astype(jnp.bfloat16)
    attended = (
        jnp.einsum("whlm,wmhd->wlhd", attn_weights, value_heads, preferred_element_type=jnp.float32)
        .reshape(slab, window_width)
        .astype(jnp.bfloat16)
    )
    atom_mid = atom_act.astype(jnp.float32) + jnp.dot(
        attended, attn_out_weight, preferred_element_type=jnp.float32
    )
    atom_norm = layer_norm(atom_mid, 1).astype(jnp.bfloat16)
    expanded = jnp.dot(atom_norm, ffn_in_weight, preferred_element_type=jnp.float32)
    hidden_width = ffn_out_weight.shape[0]
    inner = (jax.nn.silu(expanded[:, :hidden_width]) * expanded[:, hidden_width:]).astype(
        jnp.bfloat16
    )
    atom_out = (
        (atom_mid + jnp.dot(inner, ffn_out_weight, preferred_element_type=jnp.float32))
        * live[:, None]
    ).astype(jnp.bfloat16)
    features = jax.nn.relu(
        jnp.dot(atom_out, agg_weight, preferred_element_type=jnp.float32)
    ).astype(jnp.bfloat16)
    live_onehot = query_onehot * atom_mask.astype(jnp.bfloat16)[:, None]
    token_sums = jnp.einsum("at,ac->tc", live_onehot, features, preferred_element_type=jnp.float32)
    token_counts = jnp.sum(live_onehot.astype(jnp.float32), axis=0)
    token_out = (token_sums / token_counts[:, None]).astype(jnp.bfloat16)
    return (pair_out, atom_out, token_out)


LANES = 128
SUBLANES = 8
SIDE = (KEYS - QUERY_WINDOW) // 2
LIMIT = pltpu.CompilerParams(vmem_limit_bytes=8 << 20)
F32 = jnp.float32
BF16 = jnp.bfloat16
NT = (((1,), (1,)), ((), ()))
TN = (((0,), (0,)), ((), ()))
TT = (((0,), (1,)), ((), ()))


def matmul(a, b, dims=(((1,), (0,)), ((), ()))):
    return lax.dot_general(a, b, dims, preferred_element_type=F32)


def normalize(values, axis):
    average = jnp.mean(values, axis=axis, keepdims=True)
    centred = values - average
    spread = jnp.mean(centred * centred, axis=axis, keepdims=True)
    return centred * lax.rsqrt(spread + EPSILON)


def iota(shape, dim):
    return lax.broadcasted_iota(jnp.int32, shape, dim)


def column_of(row, size):
    eye = iota((size, size), 0) == iota((size, size), 1)
    return jnp.sum(jnp.where(eye, row, 0.0), axis=1, keepdims=True)


def pad_lanes(row):
    return jnp.concatenate([row, jnp.zeros((row.shape[0], LANES - row.shape[1]), row.dtype)], axis=1)


def spread(got_ref, taken):
    for b in range(taken.shape[0]):
        taken[b] = got_ref[:, b * LANES : (b + 1) * LANES].astype(F32)


def send_kernel(
    n_row, pair_hbm, in_w_hbm, cond_hbm, act_hbm, ada_w_hbm, qkv_w_hbm, mask_hbm, token_hbm, alive_hbm,
    out_ref, qkv_ref,
    pair_ref, in_w_ref, cond_ref, act_ref, ada_w_ref, qkv_w_ref, mask_ref, token_ref, alive_ref, staged, sems,
):
    sources = (pair_hbm, cond_hbm, ada_w_hbm, act_hbm, qkv_w_hbm, in_w_hbm, mask_hbm, token_hbm, alive_hbm)
    places = (pair_ref, cond_ref, ada_w_ref, act_ref, qkv_w_ref, in_w_ref, mask_ref, token_ref, alive_ref)
    loads = [pltpu.make_async_copy(a, b, sems.at[i]) for i, (a, b) in enumerate(zip(sources, places))]
    for load in loads:
        load.start()
    for load in loads:
        load.wait()
    me = lax.axis_index("row")
    rows, cols, channels = pair_ref.shape
    part = channels // n_row
    width = rows * cols
    act = act_ref[...].astype(F32)
    ada = matmul(cond_ref[...], ada_w_ref[...])
    wide = act.shape[1]
    inputs = (jax.nn.sigmoid(ada[:, :wide]) * normalize(act, 1) + ada[:, wide:]).astype(BF16)
    projected = matmul(inputs, qkv_w_ref[...]).astype(BF16)
    qkv_ref[...] = projected
    slab = act.shape[0]
    keys = projected[:, wide : 2 * wide].astype(F32)
    values = projected[:, 2 * wide :].astype(F32)
    rims = (
        jnp.concatenate([keys[slab - SIDE :], values[slab - SIDE :]], axis=0),
        jnp.concatenate([keys[:SIDE], values[:SIDE]], axis=0),
    )
    share = 2 * SIDE // n_row
    blocks = width // LANES
    for d, rim in enumerate(rims):
        for s in range(share):
            staged[blocks, pl.ds(d * share + s, n_row, stride=SUBLANES)] = rim[s * n_row : (s + 1) * n_row]
    tag = ((token_ref[...] - me * rows + 1) * alive_ref[...]).astype(F32)
    tag_rows = jnp.broadcast_to(pad_lanes(tag), (n_row, LANES))
    for s in range(2 * share, SUBLANES):
        staged[blocks, pl.ds(s, n_row, stride=SUBLANES)] = tag_rows
    normed = normalize(pair_ref[...].reshape(width, channels).astype(F32), 1).astype(BF16)
    live = mask_ref[...].astype(F32)
    lane = iota(live.shape, 1)
    both = jnp.concatenate(
        [live * jnp.sum(jnp.where(lane == me * rows + i, live, 0.0), axis=1, keepdims=True) for i in range(rows)],
        axis=1,
    )
    for side in range(2):
        first = 2 * side * channels
        value = matmul(in_w_ref[:, first : first + channels], normed, TT)
        gate = matmul(in_w_ref[:, first + channels : first + 2 * channels], normed, TT)
        term = jax.nn.sigmoid(gate) * value * both
        for q in range(part):
            for b in range(blocks):
                staged[b, pl.ds(side * part + q, n_row, stride=SUBLANES)] = term[
                    q * n_row : (q + 1) * n_row, b * LANES : (b + 1) * LANES
                ]
    for b in range(blocks + 1):
        out_ref[:, b * LANES : (b + 1) * LANES] = staged[b].astype(BF16)


def prepare_kernel(
    band_pad, pair_ref, gate_w_ref, token_ref, alive_ref, bias_w_ref,
    out_ref, tag_ref, query_hot_ref, live_ref, member_ref, bias_ref,
):
    rows, cols, channels = pair_ref.shape
    slab = token_ref.shape[1]
    token = token_ref[...] - lax.axis_index("row") * rows
    alive = alive_ref[...]
    alive_float = alive.astype(F32)
    tag_ref[...] = jnp.broadcast_to(pad_lanes(((token + 1) * alive).astype(F32)), tag_ref.shape)
    token_col = column_of(token.astype(F32), slab)
    query_hot_ref[...] = (token_col == (iota(query_hot_ref.shape, 1) // band_pad).astype(F32)).astype(F32)
    live_ref[...] = jnp.broadcast_to(column_of(alive_float, slab), live_ref.shape)
    member_ref[...] = jnp.where(iota(member_ref.shape, 0) == token, alive_float, 0.0)
    bias_ref[...] = bias_w_ref[...]
    normed = normalize(pair_ref[...].reshape(rows * cols, channels).astype(F32), 1).astype(BF16)
    out_ref[...] = jax.nn.sigmoid(matmul(normed, gate_w_ref[...]))


def triangle_kernel(n_row, rows, got_ref, out_ref, taken, right_terms, staged):
    spread(got_ref, taken)
    cols = n_row * rows
    part = SUBLANES // 2
    half = SUBLANES // rows
    per = part // half
    for q in range(part):
        left = jnp.concatenate(
            [taken[i, pl.ds(q, n_row, stride=SUBLANES)] for i in range(rows)], axis=0
        ).astype(BF16)
        for j in range(rows):
            right_terms[q, pl.ds(j, n_row, stride=rows)] = taken[j, pl.ds(part + q, n_row, stride=SUBLANES)]
        summed = matmul(left, right_terms[q].astype(BF16), NT)
        for i in range(rows):
            staged[q % per, pl.ds((q // per) * rows + i, n_row, stride=SUBLANES)] = summed[
                i * n_row : (i + 1) * n_row
            ]
    rim = taken[rows]
    nothing = jnp.zeros((SUBLANES, LANES), F32)
    from_before = jnp.concatenate([nothing, rim[:-SUBLANES]], axis=0)
    from_after = jnp.concatenate([rim[SUBLANES:], nothing], axis=0)
    share = 2 * SIDE // n_row
    place = iota(rim.shape, 0) % SUBLANES
    is_before = (place < share) | (place == 2 * share)
    for k in range(per):
        out_ref[:, k * LANES : (k + 1) * LANES] = staged[k].astype(BF16)
    out_ref[:, per * LANES :] = jnp.where(is_before, from_before, from_after).astype(BF16)


def finish_kernel(
    n_row, got_ref, pair_ref, gate_ref, out_w_ref, qkv_ref, act_ref, tag_ref, query_hot_ref, live_ref, member_ref,
    bias_w_ref, attn_w_ref, ffn_in_ref, ffn_out_ref, agg_ref,
    pair_out_ref, atom_out_ref, token_out_ref, taken, pair_new, sem,
):
    me = lax.axis_index("row")
    rows, cols, channels = pair_ref.shape
    half = SUBLANES // rows
    per = channels // n_row // half
    spread(got_ref, taken)
    out_w = out_w_ref[...]
    band_width = 3 * rows
    band_pad = 2 * SUBLANES
    target = (me - 1) * rows + iota((band_pad, cols), 0)
    select = ((target == iota((band_pad, cols), 1)) & (iota((band_pad, cols), 0) < band_width)).astype(BF16)
    bands = []
    for i in range(rows):
        sums = jnp.concatenate(
            [
                taken[k, pl.ds(h * rows + i, n_row, stride=SUBLANES)]
                for h in range(half)
                for k in range(per)
            ],
            axis=0,
        )
        update = matmul(normalize(sums, 0).astype(BF16), out_w, TN)
        fresh = (pair_ref[i].astype(F32) + gate_ref[i * cols : (i + 1) * cols] * update).astype(BF16)
        pair_new[i] = fresh
        bands.append(matmul(select, fresh))
    copy = pltpu.make_async_copy(pair_new, pair_out_ref, sem)
    copy.start()
    band_norm = normalize(jnp.concatenate(bands, axis=0), 1).astype(BF16)
    heads = bias_w_ref.shape[0]
    bias_rows = matmul(bias_w_ref[...], band_norm, NT).astype(BF16).astype(F32)
    slab = act_ref.shape[0]
    wide = act_ref.shape[1]
    share = 2 * SIDE // n_row
    own_tag = tag_ref[:1]
    before_tag = taken[per, 2 * share : 2 * share + 1]
    after_tag = taken[per, 2 * share + 1 : 2 * share + 2]
    flat = rows * band_pad
    query_hot = query_hot_ref[...]
    rims = [
        jnp.concatenate(
            [taken[per, pl.ds(d * share + s, n_row, stride=SUBLANES)] for s in range(share)], axis=0
        )
        for d in range(2)
    ]
    own = qkv_ref[...].astype(F32)
    keys_ext = jnp.concatenate([rims[0][:SIDE], own[:, wide : 2 * wide], rims[1][:SIDE]], axis=0)
    values_ext = jnp.concatenate([rims[0][SIDE:], own[:, 2 * wide :], rims[1][SIDE:]], axis=0)
    head_size = wide // heads
    head_of = iota((QUERY_WINDOW, wide), 1) // head_size
    slot = (iota((flat, KEYS), 0) % band_pad).astype(F32)
    lane = iota((1, LANES), 1)
    mixed = []
    for w in range(slab // QUERY_WINDOW):
        start = w * QUERY_WINDOW
        before_end = SIDE - start
        own_end = before_end + slab
        tag = jnp.where(
            lane < before_end,
            pltpu.roll(before_tag, (SIDE - slab - start) % LANES, 1),
            jnp.where(lane < own_end, pltpu.roll(own_tag, before_end % LANES, 1), pltpu.roll(after_tag, own_end % LANES, 1)),
        )
        offset = jnp.where(lane < before_end, 0.0, jnp.where(lane < own_end, 1.0 * rows, 2.0 * rows))
        valid = tag > 0
        key_slot = jnp.where(valid, tag - 1 + offset, -1.0)
        key_hot = (slot == key_slot).astype(BF16)
        hot = query_hot[start : start + QUERY_WINDOW]
        hot_bias = jnp.concatenate([hot * bias_rows[h : h + 1] for h in range(heads)], axis=0).astype(BF16)
        bias = matmul(hot_bias, key_hot)
        query = own[start : start + QUERY_WINDOW, :wide]
        split = jnp.concatenate([jnp.where(head_of == h, query, 0.0) for h in range(heads)], axis=0).astype(BF16)
        scores = matmul(split, keys_ext[start : start + KEYS].astype(BF16), NT) * (1 / math.sqrt(head_size)) + bias
        scores = jnp.where(valid, scores, -1e30)
        powers = jnp.exp(scores - jnp.max(scores, axis=1, keepdims=True))
        weights = (powers / jnp.sum(powers, axis=1, keepdims=True)).astype(BF16)
        blend = matmul(weights, values_ext[start : start + KEYS].astype(BF16))
        total = jnp.zeros((QUERY_WINDOW, wide), F32)
        for h in range(heads):
            total = jnp.where(head_of == h, blend[h * QUERY_WINDOW : (h + 1) * QUERY_WINDOW], total)
        mixed.append(total)
    attended = jnp.concatenate(mixed, axis=0).astype(BF16)
    middle = act_ref[...].astype(F32) + matmul(attended, attn_w_ref[...])
    expanded = matmul(normalize(middle, 1).astype(BF16), ffn_in_ref[...])
    hidden = ffn_out_ref.shape[0]
    inner = (jax.nn.silu(expanded[:, :hidden]) * expanded[:, hidden:]).astype(BF16)
    final = ((middle + matmul(inner, ffn_out_ref[...])) * live_ref[...]).astype(BF16)
    atom_out_ref[...] = final
    features = jnp.maximum(matmul(final, agg_ref[...]), 0.0).astype(BF16)
    member = member_ref[...]
    sums = matmul(member.astype(BF16), features)
    counts = jnp.maximum(jnp.sum(member, axis=1, keepdims=True), 1.0)
    token_out_ref[...] = (sums / counts).astype(BF16)[:rows]
    copy.wait()


def whole(count):
    return [pl.BlockSpec(memory_space=pltpu.VMEM)] * count


def cost(flops, nbytes, exps=0):
    return pl.CostEstimate(flops=flops, bytes_accessed=nbytes, transcendentals=exps)


def by_kernels(
    pair, token_mask, tri_in_weight, tri_gate_weight, tri_out_weight, atom_act, atom_cond, atom_token, atom_mask,
    ada_weight, qkv_weight, bias_weight, attn_out_weight, ffn_in_weight, ffn_out_weight, agg_weight,
):
    n_row = lax.axis_size("row")
    rows, cols, channels = pair.shape
    slab, wide = atom_act.shape
    width = rows * cols
    per = channels // n_row * rows // SUBLANES
    mask = token_mask.reshape(1, -1)
    token = atom_token.reshape(1, -1)
    alive = atom_mask.reshape(1, -1)
    tile_rows = n_row * SUBLANES
    sources = (pair, tri_in_weight, atom_cond, atom_act, ada_weight, qkv_weight, mask, token, alive)
    terms, qkv = pl.pallas_call(
        functools.partial(send_kernel, n_row),
        out_shape=(
            jax.ShapeDtypeStruct((tile_rows, width + LANES), BF16),
            jax.ShapeDtypeStruct((slab, 3 * wide), BF16),
        ),
        in_specs=[pl.BlockSpec(memory_space=pltpu.HBM)] * len(sources),
        out_specs=tuple(whole(2)),
        scratch_shapes=[
            *(pltpu.VMEM(a.shape, a.dtype) for a in sources),
            pltpu.VMEM((width // LANES + 1, tile_rows, LANES), F32),
            pltpu.SemaphoreType.DMA((len(sources),)),
        ],
        cost_estimate=cost(8 * width * channels * channels, 1 << 20, 2 * width * channels),
        compiler_params=LIMIT,
        name="send",
    )(*(pltpu.with_memory_space_constraint(a, pltpu.HBM) for a in sources))
    terms = terms.reshape(n_row, SUBLANES, width + LANES)
    got = lax.all_to_all(terms, "row", split_axis=0, concat_axis=0, tiled=True).reshape(tile_rows, width + LANES)
    band_pad = 2 * SUBLANES
    prepared = pl.pallas_call(
        functools.partial(prepare_kernel, band_pad),
        out_shape=(
            jax.ShapeDtypeStruct((width, channels), F32),
            jax.ShapeDtypeStruct((SUBLANES, LANES), F32),
            jax.ShapeDtypeStruct((slab, rows * band_pad), F32),
            jax.ShapeDtypeStruct((slab, wide), F32),
            jax.ShapeDtypeStruct((SUBLANES, slab), F32),
            jax.ShapeDtypeStruct(bias_weight.shape[::-1], BF16),
        ),
        in_specs=whole(5),
        out_specs=tuple(whole(6)),
        cost_estimate=cost(2 * width * channels * channels, 1 << 19, width * channels),
        compiler_params=LIMIT,
        name="prepare",
    )(pair, tri_gate_weight, token, alive, bias_weight.T)
    gate, *tables = prepared
    out_width = per * cols + LANES
    sums = pl.pallas_call(
        functools.partial(triangle_kernel, n_row, rows),
        out_shape=jax.ShapeDtypeStruct((tile_rows, out_width), BF16),
        in_specs=whole(1),
        out_specs=whole(1)[0],
        scratch_shapes=[
            pltpu.VMEM((rows + 1, tile_rows, LANES), F32),
            pltpu.VMEM((channels // n_row, cols, cols), F32),
            pltpu.VMEM((per, tile_rows, LANES), F32),
        ],
        cost_estimate=cost(2 * width * width, 1 << 19),
        compiler_params=LIMIT,
        name="triangle",
    )(got)
    sums = sums.reshape(n_row, SUBLANES, out_width)
    back = lax.all_to_all(sums, "row", split_axis=0, concat_axis=0, tiled=True).reshape(tile_rows, out_width)
    return pl.pallas_call(
        functools.partial(finish_kernel, n_row),
        out_shape=(
            jax.ShapeDtypeStruct(pair.shape, BF16),
            jax.ShapeDtypeStruct(atom_act.shape, BF16),
            jax.ShapeDtypeStruct((rows, agg_weight.shape[1]), BF16),
        ),
        in_specs=whole(15),
        out_specs=(pl.BlockSpec(memory_space=pl.ANY), *whole(2)),
        scratch_shapes=[
            pltpu.VMEM((per + 1, tile_rows, LANES), F32),
            pltpu.VMEM(pair.shape, BF16),
            pltpu.SemaphoreType.DMA,
        ],
        cost_estimate=cost(4 * width * channels * channels, 1 << 20),
        compiler_params=LIMIT,
        name="finish",
    )(
        back, pair, gate, tri_out_weight, qkv, atom_act, *tables, attn_out_weight, ffn_in_weight, ffn_out_weight,
        agg_weight,
    )


def kernels_fit(mesh, args):
    pair, atom_act, bias_weight = args[0], args[5], args[11]
    n_row = mesh.shape["row"]
    n_group = mesh.shape["groups"]
    cols, channels = pair.shape[1:]
    rows = pair.shape[0] // (n_group * n_row)
    slab = atom_act.shape[0] // (n_group * n_row)
    wide = atom_act.shape[1]
    share = 2 * SIDE // n_row
    return (
        mesh.shape["col"] == 1
        and cols == LANES
        and channels == LANES
        and wide == LANES
        and rows * 2 == SUBLANES
        and 2 * channels == n_row * SUBLANES
        and 2 * SIDE == share * n_row
        and 2 * share + 2 == SUBLANES
        and SIDE <= slab <= LANES
        and slab % QUERY_WINDOW == 0
        and slab + 2 * SIDE - KEYS == slab - QUERY_WINDOW
        and QUERY_WINDOW % (2 * SUBLANES) == 0
        and wide % bias_weight.shape[1] == 0
    )


def solution(mesh):
    in_specs = (
        P(("groups", "row"), "col", None),
        P("groups"),
        P(),
        P(),
        P(),
        P(("groups", "row"), None),
        P(("groups", "row"), None),
        P(("groups", "row")),
        P(("groups", "row")),
        P(),
        P(),
        P(),
        P(),
        P(),
        P(),
        P(),
    )
    out_specs = (
        P(("groups", "row"), "col", None),
        P(("groups", "row"), None),
        P(("groups", "row"), None),
    )

    def layer(*args):
        body = by_kernels if kernels_fit(mesh, args) else per_device
        return jax.shard_map(body, mesh=mesh, in_specs=in_specs, out_specs=out_specs, check_vma=False)(*args)

    return layer
```

```python
import functools
import math

import jax
import jax.numpy as jnp
from jax import lax
from jax.experimental import pallas as pl
from jax.experimental.pallas import tpu as pltpu
from jax.sharding import PartitionSpec as P

QUERY_WINDOW = 32
KEYS = 128


EPSILON = 1e-05


def extended(shard, sides, width):
    for axis, dim in sides:
        size, length = (lax.axis_size(axis), shard.shape[dim])
        up = [(i, (i + 1) % size) for i in range(size - 1)]
        down = [(j, i) for i, j in up]
        last = lax.slice_in_dim(shard, length - width, length, axis=dim)
        first = lax.slice_in_dim(shard, 0, width, axis=dim)
        before = lax.ppermute(last, axis, up)
        after = lax.ppermute(first, axis, down)
        shard = jnp.concatenate([before, shard, after], axis=dim)
    return shard


def layer_norm(values, along):
    average = jnp.mean(values, axis=along, keepdims=True)
    centred = values - average
    spread = jnp.mean(centred * centred, axis=along, keepdims=True)
    return centred / jnp.sqrt(spread + EPSILON)


def per_device(
    pair,
    token_mask,
    tri_in_weight,
    tri_gate_weight,
    tri_out_weight,
    atom_act,
    atom_cond,
    atom_token,
    atom_mask,
    ada_weight,
    qkv_weight,
    bias_weight,
    attn_out_weight,
    ffn_in_weight,
    ffn_out_weight,
    agg_weight,
):
    tok_rows = pair.shape[0]
    col_count = pair.shape[1]
    channels = pair.shape[2]
    row_index = lax.axis_index("row")
    col_index = lax.axis_index("col")
    pair_float = pair.astype(jnp.float32)
    pair_norm = layer_norm(pair_float, 2).astype(jnp.bfloat16)
    row_live = lax.dynamic_slice_in_dim(token_mask, row_index * tok_rows, tok_rows, 0).astype(
        jnp.float32
    )
    col_live = lax.dynamic_slice_in_dim(token_mask, col_index * col_count, col_count, 0).astype(
        jnp.float32
    )
    pair_live = row_live[:, None] * col_live[None, :]
    left_terms = jnp.einsum(
        "ijd,de->eij",
        pair_norm,
        tri_in_weight[:, : 2 * channels],
        preferred_element_type=jnp.float32,
    )
    left = (jax.nn.sigmoid(left_terms[channels:]) * left_terms[:channels] * pair_live).astype(
        jnp.bfloat16
    )
    right_terms = jnp.einsum(
        "ijd,de->eij",
        pair_norm,
        tri_in_weight[:, 2 * channels :],
        preferred_element_type=jnp.float32,
    )
    right = (jax.nn.sigmoid(right_terms[channels:]) * right_terms[:channels] * pair_live).astype(
        jnp.bfloat16
    )
    tri_gate = jax.nn.sigmoid(
        jnp.einsum("ijd,de->ije", pair_norm, tri_gate_weight, preferred_element_type=jnp.float32)
    )
    left_owned, right_owned = (
        lax.all_to_all(left, "row", split_axis=0, concat_axis=1, tiled=True),
        lax.all_to_all(right, "row", split_axis=0, concat_axis=1, tiled=True),
    )
    left_full, right_rows = (
        lax.all_gather(left_owned, "col", axis=2, tiled=True),
        lax.all_gather(right_owned, "col", axis=2, tiled=True),
    )
    right_used = lax.dynamic_slice_in_dim(right_rows, col_index * col_count, col_count, 1)
    tri_sum = jnp.einsum(
        "cik,cjk->cij", left_full, right_used, preferred_element_type=jnp.float32
    ).astype(jnp.bfloat16)
    merged = lax.all_to_all(tri_sum, "row", split_axis=1, concat_axis=0, tiled=True)
    tri_norm = layer_norm(merged.astype(jnp.float32), 0).astype(jnp.bfloat16)
    update = jnp.einsum("dij,de->ije", tri_norm, tri_out_weight, preferred_element_type=jnp.float32)
    pair_out = (pair_float + tri_gate * update).astype(jnp.bfloat16)
    band_width = 3 * tok_rows
    targets = (row_index - 1) * tok_rows + jnp.arange(band_width, dtype=jnp.int32)
    columns = col_index * col_count + jnp.arange(col_count, dtype=jnp.int32)
    selector = (columns[:, None] == targets[None, :]).astype(jnp.bfloat16)
    band_part = jnp.einsum("ijd,jb->ibd", pair_out, selector, preferred_element_type=jnp.float32)
    band = lax.psum(band_part.astype(jnp.bfloat16), "col").astype(jnp.float32)
    band_norm = layer_norm(band, 2).astype(jnp.bfloat16)
    bias_table = jnp.einsum(
        "ibd,dh->ibh", band_norm, bias_weight, preferred_element_type=jnp.float32
    ).astype(jnp.bfloat16)
    slab = atom_act.shape[0]
    window_width = atom_act.shape[1]
    heads = bias_weight.shape[1]
    head_size = window_width // heads
    side = (KEYS - QUERY_WINDOW) // 2
    windows = slab // QUERY_WINDOW
    local_token = atom_token - row_index * tok_rows
    live = atom_mask.astype(jnp.float32)
    token_tag = ((local_token + 1) * atom_mask).astype(jnp.bfloat16)
    ada = jnp.dot(atom_cond, ada_weight, preferred_element_type=jnp.float32)
    atom_inputs = (
        jax.nn.sigmoid(ada[:, :window_width]) * layer_norm(atom_act.astype(jnp.float32), 1)
        + ada[:, window_width:]
    ).astype(jnp.bfloat16)
    projected = jnp.dot(atom_inputs, qkv_weight, preferred_element_type=jnp.float32).astype(
        jnp.bfloat16
    )
    queries = projected[:, :window_width]
    ext_pairs, ext_tag = (
        extended(projected[:, window_width:], (("row", 0),), side),
        extended(token_tag, (("row", 0),), side),
    )
    ext_rows = slab + 2 * side
    ext_position = jnp.arange(ext_rows, dtype=jnp.int32)
    offset = jnp.where(
        ext_position < side, 0, jnp.where(ext_position < side + slab, tok_rows, 2 * tok_rows)
    )
    tag_value = ext_tag.astype(jnp.int32)
    key_valid = tag_value > 0
    band_index = tag_value - 1 + offset
    band_slots = jnp.arange(band_width, dtype=jnp.int32)
    key_onehot = ((band_index[:, None] == band_slots[None, :]) & key_valid[:, None]).astype(
        jnp.bfloat16
    )
    query_onehot = (local_token[:, None] == jnp.arange(tok_rows, dtype=jnp.int32)[None, :]).astype(
        jnp.bfloat16
    )
    query_bias = jnp.einsum(
        "lt,tbh->lbh", query_onehot, bias_table, preferred_element_type=jnp.float32
    ).astype(jnp.bfloat16)
    query_bias = query_bias.reshape(windows, QUERY_WINDOW, band_width, heads)
    key_index = (
        jnp.arange(windows, dtype=jnp.int32)[:, None] * QUERY_WINDOW
        + jnp.arange(KEYS, dtype=jnp.int32)[None, :]
    )
    window_pairs = ext_pairs[key_index]
    window_onehot = key_onehot[key_index]
    window_valid = key_valid[key_index]
    window_bias = jnp.einsum(
        "wlbh,wmb->whlm", query_bias, window_onehot, preferred_element_type=jnp.float32
    )
    query_heads = queries.reshape(windows, QUERY_WINDOW, heads, head_size)
    key_heads = window_pairs[..., :window_width].reshape(windows, KEYS, heads, head_size)
    value_heads = window_pairs[..., window_width:].reshape(windows, KEYS, heads, head_size)
    logit_scores = (
        jnp.einsum("wlhd,wmhd->whlm", query_heads, key_heads, preferred_element_type=jnp.float32)
        / math.sqrt(head_size)
        + window_bias
    )
    logit_scores = jnp.where(window_valid[:, None, None, :], logit_scores, -1e30)
    attn_weights = jax.nn.softmax(logit_scores, axis=-1).astype(jnp.bfloat16)
    attended = (
        jnp.einsum("whlm,wmhd->wlhd", attn_weights, value_heads, preferred_element_type=jnp.float32)
        .reshape(slab, window_width)
        .astype(jnp.bfloat16)
    )
    atom_mid = atom_act.astype(jnp.float32) + jnp.dot(
        attended, attn_out_weight, preferred_element_type=jnp.float32
    )
    atom_norm = layer_norm(atom_mid, 1).astype(jnp.bfloat16)
    expanded = jnp.dot(atom_norm, ffn_in_weight, preferred_element_type=jnp.float32)
    hidden_width = ffn_out_weight.shape[0]
    inner = (jax.nn.silu(expanded[:, :hidden_width]) * expanded[:, hidden_width:]).astype(
        jnp.bfloat16
    )
    atom_out = (
        (atom_mid + jnp.dot(inner, ffn_out_weight, preferred_element_type=jnp.float32))
        * live[:, None]
    ).astype(jnp.bfloat16)
    features = jax.nn.relu(
        jnp.dot(atom_out, agg_weight, preferred_element_type=jnp.float32)
    ).astype(jnp.bfloat16)
    live_onehot = query_onehot * atom_mask.astype(jnp.bfloat16)[:, None]
    token_sums = jnp.einsum("at,ac->tc", live_onehot, features, preferred_element_type=jnp.float32)
    token_counts = jnp.sum(live_onehot.astype(jnp.float32), axis=0)
    token_out = (token_sums / token_counts[:, None]).astype(jnp.bfloat16)
    return (pair_out, atom_out, token_out)


LANES = 128
SUBLANES = 8
SIDE = (KEYS - QUERY_WINDOW) // 2
RIM_ROWS = 4
BAND_PAD = 2 * SUBLANES
LIMIT = pltpu.CompilerParams(vmem_limit_bytes=8 << 20)
F32 = jnp.float32
BF16 = jnp.bfloat16
NT = (((1,), (1,)), ((), ()))
TN = (((0,), (0,)), ((), ()))
TT = (((0,), (1,)), ((), ()))


def matmul(a, b, dims=(((1,), (0,)), ((), ()))):
    return lax.dot_general(a, b, dims, preferred_element_type=F32)


def normalize(values, axis):
    average = jnp.mean(values, axis=axis, keepdims=True)
    centred = values - average
    spread = jnp.mean(centred * centred, axis=axis, keepdims=True)
    return centred * lax.rsqrt(spread + EPSILON)


def iota(shape, dim):
    return lax.broadcasted_iota(jnp.int32, shape, dim)


def column_of(row, size):
    eye = iota((size, size), 0) == iota((size, size), 1)
    return jnp.sum(jnp.where(eye, row, 0.0), axis=1, keepdims=True)


def pad_lanes(row):
    return jnp.concatenate([row, jnp.zeros((row.shape[0], LANES - row.shape[1]), row.dtype)], axis=1)


def strided(first, count, step):
    return pl.ds(first, count, stride=step)


def send_kernel(
    n_row, pair_hbm, act_hbm, bias_w_hbm, in_w_hbm, cond_hbm, ada_w_hbm, mask_hbm, token_hbm, alive_hbm,
    pair_ref, act_ref, bias_w_ref, out_ref, inputs_ref, slots_ref,
    in_w_ref, cond_ref, ada_w_ref, mask_ref, token_ref, alive_ref, staged, sems,
):
    sources = (pair_hbm, cond_hbm, ada_w_hbm, act_hbm, in_w_hbm, mask_hbm, token_hbm, alive_hbm, bias_w_hbm)
    places = (pair_ref, cond_ref, ada_w_ref, act_ref, in_w_ref, mask_ref, token_ref, alive_ref, bias_w_ref)
    loads = [pltpu.make_async_copy(a, b, sems.at[i]) for i, (a, b) in enumerate(zip(sources, places))]
    for load in loads:
        load.start()
    for load in loads:
        load.wait()
    me = lax.axis_index("row")
    rows, cols, channels = pair_ref.shape
    part = channels // n_row
    width = rows * cols
    step = 2 * part * rows + RIM_ROWS
    normed = normalize(pair_ref[...].reshape(width, channels).astype(F32), 1).astype(BF16)
    live = mask_ref[...].astype(F32)
    lane = iota(live.shape, 1)
    both = jnp.concatenate(
        [live * jnp.sum(jnp.where(lane == me * rows + i, live, 0.0), axis=1, keepdims=True) for i in range(rows)],
        axis=1,
    )
    for side in range(2):
        first = 2 * side * channels
        value = matmul(in_w_ref[:, first : first + channels], normed, TT)
        gate = matmul(in_w_ref[:, first + channels : first + 2 * channels], normed, TT)
        term = jax.nn.sigmoid(gate) * value * both
        for q in range(part):
            for i in range(rows):
                staged[strided((side * part + q) * rows + i, n_row, step)] = term[
                    q * n_row : (q + 1) * n_row, i * cols : (i + 1) * cols
                ]
    act = act_ref[...].astype(F32)
    ada = matmul(cond_ref[...], ada_w_ref[...])
    slab, wide = act.shape
    inputs = (jax.nn.sigmoid(ada[:, :wide]) * normalize(act, 1) + ada[:, wide:]).astype(BF16)
    inputs_ref[...] = inputs
    inputs = inputs.astype(F32)
    token = token_ref[...] - me * rows
    alive = alive_ref[...]
    tag = pad_lanes(((token + 1) * alive).astype(F32))
    slots_ref[...] = jnp.zeros(slots_ref.shape, F32)
    slots_ref[0:1] = pad_lanes(token.astype(F32))
    slots_ref[1:2] = pad_lanes(alive.astype(F32))
    slots_ref[2:3] = tag
    tags = jnp.broadcast_to(tag, (2 * n_row - SIDE, LANES))
    for d, rim in enumerate((inputs[slab - SIDE :], inputs[:SIDE])):
        block = jnp.concatenate([rim, tags], axis=0)
        for s in range(RIM_ROWS // 2):
            staged[strided(step - RIM_ROWS + d * (RIM_ROWS // 2) + s, n_row, step)] = block[
                s * n_row : (s + 1) * n_row
            ]
    out_ref[...] = staged[...].astype(BF16)


def prepare(
    pair_ref, gate_w_ref, inputs_ref, qkv_w_ref, slots_ref,
    gate_ref, qkv_ref, query_hot_ref, live_ref, member_ref, select_ref, pair_band_ref, gate_band_ref,
):
    me = lax.axis_index("row")
    rows, cols, channels = pair_ref.shape
    slab = inputs_ref.shape[0]
    token = slots_ref[0:1, :slab]
    alive = slots_ref[1:2, :slab]
    qkv_ref[...] = matmul(inputs_ref[...], qkv_w_ref[...]).astype(BF16)
    token_col = column_of(token, slab)
    query_hot_ref[...] = (token_col == (iota(query_hot_ref.shape, 1) // BAND_PAD).astype(F32)).astype(F32)
    live_ref[...] = jnp.broadcast_to(column_of(alive, slab), live_ref.shape)
    member_ref[...] = jnp.where(iota(member_ref.shape, 0).astype(F32) == token, alive, 0.0)
    normed = normalize(pair_ref[...].reshape(rows * cols, channels).astype(F32), 1).astype(BF16)
    gate_ref[...] = jax.nn.sigmoid(matmul(normed, gate_w_ref[...]))
    place = iota((BAND_PAD, cols), 0)
    target = (me - 1) * rows + place
    select = ((target == iota((BAND_PAD, cols), 1)) & (place < 3 * rows)).astype(BF16)
    select_ref[...] = select
    pair_band_ref[...] = jnp.concatenate([matmul(select, pair_ref[i]) for i in range(rows)], axis=0)
    normed_band = jnp.concatenate(
        [matmul(select, normed[i * cols : (i + 1) * cols]) for i in range(rows)], axis=0
    ).astype(BF16)
    gate_band_ref[...] = jax.nn.sigmoid(matmul(normed_band, gate_w_ref[...]))


def triangle_kernel(n_row, rows, got_ref, *refs):
    out_ref = refs[5]
    taken, right_terms, staged = refs[14:]
    prepare(*refs[:5], *refs[6:14])
    taken[...] = got_ref[...].astype(F32)
    step = got_ref.shape[0] // n_row
    part = right_terms.shape[0]
    out_step = part * rows + RIM_ROWS
    for q in range(part):
        left = jnp.concatenate(
            [taken[strided(q * rows + i, n_row, step)] for i in range(rows)], axis=0
        ).astype(BF16)
        for j in range(rows):
            right_terms[q, strided(j, n_row, rows)] = taken[strided((part + q) * rows + j, n_row, step)]
        summed = matmul(left, right_terms[q].astype(BF16), NT)
        for i in range(rows):
            staged[strided(q * rows + i, n_row, out_step)] = summed[i * n_row : (i + 1) * n_row]
    nothing = jnp.zeros((1, LANES), F32)
    for s in range(RIM_ROWS):
        rim = taken[strided(step - RIM_ROWS + s, n_row, step)]
        if s < RIM_ROWS // 2:
            rim = jnp.concatenate([nothing, rim[:-1]], axis=0)
        else:
            rim = jnp.concatenate([rim[1:], nothing], axis=0)
        staged[strided(out_step - RIM_ROWS + s, n_row, out_step)] = rim
    out_ref[...] = staged[...].astype(BF16)


def finish_kernel(
    n_row, got_ref, pair_ref, out_w_ref, act_ref, slots_ref, bias_w_ref, gate_ref, qkv_ref, query_hot_ref, live_ref,
    member_ref, select_ref, pair_band_ref, gate_band_ref, qkv_w_ref, attn_w_ref, ffn_in_ref, ffn_out_ref, agg_ref,
    pair_out, atom_out, token_out, taken, pair_new, atom_new, token_new, bias_rows, products, values_ext, sems,
):
    me = lax.axis_index("row")
    rows, cols, channels = pair_ref.shape
    part = channels // n_row
    step = part * rows + RIM_ROWS
    half = RIM_ROWS // 2
    slab, wide = act_ref.shape
    heads = bias_w_ref.shape[0]
    head_size = wide // heads
    head_of = iota((QUERY_WINDOW, wide), 1) // head_size
    windows = slab // QUERY_WINDOW
    taken[...] = got_ref[...].astype(F32)
    sums = [
        jnp.concatenate([taken[strided(q * rows + i, n_row, step)] for q in range(part)], axis=0) for i in range(rows)
    ]
    band = jnp.concatenate([matmul(select_ref[...], s.astype(BF16), NT) for s in sums], axis=0)
    band = matmul(normalize(band, 1).astype(BF16), out_w_ref[...])
    band = (pair_band_ref[...] + gate_band_ref[...] * band).astype(BF16).astype(F32)
    bias_rows[...] = matmul(bias_w_ref[...], normalize(band, 1).astype(BF16), NT).astype(BF16).astype(F32)
    outer = jnp.concatenate(
        [
            taken[strided(step - RIM_ROWS + d * half + s, n_row, step)][: min(n_row, SIDE - s * n_row)]
            for d in range(2)
            for s in range(half)
        ],
        axis=0,
    ).astype(BF16)
    outer = matmul(outer, qkv_w_ref[:, wide:]).astype(BF16).astype(F32)
    own = qkv_ref[...].astype(F32)
    keys_ext, values = (
        jnp.concatenate(
            [outer[:SIDE, at : at + wide], own[:, wide + at : 2 * wide + at], outer[SIDE:, at : at + wide]], axis=0
        )
        for at in (0, wide)
    )
    values_ext[...] = values
    for w in range(windows):
        start = w * QUERY_WINDOW
        query = own[start : start + QUERY_WINDOW, :wide]
        split = jnp.concatenate([jnp.where(head_of == h, query, 0.0) for h in range(heads)], axis=0).astype(BF16)
        products[w] = matmul(split, keys_ext[start : start + KEYS].astype(BF16), NT) * (1 / math.sqrt(head_size))
    for i in range(rows):
        update = matmul(normalize(sums[i], 0).astype(BF16), out_w_ref[...], TN)
        pair_new[i] = (pair_ref[i].astype(F32) + gate_ref[i * cols : (i + 1) * cols] * update).astype(BF16)
    pair_copy = pltpu.make_async_copy(pair_new, pair_out, sems.at[0])
    atom_copy = pltpu.make_async_copy(atom_new, atom_out, sems.at[1])
    token_copy = pltpu.make_async_copy(token_new, token_out, sems.at[2])
    pair_copy.start()

    @pl.when(me >= 0)
    def _():
        tag_at = [(step - RIM_ROWS + d * half + SIDE // n_row) + step * (SIDE % n_row) for d in range(2)]
        before_tag, after_tag = (taken[at : at + 1] for at in tag_at)
        own_tag = slots_ref[2:3]
        query_hot = query_hot_ref[...]
        flat = query_hot.shape[1]
        slot = (iota((flat, KEYS), 0) % BAND_PAD).astype(F32)
        lane = iota((1, LANES), 1)
        mixed = []
        for w in range(windows):
            start = w * QUERY_WINDOW
            before_end = SIDE - start
            own_end = before_end + slab
            is_before, is_own = lane < before_end, lane < own_end
            tag = jnp.where(
                is_before,
                pltpu.roll(before_tag, (SIDE - slab - start) % LANES, 1),
                jnp.where(
                    is_own, pltpu.roll(own_tag, before_end % LANES, 1), pltpu.roll(after_tag, own_end % LANES, 1)
                ),
            )
            offset = jnp.where(is_before, 0.0, jnp.where(is_own, 1.0 * rows, 2.0 * rows))
            valid = tag > 0
            key_slot = jnp.where(valid, tag - 1 + offset, -1.0)
            key_hot = (slot == key_slot).astype(BF16)
            hot = query_hot[start : start + QUERY_WINDOW]
            hot_bias = jnp.concatenate([hot * bias_rows[h : h + 1] for h in range(heads)], axis=0).astype(BF16)
            scores = jnp.where(valid, products[w] + matmul(hot_bias, key_hot), -1e30)
            powers = jnp.exp(scores - jnp.max(scores, axis=1, keepdims=True))
            weights = (powers / jnp.sum(powers, axis=1, keepdims=True)).astype(BF16)
            blend = matmul(weights, values_ext[start : start + KEYS].astype(BF16))
            total = jnp.zeros((QUERY_WINDOW, wide), F32)
            for h in range(heads):
                total = jnp.where(head_of == h, blend[h * QUERY_WINDOW : (h + 1) * QUERY_WINDOW], total)
            mixed.append(total)
        attended = jnp.concatenate(mixed, axis=0).astype(BF16)
        middle = act_ref[...].astype(F32) + matmul(attended, attn_w_ref[...])
        expanded = matmul(normalize(middle, 1).astype(BF16), ffn_in_ref[...])
        hidden = ffn_out_ref.shape[0]
        inner = (jax.nn.silu(expanded[:, :hidden]) * expanded[:, hidden:]).astype(BF16)
        final = ((middle + matmul(inner, ffn_out_ref[...])) * live_ref[...]).astype(BF16)
        atom_new[...] = final
        atom_copy.start()
        features = jnp.maximum(matmul(final, agg_ref[...]), 0.0).astype(BF16)
        member = member_ref[...]
        totals = matmul(member.astype(BF16), features)
        counts = jnp.maximum(jnp.sum(member, axis=1, keepdims=True), 1.0)
        token_new[...] = (totals / counts).astype(BF16)[:rows]
        token_copy.start()

    pair_copy.wait()
    atom_copy.wait()
    token_copy.wait()


def in_vmem(count):
    return [pl.BlockSpec(memory_space=pltpu.VMEM)] * count


def in_hbm(arrays):
    return [pltpu.with_memory_space_constraint(a, pltpu.HBM) for a in arrays]


def cost(flops, nbytes, exps=0):
    return pl.CostEstimate(flops=flops, bytes_accessed=nbytes, transcendentals=exps)


def exchange(blocks, n_row):
    grouped = blocks.reshape(n_row, -1, RIM_ROWS, LANES)
    return lax.all_to_all(grouped, "row", split_axis=0, concat_axis=0, tiled=True).reshape(blocks.shape)


def by_kernels(
    pair, token_mask, tri_in_weight, tri_gate_weight, tri_out_weight, atom_act, atom_cond, atom_token, atom_mask,
    ada_weight, qkv_weight, bias_weight, attn_out_weight, ffn_in_weight, ffn_out_weight, agg_weight,
):
    n_row = lax.axis_size("row")
    rows, cols, channels = pair.shape
    slab, wide = atom_act.shape
    width = rows * cols
    part = channels // n_row
    mask = token_mask.reshape(1, -1)
    token = atom_token.reshape(1, -1)
    alive = atom_mask.reshape(1, -1)
    sent = n_row * (2 * part * rows + RIM_ROWS)
    back_rows = n_row * (part * rows + RIM_ROWS)
    sources = (pair, atom_act, bias_weight.T, tri_in_weight, atom_cond, ada_weight, mask, token, alive)
    kept = 3
    pair, atom_act, bias_rows, terms, inputs, slots = pl.pallas_call(
        functools.partial(send_kernel, n_row),
        out_shape=(
            *(jax.ShapeDtypeStruct(a.shape, a.dtype) for a in sources[:kept]),
            jax.ShapeDtypeStruct((sent, LANES), BF16),
            jax.ShapeDtypeStruct((slab, wide), BF16),
            jax.ShapeDtypeStruct((SUBLANES, LANES), F32),
        ),
        in_specs=[pl.BlockSpec(memory_space=pltpu.HBM)] * len(sources),
        out_specs=tuple(in_vmem(kept + 3)),
        scratch_shapes=[
            *(pltpu.VMEM(a.shape, a.dtype) for a in sources[kept:]),
            pltpu.VMEM((sent, LANES), F32),
            pltpu.SemaphoreType.DMA((len(sources),)),
        ],
        cost_estimate=cost(8 * width * channels * channels, 1 << 20, 2 * width * channels),
        compiler_params=LIMIT,
        name="send",
    )(*in_hbm(sources))
    got = exchange(terms, n_row)
    band_shape = jax.ShapeDtypeStruct((rows * BAND_PAD, channels), F32)
    sums, *prepared = pl.pallas_call(
        functools.partial(triangle_kernel, n_row, rows),
        out_shape=(
            jax.ShapeDtypeStruct((back_rows, LANES), BF16),
            jax.ShapeDtypeStruct((width, channels), F32),
            jax.ShapeDtypeStruct((slab, 3 * wide), BF16),
            jax.ShapeDtypeStruct((slab, rows * BAND_PAD), F32),
            jax.ShapeDtypeStruct((slab, wide), F32),
            jax.ShapeDtypeStruct((SUBLANES, slab), F32),
            jax.ShapeDtypeStruct((BAND_PAD, cols), BF16),
            band_shape,
            band_shape,
        ),
        in_specs=in_vmem(6),
        out_specs=tuple(in_vmem(9)),
        scratch_shapes=[
            pltpu.VMEM((sent, LANES), F32),
            pltpu.VMEM((part, cols, cols), F32),
            pltpu.VMEM((back_rows, LANES), F32),
        ],
        cost_estimate=cost(2 * width * width, 1 << 19),
        compiler_params=LIMIT,
        name="triangle",
    )(got, pair, tri_gate_weight, inputs, qkv_weight, slots)
    back = exchange(sums, n_row)
    token_shape = (rows, agg_weight.shape[1])
    return pl.pallas_call(
        functools.partial(finish_kernel, n_row),
        out_shape=(
            jax.ShapeDtypeStruct(pair.shape, BF16),
            jax.ShapeDtypeStruct(atom_act.shape, BF16),
            jax.ShapeDtypeStruct(token_shape, BF16),
        ),
        in_specs=in_vmem(19),
        out_specs=(pl.BlockSpec(memory_space=pltpu.HBM),) * 3,
        scratch_shapes=[
            pltpu.VMEM((back_rows, LANES), F32),
            pltpu.VMEM(pair.shape, BF16),
            pltpu.VMEM(atom_act.shape, BF16),
            pltpu.VMEM(token_shape, BF16),
            pltpu.VMEM((bias_weight.shape[1], rows * BAND_PAD), F32),
            pltpu.VMEM((slab // QUERY_WINDOW, bias_weight.shape[1] * QUERY_WINDOW, KEYS), F32),
            pltpu.VMEM((slab + 2 * SIDE, wide), F32),
            pltpu.SemaphoreType.DMA((3,)),
        ],
        cost_estimate=cost(4 * width * channels * channels, 1 << 20),
        compiler_params=LIMIT,
        name="finish",
    )(
        back, pair, tri_out_weight, atom_act, slots, bias_rows, *prepared, qkv_weight, attn_out_weight, ffn_in_weight,
        ffn_out_weight, agg_weight,
    )


def kernels_fit(mesh, args):
    pair, atom_act, bias_weight = args[0], args[5], args[11]
    n_row = mesh.shape["row"]
    parts = mesh.shape["groups"] * n_row
    cols, channels = pair.shape[1:]
    rows = pair.shape[0] // parts
    slab = atom_act.shape[0] // parts
    wide = atom_act.shape[1]
    return (
        mesh.shape["col"] == 1
        and cols == channels == wide == LANES
        and cols == n_row * rows
        and channels % n_row == 0
        and n_row % SUBLANES == 0
        and SIDE < RIM_ROWS // 2 * n_row
        and 3 * rows <= BAND_PAD
        and rows <= SUBLANES
        and SIDE <= slab <= LANES
        and slab % QUERY_WINDOW == 0
        and slab - QUERY_WINDOW <= SIDE
        and wide % bias_weight.shape[1] == 0
    )


def solution(mesh):
    in_specs = (
        P(("groups", "row"), "col", None),
        P("groups"),
        P(),
        P(),
        P(),
        P(("groups", "row"), None),
        P(("groups", "row"), None),
        P(("groups", "row")),
        P(("groups", "row")),
        P(),
        P(),
        P(),
        P(),
        P(),
        P(),
        P(),
    )
    out_specs = (
        P(("groups", "row"), "col", None),
        P(("groups", "row"), None),
        P(("groups", "row"), None),
    )

    def layer(*args):
        body = by_kernels if kernels_fit(mesh, args) else per_device
        return jax.shard_map(body, mesh=mesh, in_specs=in_specs, out_specs=out_specs, check_vma=False)(*args)

    return layer
```

```python
import functools
import math

import jax
import jax.numpy as jnp
from jax import lax
from jax.experimental import pallas as pl
from jax.experimental.pallas import tpu as pltpu
from jax.sharding import PartitionSpec as P

QUERY_WINDOW = 32
KEYS = 128


EPSILON = 1e-05


def extended(shard, sides, width):
    for axis, dim in sides:
        size, length = (lax.axis_size(axis), shard.shape[dim])
        up = [(i, (i + 1) % size) for i in range(size - 1)]
        down = [(j, i) for i, j in up]
        last = lax.slice_in_dim(shard, length - width, length, axis=dim)
        first = lax.slice_in_dim(shard, 0, width, axis=dim)
        before = lax.ppermute(last, axis, up)
        after = lax.ppermute(first, axis, down)
        shard = jnp.concatenate([before, shard, after], axis=dim)
    return shard


def layer_norm(values, along):
    average = jnp.mean(values, axis=along, keepdims=True)
    centred = values - average
    spread = jnp.mean(centred * centred, axis=along, keepdims=True)
    return centred / jnp.sqrt(spread + EPSILON)


def per_device(
    pair,
    token_mask,
    tri_in_weight,
    tri_gate_weight,
    tri_out_weight,
    atom_act,
    atom_cond,
    atom_token,
    atom_mask,
    ada_weight,
    qkv_weight,
    bias_weight,
    attn_out_weight,
    ffn_in_weight,
    ffn_out_weight,
    agg_weight,
):
    tok_rows = pair.shape[0]
    col_count = pair.shape[1]
    channels = pair.shape[2]
    row_index = lax.axis_index("row")
    col_index = lax.axis_index("col")
    pair_float = pair.astype(jnp.float32)
    pair_norm = layer_norm(pair_float, 2).astype(jnp.bfloat16)
    row_live = lax.dynamic_slice_in_dim(token_mask, row_index * tok_rows, tok_rows, 0).astype(
        jnp.float32
    )
    col_live = lax.dynamic_slice_in_dim(token_mask, col_index * col_count, col_count, 0).astype(
        jnp.float32
    )
    pair_live = row_live[:, None] * col_live[None, :]
    left_terms = jnp.einsum(
        "ijd,de->eij",
        pair_norm,
        tri_in_weight[:, : 2 * channels],
        preferred_element_type=jnp.float32,
    )
    left = (jax.nn.sigmoid(left_terms[channels:]) * left_terms[:channels] * pair_live).astype(
        jnp.bfloat16
    )
    right_terms = jnp.einsum(
        "ijd,de->eij",
        pair_norm,
        tri_in_weight[:, 2 * channels :],
        preferred_element_type=jnp.float32,
    )
    right = (jax.nn.sigmoid(right_terms[channels:]) * right_terms[:channels] * pair_live).astype(
        jnp.bfloat16
    )
    tri_gate = jax.nn.sigmoid(
        jnp.einsum("ijd,de->ije", pair_norm, tri_gate_weight, preferred_element_type=jnp.float32)
    )
    left_owned, right_owned = (
        lax.all_to_all(left, "row", split_axis=0, concat_axis=1, tiled=True),
        lax.all_to_all(right, "row", split_axis=0, concat_axis=1, tiled=True),
    )
    left_full, right_rows = (
        lax.all_gather(left_owned, "col", axis=2, tiled=True),
        lax.all_gather(right_owned, "col", axis=2, tiled=True),
    )
    right_used = lax.dynamic_slice_in_dim(right_rows, col_index * col_count, col_count, 1)
    tri_sum = jnp.einsum(
        "cik,cjk->cij", left_full, right_used, preferred_element_type=jnp.float32
    ).astype(jnp.bfloat16)
    merged = lax.all_to_all(tri_sum, "row", split_axis=1, concat_axis=0, tiled=True)
    tri_norm = layer_norm(merged.astype(jnp.float32), 0).astype(jnp.bfloat16)
    update = jnp.einsum("dij,de->ije", tri_norm, tri_out_weight, preferred_element_type=jnp.float32)
    pair_out = (pair_float + tri_gate * update).astype(jnp.bfloat16)
    band_width = 3 * tok_rows
    targets = (row_index - 1) * tok_rows + jnp.arange(band_width, dtype=jnp.int32)
    columns = col_index * col_count + jnp.arange(col_count, dtype=jnp.int32)
    selector = (columns[:, None] == targets[None, :]).astype(jnp.bfloat16)
    band_part = jnp.einsum("ijd,jb->ibd", pair_out, selector, preferred_element_type=jnp.float32)
    band = lax.psum(band_part.astype(jnp.bfloat16), "col").astype(jnp.float32)
    band_norm = layer_norm(band, 2).astype(jnp.bfloat16)
    bias_table = jnp.einsum(
        "ibd,dh->ibh", band_norm, bias_weight, preferred_element_type=jnp.float32
    ).astype(jnp.bfloat16)
    slab = atom_act.shape[0]
    window_width = atom_act.shape[1]
    heads = bias_weight.shape[1]
    head_size = window_width // heads
    side = (KEYS - QUERY_WINDOW) // 2
    windows = slab // QUERY_WINDOW
    local_token = atom_token - row_index * tok_rows
    live = atom_mask.astype(jnp.float32)
    token_tag = ((local_token + 1) * atom_mask).astype(jnp.bfloat16)
    ada = jnp.dot(atom_cond, ada_weight, preferred_element_type=jnp.float32)
    atom_inputs = (
        jax.nn.sigmoid(ada[:, :window_width]) * layer_norm(atom_act.astype(jnp.float32), 1)
        + ada[:, window_width:]
    ).astype(jnp.bfloat16)
    projected = jnp.dot(atom_inputs, qkv_weight, preferred_element_type=jnp.float32).astype(
        jnp.bfloat16
    )
    queries = projected[:, :window_width]
    ext_pairs, ext_tag = (
        extended(projected[:, window_width:], (("row", 0),), side),
        extended(token_tag, (("row", 0),), side),
    )
    ext_rows = slab + 2 * side
    ext_position = jnp.arange(ext_rows, dtype=jnp.int32)
    offset = jnp.where(
        ext_position < side, 0, jnp.where(ext_position < side + slab, tok_rows, 2 * tok_rows)
    )
    tag_value = ext_tag.astype(jnp.int32)
    key_valid = tag_value > 0
    band_index = tag_value - 1 + offset
    band_slots = jnp.arange(band_width, dtype=jnp.int32)
    key_onehot = ((band_index[:, None] == band_slots[None, :]) & key_valid[:, None]).astype(
        jnp.bfloat16
    )
    query_onehot = (local_token[:, None] == jnp.arange(tok_rows, dtype=jnp.int32)[None, :]).astype(
        jnp.bfloat16
    )
    query_bias = jnp.einsum(
        "lt,tbh->lbh", query_onehot, bias_table, preferred_element_type=jnp.float32
    ).astype(jnp.bfloat16)
    query_bias = query_bias.reshape(windows, QUERY_WINDOW, band_width, heads)
    key_index = (
        jnp.arange(windows, dtype=jnp.int32)[:, None] * QUERY_WINDOW
        + jnp.arange(KEYS, dtype=jnp.int32)[None, :]
    )
    window_pairs = ext_pairs[key_index]
    window_onehot = key_onehot[key_index]
    window_valid = key_valid[key_index]
    window_bias = jnp.einsum(
        "wlbh,wmb->whlm", query_bias, window_onehot, preferred_element_type=jnp.float32
    )
    query_heads = queries.reshape(windows, QUERY_WINDOW, heads, head_size)
    key_heads = window_pairs[..., :window_width].reshape(windows, KEYS, heads, head_size)
    value_heads = window_pairs[..., window_width:].reshape(windows, KEYS, heads, head_size)
    logit_scores = (
        jnp.einsum("wlhd,wmhd->whlm", query_heads, key_heads, preferred_element_type=jnp.float32)
        / math.sqrt(head_size)
        + window_bias
    )
    logit_scores = jnp.where(window_valid[:, None, None, :], logit_scores, -1e30)
    attn_weights = jax.nn.softmax(logit_scores, axis=-1).astype(jnp.bfloat16)
    attended = (
        jnp.einsum("whlm,wmhd->wlhd", attn_weights, value_heads, preferred_element_type=jnp.float32)
        .reshape(slab, window_width)
        .astype(jnp.bfloat16)
    )
    atom_mid = atom_act.astype(jnp.float32) + jnp.dot(
        attended, attn_out_weight, preferred_element_type=jnp.float32
    )
    atom_norm = layer_norm(atom_mid, 1).astype(jnp.bfloat16)
    expanded = jnp.dot(atom_norm, ffn_in_weight, preferred_element_type=jnp.float32)
    hidden_width = ffn_out_weight.shape[0]
    inner = (jax.nn.silu(expanded[:, :hidden_width]) * expanded[:, hidden_width:]).astype(
        jnp.bfloat16
    )
    atom_out = (
        (atom_mid + jnp.dot(inner, ffn_out_weight, preferred_element_type=jnp.float32))
        * live[:, None]
    ).astype(jnp.bfloat16)
    features = jax.nn.relu(
        jnp.dot(atom_out, agg_weight, preferred_element_type=jnp.float32)
    ).astype(jnp.bfloat16)
    live_onehot = query_onehot * atom_mask.astype(jnp.bfloat16)[:, None]
    token_sums = jnp.einsum("at,ac->tc", live_onehot, features, preferred_element_type=jnp.float32)
    token_counts = jnp.sum(live_onehot.astype(jnp.float32), axis=0)
    token_out = (token_sums / token_counts[:, None]).astype(jnp.bfloat16)
    return (pair_out, atom_out, token_out)


LANES = 128
SUBLANES = 8
SIDE = (KEYS - QUERY_WINDOW) // 2
RIM_ROWS = 4
BAND_PAD = 2 * SUBLANES
LIMIT = pltpu.CompilerParams(vmem_limit_bytes=8 << 20)
F32 = jnp.float32
BF16 = jnp.bfloat16
NT = (((1,), (1,)), ((), ()))
TN = (((0,), (0,)), ((), ()))
TT = (((0,), (1,)), ((), ()))


def matmul(a, b, dims=(((1,), (0,)), ((), ()))):
    return lax.dot_general(a, b, dims, preferred_element_type=F32)


def normalize(values, axis):
    average = jnp.mean(values, axis=axis, keepdims=True)
    centred = values - average
    spread = jnp.mean(centred * centred, axis=axis, keepdims=True)
    return centred * lax.rsqrt(spread + EPSILON)


def iota(shape, dim):
    return lax.broadcasted_iota(jnp.int32, shape, dim)


def column_of(row, size):
    eye = iota((size, size), 0) == iota((size, size), 1)
    return jnp.sum(jnp.where(eye, row, 0.0), axis=1, keepdims=True)


def pad_lanes(row):
    return jnp.concatenate([row, jnp.zeros((row.shape[0], LANES - row.shape[1]), row.dtype)], axis=1)


def strided(first, count, step):
    return pl.ds(first, count, stride=step)


def send_kernel(
    n_row, pair_hbm, act_hbm, bias_w_hbm, in_w_hbm, cond_hbm, ada_w_hbm, mask_hbm, token_hbm, alive_hbm,
    pair_ref, act_ref, bias_w_ref, out_ref, inputs_ref, slots_ref,
    in_w_ref, cond_ref, ada_w_ref, mask_ref, token_ref, alive_ref, staged, sems,
):
    sources = (pair_hbm, cond_hbm, act_hbm, mask_hbm, token_hbm, alive_hbm, bias_w_hbm, ada_w_hbm, in_w_hbm)
    places = (pair_ref, cond_ref, act_ref, mask_ref, token_ref, alive_ref, bias_w_ref, ada_w_ref, in_w_ref)
    loads = [pltpu.make_async_copy(a, b, sems.at[i]) for i, (a, b) in enumerate(zip(sources, places))]
    for load in loads:
        load.start()
    loads[0].wait()
    me = lax.axis_index("row")
    rows, cols, channels = pair_ref.shape
    part = channels // n_row
    width = rows * cols
    step = 2 * part * rows + RIM_ROWS
    normed = normalize(pair_ref[...].reshape(width, channels).astype(F32), 1).astype(BF16)
    for load in loads[1:]:
        load.wait()
    live = mask_ref[...].astype(F32)
    lane = iota(live.shape, 1)
    both = jnp.concatenate(
        [live * jnp.sum(jnp.where(lane == me * rows + i, live, 0.0), axis=1, keepdims=True) for i in range(rows)],
        axis=1,
    )
    for side in range(2):
        first = 2 * side * channels
        value = matmul(in_w_ref[:, first : first + channels], normed, TT)
        gate = matmul(in_w_ref[:, first + channels : first + 2 * channels], normed, TT)
        term = jax.nn.sigmoid(gate) * value * both
        for q in range(part):
            for i in range(rows):
                staged[strided((side * part + q) * rows + i, n_row, step)] = term[
                    q * n_row : (q + 1) * n_row, i * cols : (i + 1) * cols
                ]
    act = act_ref[...].astype(F32)
    ada = matmul(cond_ref[...], ada_w_ref[...])
    slab, wide = act.shape
    inputs = (jax.nn.sigmoid(ada[:, :wide]) * normalize(act, 1) + ada[:, wide:]).astype(BF16)
    inputs_ref[...] = inputs
    inputs = inputs.astype(F32)
    token = token_ref[...] - me * rows
    alive = alive_ref[...]
    tag = pad_lanes(((token + 1) * alive).astype(F32))
    slots_ref[...] = jnp.zeros(slots_ref.shape, F32)
    slots_ref[0:1] = pad_lanes(token.astype(F32))
    slots_ref[1:2] = pad_lanes(alive.astype(F32))
    slots_ref[2:3] = tag
    tags = jnp.broadcast_to(tag, (2 * n_row - SIDE, LANES))
    for d, rim in enumerate((inputs[slab - SIDE :], inputs[:SIDE])):
        block = jnp.concatenate([rim, tags], axis=0)
        for s in range(RIM_ROWS // 2):
            staged[strided(step - RIM_ROWS + d * (RIM_ROWS // 2) + s, n_row, step)] = block[
                s * n_row : (s + 1) * n_row
            ]
    out_ref[...] = staged[...].astype(BF16)


def prepare(
    pair_ref, gate_w_ref, inputs_ref, qkv_w_ref, slots_ref,
    gate_ref, qkv_ref, query_hot_ref, live_ref, member_ref,
):
    rows, cols, channels = pair_ref.shape
    slab = inputs_ref.shape[0]
    token = slots_ref[0:1, :slab]
    alive = slots_ref[1:2, :slab]
    qkv_ref[...] = matmul(inputs_ref[...], qkv_w_ref[...]).astype(BF16)
    token_col = column_of(token, slab)
    query_hot_ref[...] = (token_col == (iota(query_hot_ref.shape, 1) // BAND_PAD).astype(F32)).astype(F32)
    live_ref[...] = jnp.broadcast_to(column_of(alive, slab), live_ref.shape)
    member_ref[...] = jnp.where(iota(member_ref.shape, 0).astype(F32) == token, alive, 0.0)
    normed = normalize(pair_ref[...].reshape(rows * cols, channels).astype(F32), 1).astype(BF16)
    gate_ref[...] = jax.nn.sigmoid(matmul(normed, gate_w_ref[...]))


def triangle_kernel(n_row, rows, got_ref, *refs):
    out_ref = refs[5]
    taken, right_terms, staged = refs[11:]
    prepare(*refs[:5], *refs[6:11])
    taken[...] = got_ref[...].astype(F32)
    step = got_ref.shape[0] // n_row
    part = right_terms.shape[0]
    out_step = part * rows + RIM_ROWS
    for q in range(part):
        left = jnp.concatenate(
            [taken[strided(q * rows + i, n_row, step)] for i in range(rows)], axis=0
        ).astype(BF16)
        for j in range(rows):
            right_terms[q, strided(j, n_row, rows)] = taken[strided((part + q) * rows + j, n_row, step)]
        summed = matmul(left, right_terms[q].astype(BF16), NT)
        for i in range(rows):
            staged[strided(q * rows + i, n_row, out_step)] = summed[i * n_row : (i + 1) * n_row]
    nothing = jnp.zeros((1, LANES), F32)
    for s in range(RIM_ROWS):
        rim = taken[strided(step - RIM_ROWS + s, n_row, step)]
        if s < RIM_ROWS // 2:
            rim = jnp.concatenate([nothing, rim[:-1]], axis=0)
        else:
            rim = jnp.concatenate([rim[1:], nothing], axis=0)
        staged[strided(out_step - RIM_ROWS + s, n_row, out_step)] = rim
    out_ref[...] = staged[...].astype(BF16)


def finish_kernel(
    n_row, got_ref, pair_ref, out_w_ref, act_ref, slots_ref, bias_w_ref, gate_ref, qkv_ref, query_hot_ref, live_ref,
    member_ref, qkv_w_ref, attn_w_ref, ffn_in_ref, ffn_out_ref, agg_ref,
    pair_out, atom_out, token_out, taken, pair_new, atom_new, token_new, padded, products, values_ext, sems,
):
    me = lax.axis_index("row")
    rows, cols, channels = pair_ref.shape
    part = channels // n_row
    step = part * rows + RIM_ROWS
    half = RIM_ROWS // 2
    slab, wide = act_ref.shape
    heads = bias_w_ref.shape[0]
    head_size = wide // heads
    head_of = iota((QUERY_WINDOW, wide), 1) // head_size
    windows = slab // QUERY_WINDOW
    taken[...] = got_ref[...].astype(F32)
    sums = [
        jnp.concatenate([taken[strided(q * rows + i, n_row, step)] for q in range(part)], axis=0) for i in range(rows)
    ]
    outer = jnp.concatenate(
        [
            taken[strided(step - RIM_ROWS + d * half + s, n_row, step)][: min(n_row, SIDE - s * n_row)]
            for d in range(2)
            for s in range(half)
        ],
        axis=0,
    ).astype(BF16)
    outer = matmul(outer, qkv_w_ref[:, wide:]).astype(BF16).astype(F32)
    own = qkv_ref[...].astype(F32)
    keys_ext, values = (
        jnp.concatenate(
            [outer[:SIDE, at : at + wide], own[:, wide + at : 2 * wide + at], outer[SIDE:, at : at + wide]], axis=0
        )
        for at in (0, wide)
    )
    values_ext[...] = values
    for w in range(windows):
        start = w * QUERY_WINDOW
        query = own[start : start + QUERY_WINDOW, :wide]
        split = jnp.concatenate([jnp.where(head_of == h, query, 0.0) for h in range(heads)], axis=0).astype(BF16)
        products[w] = matmul(split, keys_ext[start : start + KEYS].astype(BF16), NT) * (1 / math.sqrt(head_size))
    for i in range(rows):
        update = matmul(normalize(sums[i], 0).astype(BF16), out_w_ref[...], TN)
        fresh = (pair_ref[i].astype(F32) + gate_ref[i * cols : (i + 1) * cols] * update).astype(BF16)
        pair_new[i] = fresh
        padded[i, :SUBLANES] = jnp.zeros((SUBLANES, channels), F32)
        padded[i, SUBLANES : SUBLANES + cols] = fresh.astype(F32)
        padded[i, SUBLANES + cols :] = jnp.zeros((BAND_PAD, channels), F32)
    pair_copy = pltpu.make_async_copy(pair_new, pair_out, sems.at[0])
    atom_copy = pltpu.make_async_copy(atom_new, atom_out, sems.at[1])
    token_copy = pltpu.make_async_copy(token_new, token_out, sems.at[2])
    pair_copy.start()

    @pl.when(me >= 0)
    def _():
        band = [padded[i, pl.ds(SUBLANES + (me - 1) * rows, BAND_PAD)] for i in range(rows)]
        band = normalize(jnp.concatenate(band, axis=0), 1).astype(BF16)
        bias_rows = matmul(bias_w_ref[...], band, NT).astype(BF16).astype(F32)
        tag_at = [(step - RIM_ROWS + d * half + SIDE // n_row) + step * (SIDE % n_row) for d in range(2)]
        before_tag, after_tag = (taken[at : at + 1] for at in tag_at)
        own_tag = slots_ref[2:3]
        query_hot = query_hot_ref[...]
        flat = query_hot.shape[1]
        slot = (iota((flat, KEYS), 0) % BAND_PAD).astype(F32)
        lane = iota((1, LANES), 1)
        mixed = []
        for w in range(windows):
            start = w * QUERY_WINDOW
            before_end = SIDE - start
            own_end = before_end + slab
            is_before, is_own = lane < before_end, lane < own_end
            tag = jnp.where(
                is_before,
                pltpu.roll(before_tag, (SIDE - slab - start) % LANES, 1),
                jnp.where(
                    is_own, pltpu.roll(own_tag, before_end % LANES, 1), pltpu.roll(after_tag, own_end % LANES, 1)
                ),
            )
            offset = jnp.where(is_before, 0.0, jnp.where(is_own, 1.0 * rows, 2.0 * rows))
            valid = tag > 0
            key_slot = jnp.where(valid, tag - 1 + offset, -1.0)
            key_hot = (slot == key_slot).astype(BF16)
            hot = query_hot[start : start + QUERY_WINDOW]
            hot_bias = jnp.concatenate([hot * bias_rows[h : h + 1] for h in range(heads)], axis=0).astype(BF16)
            scores = jnp.where(valid, products[w] + matmul(hot_bias, key_hot), -1e30)
            powers = jnp.exp(scores - jnp.max(scores, axis=1, keepdims=True))
            blend = matmul(powers.astype(BF16), values_ext[start : start + KEYS].astype(BF16))
            blend = blend / jnp.sum(powers, axis=1, keepdims=True)
            total = jnp.zeros((QUERY_WINDOW, wide), F32)
            for h in range(heads):
                total = jnp.where(head_of == h, blend[h * QUERY_WINDOW : (h + 1) * QUERY_WINDOW], total)
            mixed.append(total)
        attended = jnp.concatenate(mixed, axis=0).astype(BF16)
        middle = act_ref[...].astype(F32) + matmul(attended, attn_w_ref[...])
        expanded = matmul(normalize(middle, 1).astype(BF16), ffn_in_ref[...])
        hidden = ffn_out_ref.shape[0]
        inner = (jax.nn.silu(expanded[:, :hidden]) * expanded[:, hidden:]).astype(BF16)
        final = ((middle + matmul(inner, ffn_out_ref[...])) * live_ref[...]).astype(BF16)
        atom_new[...] = final
        atom_copy.start()
        features = jnp.maximum(matmul(final, agg_ref[...]), 0.0).astype(BF16)
        member = member_ref[...]
        totals = matmul(member.astype(BF16), features)
        counts = jnp.maximum(jnp.sum(member, axis=1, keepdims=True), 1.0)
        token_new[...] = (totals / counts).astype(BF16)[:rows]
        token_copy.start()

    pair_copy.wait()
    atom_copy.wait()
    token_copy.wait()


def in_vmem(count):
    return [pl.BlockSpec(memory_space=pltpu.VMEM)] * count


def in_hbm(arrays):
    return [pltpu.with_memory_space_constraint(a, pltpu.HBM) for a in arrays]


def cost(flops, nbytes, exps=0):
    return pl.CostEstimate(flops=flops, bytes_accessed=nbytes, transcendentals=exps)


def exchange(blocks, n_row):
    grouped = blocks.reshape(n_row, -1, RIM_ROWS, LANES)
    return lax.all_to_all(grouped, "row", split_axis=0, concat_axis=0, tiled=True).reshape(blocks.shape)


def by_kernels(
    pair, token_mask, tri_in_weight, tri_gate_weight, tri_out_weight, atom_act, atom_cond, atom_token, atom_mask,
    ada_weight, qkv_weight, bias_weight, attn_out_weight, ffn_in_weight, ffn_out_weight, agg_weight,
):
    n_row = lax.axis_size("row")
    rows, cols, channels = pair.shape
    slab, wide = atom_act.shape
    width = rows * cols
    part = channels // n_row
    mask = token_mask.reshape(1, -1)
    token = atom_token.reshape(1, -1)
    alive = atom_mask.reshape(1, -1)
    sent = n_row * (2 * part * rows + RIM_ROWS)
    back_rows = n_row * (part * rows + RIM_ROWS)
    sources = (pair, atom_act, bias_weight.T, tri_in_weight, atom_cond, ada_weight, mask, token, alive)
    kept = 3
    pair, atom_act, bias_rows, terms, inputs, slots = pl.pallas_call(
        functools.partial(send_kernel, n_row),
        out_shape=(
            *(jax.ShapeDtypeStruct(a.shape, a.dtype) for a in sources[:kept]),
            jax.ShapeDtypeStruct((sent, LANES), BF16),
            jax.ShapeDtypeStruct((slab, wide), BF16),
            jax.ShapeDtypeStruct((SUBLANES, LANES), F32),
        ),
        in_specs=[pl.BlockSpec(memory_space=pltpu.HBM)] * len(sources),
        out_specs=tuple(in_vmem(kept + 3)),
        scratch_shapes=[
            *(pltpu.VMEM(a.shape, a.dtype) for a in sources[kept:]),
            pltpu.VMEM((sent, LANES), F32),
            pltpu.SemaphoreType.DMA((len(sources),)),
        ],
        cost_estimate=cost(8 * width * channels * channels, 1 << 20, 2 * width * channels),
        compiler_params=LIMIT,
        name="send",
    )(*in_hbm(sources))
    got = exchange(terms, n_row)
    sums, *prepared = pl.pallas_call(
        functools.partial(triangle_kernel, n_row, rows),
        out_shape=(
            jax.ShapeDtypeStruct((back_rows, LANES), BF16),
            jax.ShapeDtypeStruct((width, channels), F32),
            jax.ShapeDtypeStruct((slab, 3 * wide), BF16),
            jax.ShapeDtypeStruct((slab, rows * BAND_PAD), F32),
            jax.ShapeDtypeStruct((slab, wide), F32),
            jax.ShapeDtypeStruct((SUBLANES, slab), F32),
        ),
        in_specs=in_vmem(6),
        out_specs=tuple(in_vmem(6)),
        scratch_shapes=[
            pltpu.VMEM((sent, LANES), F32),
            pltpu.VMEM((part, cols, cols), F32),
            pltpu.VMEM((back_rows, LANES), F32),
        ],
        cost_estimate=cost(2 * width * width, 1 << 19),
        compiler_params=LIMIT,
        name="triangle",
    )(got, pair, tri_gate_weight, inputs, qkv_weight, slots)
    back = exchange(sums, n_row)
    token_shape = (rows, agg_weight.shape[1])
    return pl.pallas_call(
        functools.partial(finish_kernel, n_row),
        out_shape=(
            jax.ShapeDtypeStruct(pair.shape, BF16),
            jax.ShapeDtypeStruct(atom_act.shape, BF16),
            jax.ShapeDtypeStruct(token_shape, BF16),
        ),
        in_specs=in_vmem(16),
        out_specs=(pl.BlockSpec(memory_space=pltpu.HBM),) * 3,
        scratch_shapes=[
            pltpu.VMEM((back_rows, LANES), F32),
            pltpu.VMEM(pair.shape, BF16),
            pltpu.VMEM(atom_act.shape, BF16),
            pltpu.VMEM(token_shape, BF16),
            pltpu.VMEM((rows, SUBLANES + cols + BAND_PAD, channels), F32),
            pltpu.VMEM((slab // QUERY_WINDOW, bias_weight.shape[1] * QUERY_WINDOW, KEYS), F32),
            pltpu.VMEM((slab + 2 * SIDE, wide), F32),
            pltpu.SemaphoreType.DMA((3,)),
        ],
        cost_estimate=cost(4 * width * channels * channels, 1 << 20),
        compiler_params=LIMIT,
        name="finish",
    )(
        back, pair, tri_out_weight, atom_act, slots, bias_rows, *prepared, qkv_weight, attn_out_weight, ffn_in_weight,
        ffn_out_weight, agg_weight,
    )


def kernels_fit(mesh, args):
    pair, atom_act, bias_weight = args[0], args[5], args[11]
    n_row = mesh.shape["row"]
    parts = mesh.shape["groups"] * n_row
    cols, channels = pair.shape[1:]
    rows = pair.shape[0] // parts
    slab = atom_act.shape[0] // parts
    wide = atom_act.shape[1]
    return (
        mesh.shape["col"] == 1
        and cols == channels == wide == LANES
        and cols == n_row * rows
        and channels % n_row == 0
        and n_row % SUBLANES == 0
        and SIDE < RIM_ROWS // 2 * n_row
        and 3 * rows <= BAND_PAD
        and rows <= SUBLANES
        and SIDE <= slab <= LANES
        and slab % QUERY_WINDOW == 0
        and slab - QUERY_WINDOW <= SIDE
        and wide % bias_weight.shape[1] == 0
    )


def solution(mesh):
    in_specs = (
        P(("groups", "row"), "col", None),
        P("groups"),
        P(),
        P(),
        P(),
        P(("groups", "row"), None),
        P(("groups", "row"), None),
        P(("groups", "row")),
        P(("groups", "row")),
        P(),
        P(),
        P(),
        P(),
        P(),
        P(),
        P(),
    )
    out_specs = (
        P(("groups", "row"), "col", None),
        P(("groups", "row"), None),
        P(("groups", "row"), None),
    )

    def layer(*args):
        body = by_kernels if kernels_fit(mesh, args) else per_device
        return jax.shard_map(body, mesh=mesh, in_specs=in_specs, out_specs=out_specs, check_vma=False)(*args)

    return layer
```

```python
import functools
import math

import jax
import jax.numpy as jnp
from jax import lax
from jax.experimental import pallas as pl
from jax.experimental.pallas import tpu as pltpu
from jax.sharding import PartitionSpec as P

QUERY_WINDOW = 32
KEYS = 128


EPSILON = 1e-05


def extended(shard, sides, width):
    for axis, dim in sides:
        size, length = (lax.axis_size(axis), shard.shape[dim])
        up = [(i, (i + 1) % size) for i in range(size - 1)]
        down = [(j, i) for i, j in up]
        last = lax.slice_in_dim(shard, length - width, length, axis=dim)
        first = lax.slice_in_dim(shard, 0, width, axis=dim)
        before = lax.ppermute(last, axis, up)
        after = lax.ppermute(first, axis, down)
        shard = jnp.concatenate([before, shard, after], axis=dim)
    return shard


def layer_norm(values, along):
    average = jnp.mean(values, axis=along, keepdims=True)
    centred = values - average
    spread = jnp.mean(centred * centred, axis=along, keepdims=True)
    return centred / jnp.sqrt(spread + EPSILON)


def per_device(
    pair,
    token_mask,
    tri_in_weight,
    tri_gate_weight,
    tri_out_weight,
    atom_act,
    atom_cond,
    atom_token,
    atom_mask,
    ada_weight,
    qkv_weight,
    bias_weight,
    attn_out_weight,
    ffn_in_weight,
    ffn_out_weight,
    agg_weight,
):
    tok_rows = pair.shape[0]
    col_count = pair.shape[1]
    channels = pair.shape[2]
    row_index = lax.axis_index("row")
    col_index = lax.axis_index("col")
    pair_float = pair.astype(jnp.float32)
    pair_norm = layer_norm(pair_float, 2).astype(jnp.bfloat16)
    row_live = lax.dynamic_slice_in_dim(token_mask, row_index * tok_rows, tok_rows, 0).astype(
        jnp.float32
    )
    col_live = lax.dynamic_slice_in_dim(token_mask, col_index * col_count, col_count, 0).astype(
        jnp.float32
    )
    pair_live = row_live[:, None] * col_live[None, :]
    left_terms = jnp.einsum(
        "ijd,de->eij",
        pair_norm,
        tri_in_weight[:, : 2 * channels],
        preferred_element_type=jnp.float32,
    )
    left = (jax.nn.sigmoid(left_terms[channels:]) * left_terms[:channels] * pair_live).astype(
        jnp.bfloat16
    )
    right_terms = jnp.einsum(
        "ijd,de->eij",
        pair_norm,
        tri_in_weight[:, 2 * channels :],
        preferred_element_type=jnp.float32,
    )
    right = (jax.nn.sigmoid(right_terms[channels:]) * right_terms[:channels] * pair_live).astype(
        jnp.bfloat16
    )
    tri_gate = jax.nn.sigmoid(
        jnp.einsum("ijd,de->ije", pair_norm, tri_gate_weight, preferred_element_type=jnp.float32)
    )
    left_owned, right_owned = (
        lax.all_to_all(left, "row", split_axis=0, concat_axis=1, tiled=True),
        lax.all_to_all(right, "row", split_axis=0, concat_axis=1, tiled=True),
    )
    left_full, right_rows = (
        lax.all_gather(left_owned, "col", axis=2, tiled=True),
        lax.all_gather(right_owned, "col", axis=2, tiled=True),
    )
    right_used = lax.dynamic_slice_in_dim(right_rows, col_index * col_count, col_count, 1)
    tri_sum = jnp.einsum(
        "cik,cjk->cij", left_full, right_used, preferred_element_type=jnp.float32
    ).astype(jnp.bfloat16)
    merged = lax.all_to_all(tri_sum, "row", split_axis=1, concat_axis=0, tiled=True)
    tri_norm = layer_norm(merged.astype(jnp.float32), 0).astype(jnp.bfloat16)
    update = jnp.einsum("dij,de->ije", tri_norm, tri_out_weight, preferred_element_type=jnp.float32)
    pair_out = (pair_float + tri_gate * update).astype(jnp.bfloat16)
    band_width = 3 * tok_rows
    targets = (row_index - 1) * tok_rows + jnp.arange(band_width, dtype=jnp.int32)
    columns = col_index * col_count + jnp.arange(col_count, dtype=jnp.int32)
    selector = (columns[:, None] == targets[None, :]).astype(jnp.bfloat16)
    band_part = jnp.einsum("ijd,jb->ibd", pair_out, selector, preferred_element_type=jnp.float32)
    band = lax.psum(band_part.astype(jnp.bfloat16), "col").astype(jnp.float32)
    band_norm = layer_norm(band, 2).astype(jnp.bfloat16)
    bias_table = jnp.einsum(
        "ibd,dh->ibh", band_norm, bias_weight, preferred_element_type=jnp.float32
    ).astype(jnp.bfloat16)
    slab = atom_act.shape[0]
    window_width = atom_act.shape[1]
    heads = bias_weight.shape[1]
    head_size = window_width // heads
    side = (KEYS - QUERY_WINDOW) // 2
    windows = slab // QUERY_WINDOW
    local_token = atom_token - row_index * tok_rows
    live = atom_mask.astype(jnp.float32)
    token_tag = ((local_token + 1) * atom_mask).astype(jnp.bfloat16)
    ada = jnp.dot(atom_cond, ada_weight, preferred_element_type=jnp.float32)
    atom_inputs = (
        jax.nn.sigmoid(ada[:, :window_width]) * layer_norm(atom_act.astype(jnp.float32), 1)
        + ada[:, window_width:]
    ).astype(jnp.bfloat16)
    projected = jnp.dot(atom_inputs, qkv_weight, preferred_element_type=jnp.float32).astype(
        jnp.bfloat16
    )
    queries = projected[:, :window_width]
    ext_pairs, ext_tag = (
        extended(projected[:, window_width:], (("row", 0),), side),
        extended(token_tag, (("row", 0),), side),
    )
    ext_rows = slab + 2 * side
    ext_position = jnp.arange(ext_rows, dtype=jnp.int32)
    offset = jnp.where(
        ext_position < side, 0, jnp.where(ext_position < side + slab, tok_rows, 2 * tok_rows)
    )
    tag_value = ext_tag.astype(jnp.int32)
    key_valid = tag_value > 0
    band_index = tag_value - 1 + offset
    band_slots = jnp.arange(band_width, dtype=jnp.int32)
    key_onehot = ((band_index[:, None] == band_slots[None, :]) & key_valid[:, None]).astype(
        jnp.bfloat16
    )
    query_onehot = (local_token[:, None] == jnp.arange(tok_rows, dtype=jnp.int32)[None, :]).astype(
        jnp.bfloat16
    )
    query_bias = jnp.einsum(
        "lt,tbh->lbh", query_onehot, bias_table, preferred_element_type=jnp.float32
    ).astype(jnp.bfloat16)
    query_bias = query_bias.reshape(windows, QUERY_WINDOW, band_width, heads)
    key_index = (
        jnp.arange(windows, dtype=jnp.int32)[:, None] * QUERY_WINDOW
        + jnp.arange(KEYS, dtype=jnp.int32)[None, :]
    )
    window_pairs = ext_pairs[key_index]
    window_onehot = key_onehot[key_index]
    window_valid = key_valid[key_index]
    window_bias = jnp.einsum(
        "wlbh,wmb->whlm", query_bias, window_onehot, preferred_element_type=jnp.float32
    )
    query_heads = queries.reshape(windows, QUERY_WINDOW, heads, head_size)
    key_heads = window_pairs[..., :window_width].reshape(windows, KEYS, heads, head_size)
    value_heads = window_pairs[..., window_width:].reshape(windows, KEYS, heads, head_size)
    logit_scores = (
        jnp.einsum("wlhd,wmhd->whlm", query_heads, key_heads, preferred_element_type=jnp.float32)
        / math.sqrt(head_size)
        + window_bias
    )
    logit_scores = jnp.where(window_valid[:, None, None, :], logit_scores, -1e30)
    attn_weights = jax.nn.softmax(logit_scores, axis=-1).astype(jnp.bfloat16)
    attended = (
        jnp.einsum("whlm,wmhd->wlhd", attn_weights, value_heads, preferred_element_type=jnp.float32)
        .reshape(slab, window_width)
        .astype(jnp.bfloat16)
    )
    atom_mid = atom_act.astype(jnp.float32) + jnp.dot(
        attended, attn_out_weight, preferred_element_type=jnp.float32
    )
    atom_norm = layer_norm(atom_mid, 1).astype(jnp.bfloat16)
    expanded = jnp.dot(atom_norm, ffn_in_weight, preferred_element_type=jnp.float32)
    hidden_width = ffn_out_weight.shape[0]
    inner = (jax.nn.silu(expanded[:, :hidden_width]) * expanded[:, hidden_width:]).astype(
        jnp.bfloat16
    )
    atom_out = (
        (atom_mid + jnp.dot(inner, ffn_out_weight, preferred_element_type=jnp.float32))
        * live[:, None]
    ).astype(jnp.bfloat16)
    features = jax.nn.relu(
        jnp.dot(atom_out, agg_weight, preferred_element_type=jnp.float32)
    ).astype(jnp.bfloat16)
    live_onehot = query_onehot * atom_mask.astype(jnp.bfloat16)[:, None]
    token_sums = jnp.einsum("at,ac->tc", live_onehot, features, preferred_element_type=jnp.float32)
    token_counts = jnp.sum(live_onehot.astype(jnp.float32), axis=0)
    token_out = (token_sums / token_counts[:, None]).astype(jnp.bfloat16)
    return (pair_out, atom_out, token_out)


LANES = 128
SUBLANES = 8
SIDE = (KEYS - QUERY_WINDOW) // 2
RIM_ROWS = 4
BAND_PAD = 2 * SUBLANES
LIMIT = pltpu.CompilerParams(vmem_limit_bytes=8 << 20)
F32 = jnp.float32
BF16 = jnp.bfloat16
NT = (((1,), (1,)), ((), ()))
TN = (((0,), (0,)), ((), ()))
TT = (((0,), (1,)), ((), ()))


def matmul(a, b, dims=(((1,), (0,)), ((), ()))):
    return lax.dot_general(a, b, dims, preferred_element_type=F32)


def normalize(values, axis):
    average = jnp.mean(values, axis=axis, keepdims=True)
    centred = values - average
    spread = jnp.mean(centred * centred, axis=axis, keepdims=True)
    return centred * lax.rsqrt(spread + EPSILON)


def iota(shape, dim):
    return lax.broadcasted_iota(jnp.int32, shape, dim)


def column_of(row, size):
    eye = iota((size, size), 0) == iota((size, size), 1)
    return jnp.sum(jnp.where(eye, row, 0.0), axis=1, keepdims=True)


def pad_lanes(row):
    return jnp.concatenate([row, jnp.zeros((row.shape[0], LANES - row.shape[1]), row.dtype)], axis=1)


def strided(first, count, step):
    return pl.ds(first, count, stride=step)


def send_kernel(
    n_row, pair_hbm, act_hbm, bias_w_hbm, in_w_hbm, cond_hbm, ada_w_hbm, mask_hbm, token_hbm, alive_hbm,
    pair_ref, act_ref, bias_w_ref, out_ref, inputs_ref, slots_ref,
    in_w_ref, cond_ref, ada_w_ref, mask_ref, token_ref, alive_ref, staged, sems,
):
    sources = (pair_hbm, cond_hbm, act_hbm, mask_hbm, token_hbm, alive_hbm, bias_w_hbm, ada_w_hbm, in_w_hbm)
    places = (pair_ref, cond_ref, act_ref, mask_ref, token_ref, alive_ref, bias_w_ref, ada_w_ref, in_w_ref)
    loads = [pltpu.make_async_copy(a, b, sems.at[i]) for i, (a, b) in enumerate(zip(sources, places))]
    for load in loads:
        load.start()
    loads[0].wait()
    me = lax.axis_index("row")
    rows, cols, channels = pair_ref.shape
    part = channels // n_row
    width = rows * cols
    step = 2 * part * rows + RIM_ROWS
    normed = normalize(pair_ref[...].reshape(width, channels).astype(F32), 1).astype(BF16)
    for load in loads[1:]:
        load.wait()
    live = mask_ref[...].astype(F32)
    lane = iota(live.shape, 1)
    both = jnp.concatenate(
        [live * jnp.sum(jnp.where(lane == me * rows + i, live, 0.0), axis=1, keepdims=True) for i in range(rows)],
        axis=1,
    )
    for side in range(2):
        first = 2 * side * channels
        value = matmul(in_w_ref[:, first : first + channels], normed, TT)
        gate = matmul(in_w_ref[:, first + channels : first + 2 * channels], normed, TT)
        term = jax.nn.sigmoid(gate) * value * both
        for q in range(part):
            for i in range(rows):
                staged[strided((side * part + q) * rows + i, n_row, step)] = term[
                    q * n_row : (q + 1) * n_row, i * cols : (i + 1) * cols
                ]
    act = act_ref[...].astype(F32)
    ada = matmul(cond_ref[...], ada_w_ref[...])
    slab, wide = act.shape
    inputs = (jax.nn.sigmoid(ada[:, :wide]) * normalize(act, 1) + ada[:, wide:]).astype(BF16)
    inputs_ref[...] = inputs
    inputs = inputs.astype(F32)
    token = token_ref[...] - me * rows
    alive = alive_ref[...]
    tag = pad_lanes(((token + 1) * alive).astype(F32))
    slots_ref[...] = jnp.zeros(slots_ref.shape, F32)
    slots_ref[0:1] = pad_lanes(token.astype(F32))
    slots_ref[1:2] = pad_lanes(alive.astype(F32))
    slots_ref[2:3] = tag
    tags = jnp.broadcast_to(tag, (2 * n_row - SIDE, LANES))
    for d, rim in enumerate((inputs[slab - SIDE :], inputs[:SIDE])):
        block = jnp.concatenate([rim, tags], axis=0)
        for s in range(RIM_ROWS // 2):
            staged[strided(step - RIM_ROWS + d * (RIM_ROWS // 2) + s, n_row, step)] = block[
                s * n_row : (s + 1) * n_row
            ]
    out_ref[...] = staged[...].astype(BF16)


def prepare(
    pair_ref, gate_w_ref, inputs_ref, qkv_w_ref, slots_ref, act_ref, attn_w_ref,
    gate_ref, qkv_ref, query_hot_ref, live_ref, member_ref, counts_ref, act_mean_ref, attn_wide_ref,
):
    rows, cols, channels = pair_ref.shape
    slab = inputs_ref.shape[0]
    token = slots_ref[0:1, :slab]
    alive = slots_ref[1:2, :slab]
    qkv_ref[...] = matmul(inputs_ref[...], qkv_w_ref[...]).astype(BF16)
    token_col = column_of(token, slab)
    query_hot_ref[...] = (token_col == (iota(query_hot_ref.shape, 1) // BAND_PAD).astype(F32)).astype(F32)
    live_ref[...] = jnp.broadcast_to(column_of(alive, slab), live_ref.shape)
    live_col = column_of(alive, slab)
    for t in range(rows):
        member_ref[t] = jnp.broadcast_to(jnp.where(token_col == t, live_col, 0.0), member_ref.shape[1:])
    counts = jnp.sum(jnp.where(iota((SUBLANES, slab), 0).astype(F32) == token, alive, 0.0), axis=1, keepdims=True)
    counts_ref[...] = jnp.broadcast_to(jnp.maximum(counts, 1.0), counts_ref.shape)
    act_mean_ref[...] = jnp.broadcast_to(jnp.mean(act_ref[...].astype(F32), axis=1, keepdims=True), act_mean_ref.shape)
    wide = attn_w_ref.shape[1]
    attn_wide_ref[:, :wide] = attn_w_ref[...]
    rest = jnp.broadcast_to(jnp.mean(attn_w_ref[...].astype(F32), axis=1, keepdims=True), attn_w_ref.shape)
    for k in range(1, 4):
        piece = rest.astype(BF16)
        attn_wide_ref[:, k * wide : (k + 1) * wide] = piece
        rest = rest - piece.astype(F32)
    normed = normalize(pair_ref[...].reshape(rows * cols, channels).astype(F32), 1).astype(BF16)
    gate_ref[...] = jax.nn.sigmoid(matmul(normed, gate_w_ref[...]))


def triangle_kernel(n_row, rows, got_ref, *refs):
    out_ref = refs[7]
    taken, right_terms, staged = refs[16:]
    prepare(*refs[:7], *refs[8:16])
    taken[...] = got_ref[...].astype(F32)
    step = got_ref.shape[0] // n_row
    part = right_terms.shape[0]
    out_step = part * rows + RIM_ROWS
    for q in range(part):
        left = jnp.concatenate(
            [taken[strided(q * rows + i, n_row, step)] for i in range(rows)], axis=0
        ).astype(BF16)
        for j in range(rows):
            right_terms[q, strided(j, n_row, rows)] = taken[strided((part + q) * rows + j, n_row, step)]
        summed = matmul(left, right_terms[q].astype(BF16), NT)
        for i in range(rows):
            staged[strided(q * rows + i, n_row, out_step)] = summed[i * n_row : (i + 1) * n_row]
    nothing = jnp.zeros((1, LANES), F32)
    for s in range(RIM_ROWS):
        rim = taken[strided(step - RIM_ROWS + s, n_row, step)]
        if s < RIM_ROWS // 2:
            rim = jnp.concatenate([nothing, rim[:-1]], axis=0)
        else:
            rim = jnp.concatenate([rim[1:], nothing], axis=0)
        staged[strided(out_step - RIM_ROWS + s, n_row, out_step)] = rim
    out_ref[...] = staged[...].astype(BF16)


def finish_kernel(
    n_row, got_ref, pair_ref, out_w_ref, act_ref, slots_ref, bias_w_ref, gate_ref, qkv_ref, query_hot_ref, live_ref,
    member_ref, counts_ref, act_mean_ref, attn_wide_ref, qkv_w_ref, ffn_in_ref, ffn_out_ref, agg_ref,
    pair_out, atom_out, token_out, taken, pair_new, atom_new, token_new, padded, products, values_ext, key_slots, sems,
):
    me = lax.axis_index("row")
    rows, cols, channels = pair_ref.shape
    part = channels // n_row
    step = part * rows + RIM_ROWS
    half = RIM_ROWS // 2
    slab, wide = act_ref.shape
    heads = bias_w_ref.shape[0]
    head_size = wide // heads
    head_of = iota((QUERY_WINDOW, wide), 1) // head_size
    windows = slab // QUERY_WINDOW
    taken[...] = got_ref[...].astype(F32)
    sums = [
        jnp.concatenate([taken[strided(q * rows + i, n_row, step)] for q in range(part)], axis=0) for i in range(rows)
    ]
    outer = jnp.concatenate(
        [
            taken[strided(step - RIM_ROWS + d * half + s, n_row, step)][: min(n_row, SIDE - s * n_row)]
            for d in range(2)
            for s in range(half)
        ],
        axis=0,
    ).astype(BF16)
    outer = matmul(outer, qkv_w_ref[:, wide:]).astype(BF16).astype(F32)
    own = qkv_ref[...].astype(F32)
    keys_ext, values = (
        jnp.concatenate(
            [outer[:SIDE, at : at + wide], own[:, wide + at : 2 * wide + at], outer[SIDE:, at : at + wide]], axis=0
        )
        for at in (0, wide)
    )
    values_ext[...] = values
    tag_at = [(step - RIM_ROWS + d * half + SIDE // n_row) + step * (SIDE % n_row) for d in range(2)]
    before_tag, after_tag = (taken[at : at + 1] for at in tag_at)
    own_tag = slots_ref[2:3]
    lane = iota((1, LANES), 1)
    for w in range(windows):
        start = w * QUERY_WINDOW
        query = own[start : start + QUERY_WINDOW, :wide]
        split = jnp.concatenate([jnp.where(head_of == h, query, 0.0) for h in range(heads)], axis=0).astype(BF16)
        before_end = SIDE - start
        own_end = before_end + slab
        is_before, is_own = lane < before_end, lane < own_end
        tag = jnp.where(
            is_before,
            pltpu.roll(before_tag, (SIDE - slab - start) % LANES, 1),
            jnp.where(
                is_own, pltpu.roll(own_tag, before_end % LANES, 1), pltpu.roll(after_tag, own_end % LANES, 1)
            ),
        )
        offset = jnp.where(is_before, 0.0, jnp.where(is_own, 1.0 * rows, 2.0 * rows))
        valid = tag > 0
        key_slot = jnp.where(valid, tag - 1 + offset, -1.0)
        key_slots[w : w + 1] = key_slot
        product = matmul(split, keys_ext[start : start + KEYS].astype(BF16), NT) * (1 / math.sqrt(head_size))
        product = jnp.where(valid, product, -1e30)
        products[w] = product - jnp.max(product, axis=1, keepdims=True)
    for i in range(rows):
        update = matmul(normalize(sums[i], 0).astype(BF16), out_w_ref[...], TN)
        fresh = (pair_ref[i].astype(F32) + gate_ref[i * cols : (i + 1) * cols] * update).astype(BF16)
        pair_new[i] = fresh
        padded[i, :SUBLANES] = jnp.zeros((SUBLANES, channels), F32)
        padded[i, SUBLANES : SUBLANES + cols] = fresh.astype(F32)
        padded[i, SUBLANES + cols :] = jnp.zeros((BAND_PAD, channels), F32)
    pair_copy = pltpu.make_async_copy(pair_new, pair_out, sems.at[0])
    atom_copy = pltpu.make_async_copy(atom_new, atom_out, sems.at[1])
    token_copy = pltpu.make_async_copy(token_new, token_out, sems.at[2])
    pair_copy.start()

    @pl.when(me >= 0)
    def _():
        band = [padded[i, pl.ds(SUBLANES + (me - 1) * rows, BAND_PAD)] for i in range(rows)]
        band = normalize(jnp.concatenate(band, axis=0), 1).astype(BF16)
        bias_rows = matmul(bias_w_ref[...], band, NT).astype(BF16).astype(F32)
        query_hot = query_hot_ref[...]
        flat = query_hot.shape[1]
        slot = (iota((flat, KEYS), 0) % BAND_PAD).astype(F32)
        mixed = []
        for w in range(windows):
            start = w * QUERY_WINDOW
            key_hot = (slot == key_slots[w : w + 1]).astype(BF16)
            hot = query_hot[start : start + QUERY_WINDOW]
            hot_bias = jnp.concatenate([hot * bias_rows[h : h + 1] for h in range(heads)], axis=0).astype(BF16)
            powers = jnp.exp(products[w] + matmul(hot_bias, key_hot))
            blend = matmul(powers.astype(BF16), values_ext[start : start + KEYS].astype(BF16))
            blend = blend / jnp.sum(powers, axis=1, keepdims=True)
            total = jnp.zeros((QUERY_WINDOW, wide), F32)
            for h in range(heads):
                total = jnp.where(head_of == h, blend[h * QUERY_WINDOW : (h + 1) * QUERY_WINDOW], total)
            mixed.append(total)
        attended = jnp.concatenate(mixed, axis=0).astype(BF16)
        mixture = matmul(attended, attn_wide_ref[...])
        middle = act_ref[...].astype(F32) + mixture[:, :wide]
        shift = mixture[:, wide : 2 * wide] + mixture[:, 2 * wide : 3 * wide] + mixture[:, 3 * wide :]
        centred = middle - (act_mean_ref[...] + shift)
        spread = jnp.mean(centred * centred, axis=1, keepdims=True)
        expanded = matmul((centred * lax.rsqrt(spread + EPSILON)).astype(BF16), ffn_in_ref[...])
        hidden = ffn_out_ref.shape[0]
        inner = (jax.nn.silu(expanded[:, :hidden]) * expanded[:, hidden:]).astype(BF16)
        final = ((middle + matmul(inner, ffn_out_ref[...])) * live_ref[...]).astype(BF16)
        atom_new[...] = final
        atom_copy.start()
        features = jnp.maximum(matmul(final, agg_ref[...]), 0.0).astype(BF16).astype(F32)
        for b in range(features.shape[1] // LANES):
            block = features[:, b * LANES : (b + 1) * LANES]
            totals = [jnp.sum(block * member_ref[t], axis=0, keepdims=True) for t in range(rows)]
            token_new[:, b * LANES : (b + 1) * LANES] = (
                jnp.concatenate(totals, axis=0) / counts_ref[:rows]
            ).astype(BF16)
        token_copy.start()

    pair_copy.wait()
    atom_copy.wait()
    token_copy.wait()


def in_vmem(count):
    return [pl.BlockSpec(memory_space=pltpu.VMEM)] * count


def in_hbm(arrays):
    return [pltpu.with_memory_space_constraint(a, pltpu.HBM) for a in arrays]


def cost(flops, nbytes, exps=0):
    return pl.CostEstimate(flops=flops, bytes_accessed=nbytes, transcendentals=exps)


def exchange(blocks, n_row):
    grouped = blocks.reshape(n_row, -1, RIM_ROWS, LANES)
    return lax.all_to_all(grouped, "row", split_axis=0, concat_axis=0, tiled=True).reshape(blocks.shape)


def by_kernels(
    pair, token_mask, tri_in_weight, tri_gate_weight, tri_out_weight, atom_act, atom_cond, atom_token, atom_mask,
    ada_weight, qkv_weight, bias_weight, attn_out_weight, ffn_in_weight, ffn_out_weight, agg_weight,
):
    n_row = lax.axis_size("row")
    rows, cols, channels = pair.shape
    slab, wide = atom_act.shape
    width = rows * cols
    part = channels // n_row
    mask = token_mask.reshape(1, -1)
    token = atom_token.reshape(1, -1)
    alive = atom_mask.reshape(1, -1)
    sent = n_row * (2 * part * rows + RIM_ROWS)
    back_rows = n_row * (part * rows + RIM_ROWS)
    sources = (pair, atom_act, bias_weight.T, tri_in_weight, atom_cond, ada_weight, mask, token, alive)
    kept = 3
    pair, atom_act, bias_rows, terms, inputs, slots = pl.pallas_call(
        functools.partial(send_kernel, n_row),
        out_shape=(
            *(jax.ShapeDtypeStruct(a.shape, a.dtype) for a in sources[:kept]),
            jax.ShapeDtypeStruct((sent, LANES), BF16),
            jax.ShapeDtypeStruct((slab, wide), BF16),
            jax.ShapeDtypeStruct((SUBLANES, LANES), F32),
        ),
        in_specs=[pl.BlockSpec(memory_space=pltpu.HBM)] * len(sources),
        out_specs=tuple(in_vmem(kept + 3)),
        scratch_shapes=[
            *(pltpu.VMEM(a.shape, a.dtype) for a in sources[kept:]),
            pltpu.VMEM((sent, LANES), F32),
            pltpu.SemaphoreType.DMA((len(sources),)),
        ],
        cost_estimate=cost(8 * width * channels * channels, 1 << 20, 2 * width * channels),
        compiler_params=LIMIT,
        name="send",
    )(*in_hbm(sources))
    got = exchange(terms, n_row)
    sums, *prepared = pl.pallas_call(
        functools.partial(triangle_kernel, n_row, rows),
        out_shape=(
            jax.ShapeDtypeStruct((back_rows, LANES), BF16),
            jax.ShapeDtypeStruct((width, channels), F32),
            jax.ShapeDtypeStruct((slab, 3 * wide), BF16),
            jax.ShapeDtypeStruct((slab, rows * BAND_PAD), F32),
            jax.ShapeDtypeStruct((slab, wide), F32),
            jax.ShapeDtypeStruct((rows, slab, LANES), F32),
            jax.ShapeDtypeStruct((SUBLANES, LANES), F32),
            jax.ShapeDtypeStruct((slab, wide), F32),
            jax.ShapeDtypeStruct((wide, 4 * wide), BF16),
        ),
        in_specs=in_vmem(8),
        out_specs=tuple(in_vmem(9)),
        scratch_shapes=[
            pltpu.VMEM((sent, LANES), F32),
            pltpu.VMEM((part, cols, cols), F32),
            pltpu.VMEM((back_rows, LANES), F32),
        ],
        cost_estimate=cost(2 * width * width, 1 << 19),
        compiler_params=LIMIT,
        name="triangle",
    )(got, pair, tri_gate_weight, inputs, qkv_weight, slots, atom_act, attn_out_weight)
    back = exchange(sums, n_row)
    token_shape = (rows, agg_weight.shape[1])
    return pl.pallas_call(
        functools.partial(finish_kernel, n_row),
        out_shape=(
            jax.ShapeDtypeStruct(pair.shape, BF16),
            jax.ShapeDtypeStruct(atom_act.shape, BF16),
            jax.ShapeDtypeStruct(token_shape, BF16),
        ),
        in_specs=in_vmem(18),
        out_specs=(pl.BlockSpec(memory_space=pltpu.HBM),) * 3,
        scratch_shapes=[
            pltpu.VMEM((back_rows, LANES), F32),
            pltpu.VMEM(pair.shape, BF16),
            pltpu.VMEM(atom_act.shape, BF16),
            pltpu.VMEM(token_shape, BF16),
            pltpu.VMEM((rows, SUBLANES + cols + BAND_PAD, channels), F32),
            pltpu.VMEM((slab // QUERY_WINDOW, bias_weight.shape[1] * QUERY_WINDOW, KEYS), F32),
            pltpu.VMEM((slab + 2 * SIDE, wide), F32),
            pltpu.VMEM((SUBLANES, LANES), F32),
            pltpu.SemaphoreType.DMA((3,)),
        ],
        cost_estimate=cost(4 * width * channels * channels, 1 << 20),
        compiler_params=LIMIT,
        name="finish",
    )(
        back, pair, tri_out_weight, atom_act, slots, bias_rows, *prepared, qkv_weight, ffn_in_weight,
        ffn_out_weight, agg_weight,
    )


def kernels_fit(mesh, args):
    pair, atom_act, bias_weight = args[0], args[5], args[11]
    n_row = mesh.shape["row"]
    parts = mesh.shape["groups"] * n_row
    cols, channels = pair.shape[1:]
    rows = pair.shape[0] // parts
    slab = atom_act.shape[0] // parts
    wide = atom_act.shape[1]
    return (
        mesh.shape["col"] == 1
        and cols == channels == wide == LANES
        and cols == n_row * rows
        and channels % n_row == 0
        and n_row % SUBLANES == 0
        and SIDE < RIM_ROWS // 2 * n_row
        and 3 * rows <= BAND_PAD
        and rows <= SUBLANES
        and slab // QUERY_WINDOW <= SUBLANES
        and SIDE <= slab <= LANES
        and slab % QUERY_WINDOW == 0
        and slab - QUERY_WINDOW <= SIDE
        and wide % bias_weight.shape[1] == 0
    )


def solution(mesh):
    in_specs = (
        P(("groups", "row"), "col", None),
        P("groups"),
        P(),
        P(),
        P(),
        P(("groups", "row"), None),
        P(("groups", "row"), None),
        P(("groups", "row")),
        P(("groups", "row")),
        P(),
        P(),
        P(),
        P(),
        P(),
        P(),
        P(),
    )
    out_specs = (
        P(("groups", "row"), "col", None),
        P(("groups", "row"), None),
        P(("groups", "row"), None),
    )

    def layer(*args):
        body = by_kernels if kernels_fit(mesh, args) else per_device
        return jax.shard_map(body, mesh=mesh, in_specs=in_specs, out_specs=out_specs, check_vma=False)(*args)

    return layer
```

```python
import functools
import math

import jax
import jax.numpy as jnp
from jax import lax
from jax.experimental import pallas as pl
from jax.experimental.pallas import tpu as pltpu
from jax.sharding import PartitionSpec as P

QUERY_WINDOW = 32
KEYS = 128


EPSILON = 1e-05


def extended(shard, sides, width):
    for axis, dim in sides:
        size, length = (lax.axis_size(axis), shard.shape[dim])
        up = [(i, (i + 1) % size) for i in range(size - 1)]
        down = [(j, i) for i, j in up]
        last = lax.slice_in_dim(shard, length - width, length, axis=dim)
        first = lax.slice_in_dim(shard, 0, width, axis=dim)
        before = lax.ppermute(last, axis, up)
        after = lax.ppermute(first, axis, down)
        shard = jnp.concatenate([before, shard, after], axis=dim)
    return shard


def layer_norm(values, along):
    average = jnp.mean(values, axis=along, keepdims=True)
    centred = values - average
    spread = jnp.mean(centred * centred, axis=along, keepdims=True)
    return centred / jnp.sqrt(spread + EPSILON)


def per_device(
    pair,
    token_mask,
    tri_in_weight,
    tri_gate_weight,
    tri_out_weight,
    atom_act,
    atom_cond,
    atom_token,
    atom_mask,
    ada_weight,
    qkv_weight,
    bias_weight,
    attn_out_weight,
    ffn_in_weight,
    ffn_out_weight,
    agg_weight,
):
    tok_rows = pair.shape[0]
    col_count = pair.shape[1]
    channels = pair.shape[2]
    row_index = lax.axis_index("row")
    col_index = lax.axis_index("col")
    pair_float = pair.astype(jnp.float32)
    pair_norm = layer_norm(pair_float, 2).astype(jnp.bfloat16)
    row_live = lax.dynamic_slice_in_dim(token_mask, row_index * tok_rows, tok_rows, 0).astype(
        jnp.float32
    )
    col_live = lax.dynamic_slice_in_dim(token_mask, col_index * col_count, col_count, 0).astype(
        jnp.float32
    )
    pair_live = row_live[:, None] * col_live[None, :]
    left_terms = jnp.einsum(
        "ijd,de->eij",
        pair_norm,
        tri_in_weight[:, : 2 * channels],
        preferred_element_type=jnp.float32,
    )
    left = (jax.nn.sigmoid(left_terms[channels:]) * left_terms[:channels] * pair_live).astype(
        jnp.bfloat16
    )
    right_terms = jnp.einsum(
        "ijd,de->eij",
        pair_norm,
        tri_in_weight[:, 2 * channels :],
        preferred_element_type=jnp.float32,
    )
    right = (jax.nn.sigmoid(right_terms[channels:]) * right_terms[:channels] * pair_live).astype(
        jnp.bfloat16
    )
    tri_gate = jax.nn.sigmoid(
        jnp.einsum("ijd,de->ije", pair_norm, tri_gate_weight, preferred_element_type=jnp.float32)
    )
    left_owned, right_owned = (
        lax.all_to_all(left, "row", split_axis=0, concat_axis=1, tiled=True),
        lax.all_to_all(right, "row", split_axis=0, concat_axis=1, tiled=True),
    )
    left_full, right_rows = (
        lax.all_gather(left_owned, "col", axis=2, tiled=True),
        lax.all_gather(right_owned, "col", axis=2, tiled=True),
    )
    right_used = lax.dynamic_slice_in_dim(right_rows, col_index * col_count, col_count, 1)
    tri_sum = jnp.einsum(
        "cik,cjk->cij", left_full, right_used, preferred_element_type=jnp.float32
    ).astype(jnp.bfloat16)
    merged = lax.all_to_all(tri_sum, "row", split_axis=1, concat_axis=0, tiled=True)
    tri_norm = layer_norm(merged.astype(jnp.float32), 0).astype(jnp.bfloat16)
    update = jnp.einsum("dij,de->ije", tri_norm, tri_out_weight, preferred_element_type=jnp.float32)
    pair_out = (pair_float + tri_gate * update).astype(jnp.bfloat16)
    band_width = 3 * tok_rows
    targets = (row_index - 1) * tok_rows + jnp.arange(band_width, dtype=jnp.int32)
    columns = col_index * col_count + jnp.arange(col_count, dtype=jnp.int32)
    selector = (columns[:, None] == targets[None, :]).astype(jnp.bfloat16)
    band_part = jnp.einsum("ijd,jb->ibd", pair_out, selector, preferred_element_type=jnp.float32)
    band = lax.psum(band_part.astype(jnp.bfloat16), "col").astype(jnp.float32)
    band_norm = layer_norm(band, 2).astype(jnp.bfloat16)
    bias_table = jnp.einsum(
        "ibd,dh->ibh", band_norm, bias_weight, preferred_element_type=jnp.float32
    ).astype(jnp.bfloat16)
    slab = atom_act.shape[0]
    window_width = atom_act.shape[1]
    heads = bias_weight.shape[1]
    head_size = window_width // heads
    side = (KEYS - QUERY_WINDOW) // 2
    windows = slab // QUERY_WINDOW
    local_token = atom_token - row_index * tok_rows
    live = atom_mask.astype(jnp.float32)
    token_tag = ((local_token + 1) * atom_mask).astype(jnp.bfloat16)
    ada = jnp.dot(atom_cond, ada_weight, preferred_element_type=jnp.float32)
    atom_inputs = (
        jax.nn.sigmoid(ada[:, :window_width]) * layer_norm(atom_act.astype(jnp.float32), 1)
        + ada[:, window_width:]
    ).astype(jnp.bfloat16)
    projected = jnp.dot(atom_inputs, qkv_weight, preferred_element_type=jnp.float32).astype(
        jnp.bfloat16
    )
    queries = projected[:, :window_width]
    ext_pairs, ext_tag = (
        extended(projected[:, window_width:], (("row", 0),), side),
        extended(token_tag, (("row", 0),), side),
    )
    ext_rows = slab + 2 * side
    ext_position = jnp.arange(ext_rows, dtype=jnp.int32)
    offset = jnp.where(
        ext_position < side, 0, jnp.where(ext_position < side + slab, tok_rows, 2 * tok_rows)
    )
    tag_value = ext_tag.astype(jnp.int32)
    key_valid = tag_value > 0
    band_index = tag_value - 1 + offset
    band_slots = jnp.arange(band_width, dtype=jnp.int32)
    key_onehot = ((band_index[:, None] == band_slots[None, :]) & key_valid[:, None]).astype(
        jnp.bfloat16
    )
    query_onehot = (local_token[:, None] == jnp.arange(tok_rows, dtype=jnp.int32)[None, :]).astype(
        jnp.bfloat16
    )
    query_bias = jnp.einsum(
        "lt,tbh->lbh", query_onehot, bias_table, preferred_element_type=jnp.float32
    ).astype(jnp.bfloat16)
    query_bias = query_bias.reshape(windows, QUERY_WINDOW, band_width, heads)
    key_index = (
        jnp.arange(windows, dtype=jnp.int32)[:, None] * QUERY_WINDOW
        + jnp.arange(KEYS, dtype=jnp.int32)[None, :]
    )
    window_pairs = ext_pairs[key_index]
    window_onehot = key_onehot[key_index]
    window_valid = key_valid[key_index]
    window_bias = jnp.einsum(
        "wlbh,wmb->whlm", query_bias, window_onehot, preferred_element_type=jnp.float32
    )
    query_heads = queries.reshape(windows, QUERY_WINDOW, heads, head_size)
    key_heads = window_pairs[..., :window_width].reshape(windows, KEYS, heads, head_size)
    value_heads = window_pairs[..., window_width:].reshape(windows, KEYS, heads, head_size)
    logit_scores = (
        jnp.einsum("wlhd,wmhd->whlm", query_heads, key_heads, preferred_element_type=jnp.float32)
        / math.sqrt(head_size)
        + window_bias
    )
    logit_scores = jnp.where(window_valid[:, None, None, :], logit_scores, -1e30)
    attn_weights = jax.nn.softmax(logit_scores, axis=-1).astype(jnp.bfloat16)
    attended = (
        jnp.einsum("whlm,wmhd->wlhd", attn_weights, value_heads, preferred_element_type=jnp.float32)
        .reshape(slab, window_width)
        .astype(jnp.bfloat16)
    )
    atom_mid = atom_act.astype(jnp.float32) + jnp.dot(
        attended, attn_out_weight, preferred_element_type=jnp.float32
    )
    atom_norm = layer_norm(atom_mid, 1).astype(jnp.bfloat16)
    expanded = jnp.dot(atom_norm, ffn_in_weight, preferred_element_type=jnp.float32)
    hidden_width = ffn_out_weight.shape[0]
    inner = (jax.nn.silu(expanded[:, :hidden_width]) * expanded[:, hidden_width:]).astype(
        jnp.bfloat16
    )
    atom_out = (
        (atom_mid + jnp.dot(inner, ffn_out_weight, preferred_element_type=jnp.float32))
        * live[:, None]
    ).astype(jnp.bfloat16)
    features = jax.nn.relu(
        jnp.dot(atom_out, agg_weight, preferred_element_type=jnp.float32)
    ).astype(jnp.bfloat16)
    live_onehot = query_onehot * atom_mask.astype(jnp.bfloat16)[:, None]
    token_sums = jnp.einsum("at,ac->tc", live_onehot, features, preferred_element_type=jnp.float32)
    token_counts = jnp.sum(live_onehot.astype(jnp.float32), axis=0)
    token_out = (token_sums / token_counts[:, None]).astype(jnp.bfloat16)
    return (pair_out, atom_out, token_out)


LANES = 128
SUBLANES = 8
SIDE = (KEYS - QUERY_WINDOW) // 2
RIM_ROWS = 4
BAND_PAD = 2 * SUBLANES
LIMIT = pltpu.CompilerParams(vmem_limit_bytes=8 << 20)
F32 = jnp.float32
BF16 = jnp.bfloat16
NT = (((1,), (1,)), ((), ()))
TN = (((0,), (0,)), ((), ()))
TT = (((0,), (1,)), ((), ()))


def matmul(a, b, dims=(((1,), (0,)), ((), ()))):
    return lax.dot_general(a, b, dims, preferred_element_type=F32)


def normalize(values, axis):
    average = jnp.mean(values, axis=axis, keepdims=True)
    centred = values - average
    spread = jnp.mean(centred * centred, axis=axis, keepdims=True)
    return centred * lax.rsqrt(spread + EPSILON)


def iota(shape, dim):
    return lax.broadcasted_iota(jnp.int32, shape, dim)


def column_of(row, size):
    eye = iota((size, size), 0) == iota((size, size), 1)
    return jnp.sum(jnp.where(eye, row, 0.0), axis=1, keepdims=True)


def pad_lanes(row):
    return jnp.concatenate([row, jnp.zeros((row.shape[0], LANES - row.shape[1]), row.dtype)], axis=1)


def strided(first, count, step):
    return pl.ds(first, count, stride=step)


def send_kernel(
    n_row, pair_hbm, act_hbm, bias_w_hbm, in_w_hbm, cond_hbm, ada_w_hbm, mask_hbm, token_hbm, alive_hbm,
    pair_ref, act_ref, bias_w_ref, out_ref, normed_ref, inputs_ref, slots_ref,
    in_w_ref, cond_ref, ada_w_ref, mask_ref, token_ref, alive_ref, staged, sems,
):
    sources = (pair_hbm, cond_hbm, act_hbm, mask_hbm, token_hbm, alive_hbm, bias_w_hbm, ada_w_hbm, in_w_hbm)
    places = (pair_ref, cond_ref, act_ref, mask_ref, token_ref, alive_ref, bias_w_ref, ada_w_ref, in_w_ref)
    loads = [pltpu.make_async_copy(a, b, sems.at[i]) for i, (a, b) in enumerate(zip(sources, places))]
    for load in loads:
        load.start()
    loads[0].wait()
    me = lax.axis_index("row")
    rows, cols, channels = pair_ref.shape
    part = channels // n_row
    width = rows * cols
    step = 2 * part * rows + RIM_ROWS
    normed = normalize(pair_ref[...].reshape(width, channels).astype(F32), 1).astype(BF16)
    normed_ref[...] = normed
    for load in loads[1:]:
        load.wait()
    live = mask_ref[...].astype(F32)
    lane = iota(live.shape, 1)
    both = jnp.concatenate(
        [live * jnp.sum(jnp.where(lane == me * rows + i, live, 0.0), axis=1, keepdims=True) for i in range(rows)],
        axis=1,
    )
    for side in range(2):
        first = 2 * side * channels
        value = matmul(in_w_ref[:, first : first + channels], normed, TT)
        gate = matmul(in_w_ref[:, first + channels : first + 2 * channels], normed, TT)
        term = jax.nn.sigmoid(gate) * value * both
        for q in range(part):
            for i in range(rows):
                staged[strided((side * part + q) * rows + i, n_row, step)] = term[
                    q * n_row : (q + 1) * n_row, i * cols : (i + 1) * cols
                ]
    act = act_ref[...].astype(F32)
    ada = matmul(cond_ref[...], ada_w_ref[...])
    slab, wide = act.shape
    inputs = (jax.nn.sigmoid(ada[:, :wide]) * normalize(act, 1) + ada[:, wide:]).astype(BF16)
    inputs_ref[...] = inputs
    inputs = inputs.astype(F32)
    token = token_ref[...] - me * rows
    alive = alive_ref[...]
    tag = pad_lanes(((token + 1) * alive).astype(F32))
    slots_ref[...] = jnp.zeros(slots_ref.shape, F32)
    slots_ref[0:1] = pad_lanes(token.astype(F32))
    slots_ref[1:2] = pad_lanes(alive.astype(F32))
    slots_ref[2:3] = tag
    tags = jnp.broadcast_to(tag, (2 * n_row - SIDE, LANES))
    for d, rim in enumerate((inputs[slab - SIDE :], inputs[:SIDE])):
        block = jnp.concatenate([rim, tags], axis=0)
        for s in range(RIM_ROWS // 2):
            staged[strided(step - RIM_ROWS + d * (RIM_ROWS // 2) + s, n_row, step)] = block[
                s * n_row : (s + 1) * n_row
            ]
    out_ref[...] = staged[...].astype(BF16)


def prepare(
    inputs_ref, qkv_w_ref, slots_ref, act_ref, attn_w_ref,
    qkv_ref, query_hot_ref, live_ref, member_ref, counts_ref, act_mean_ref, attn_wide_ref,
):
    rows = member_ref.shape[0]
    slab = inputs_ref.shape[0]
    token = slots_ref[0:1, :slab]
    alive = slots_ref[1:2, :slab]
    qkv_ref[...] = matmul(inputs_ref[...], qkv_w_ref[...]).astype(BF16)
    token_col = column_of(token, slab)
    query_hot_ref[...] = (token_col == (iota(query_hot_ref.shape, 1) // BAND_PAD).astype(F32)).astype(F32)
    live_ref[...] = jnp.broadcast_to(column_of(alive, slab), live_ref.shape)
    live_col = column_of(alive, slab)
    for t in range(rows):
        member_ref[t] = jnp.broadcast_to(jnp.where(token_col == t, live_col, 0.0), member_ref.shape[1:])
    counts = jnp.sum(jnp.where(iota((SUBLANES, slab), 0).astype(F32) == token, alive, 0.0), axis=1, keepdims=True)
    counts_ref[...] = jnp.broadcast_to(jnp.maximum(counts, 1.0), counts_ref.shape)
    act_mean_ref[...] = jnp.broadcast_to(jnp.mean(act_ref[...].astype(F32), axis=1, keepdims=True), act_mean_ref.shape)
    wide = attn_w_ref.shape[1]
    attn_wide_ref[:, :wide] = attn_w_ref[...]
    rest = jnp.broadcast_to(jnp.mean(attn_w_ref[...].astype(F32), axis=1, keepdims=True), attn_w_ref.shape)
    for k in range(1, 4):
        piece = rest.astype(BF16)
        attn_wide_ref[:, k * wide : (k + 1) * wide] = piece
        rest = rest - piece.astype(F32)


def triangle_kernel(n_row, rows, got_ref, normed_ref, gate_w_ref, out_ref, gate_ref, taken, right_terms, staged):
    gate_ref[...] = jax.nn.sigmoid(matmul(normed_ref[...], gate_w_ref[...]))
    taken[...] = got_ref[...].astype(F32)
    step = got_ref.shape[0] // n_row
    part = right_terms.shape[0]
    out_step = part * rows + RIM_ROWS
    for q in range(part):
        left = jnp.concatenate(
            [taken[strided(q * rows + i, n_row, step)] for i in range(rows)], axis=0
        ).astype(BF16)
        for j in range(rows):
            right_terms[q, strided(j, n_row, rows)] = taken[strided((part + q) * rows + j, n_row, step)]
        summed = matmul(left, right_terms[q].astype(BF16), NT)
        for i in range(rows):
            staged[strided(q * rows + i, n_row, out_step)] = summed[i * n_row : (i + 1) * n_row]
    nothing = jnp.zeros((1, LANES), F32)
    for s in range(RIM_ROWS):
        rim = taken[strided(step - RIM_ROWS + s, n_row, step)]
        if s < RIM_ROWS // 2:
            rim = jnp.concatenate([nothing, rim[:-1]], axis=0)
        else:
            rim = jnp.concatenate([rim[1:], nothing], axis=0)
        staged[strided(out_step - RIM_ROWS + s, n_row, out_step)] = rim
    out_ref[...] = staged[...].astype(BF16)


def finish_kernel(
    n_row, got_ref, pair_ref, out_w_ref, act_ref, slots_ref, bias_w_ref, gate_ref, inputs_ref, qkv_w_ref, attn_w_ref,
    ffn_in_ref, ffn_out_ref, agg_ref,
    pair_out, atom_out, token_out, taken, pair_new, atom_new, token_new, padded, products, values_ext, key_slots,
    qkv_ref, query_hot_ref, live_ref, member_ref, counts_ref, act_mean_ref, attn_wide_ref, sems,
):
    me = lax.axis_index("row")
    rows, cols, channels = pair_ref.shape
    part = channels // n_row
    step = part * rows + RIM_ROWS
    half = RIM_ROWS // 2
    slab, wide = act_ref.shape
    heads = bias_w_ref.shape[0]
    head_size = wide // heads
    head_of = iota((QUERY_WINDOW, wide), 1) // head_size
    windows = slab // QUERY_WINDOW
    taken[...] = got_ref[...].astype(F32)
    prepare(
        inputs_ref, qkv_w_ref, slots_ref, act_ref, attn_w_ref,
        qkv_ref, query_hot_ref, live_ref, member_ref, counts_ref, act_mean_ref, attn_wide_ref,
    )
    sums = [
        jnp.concatenate([taken[strided(q * rows + i, n_row, step)] for q in range(part)], axis=0) for i in range(rows)
    ]
    outer = jnp.concatenate(
        [
            taken[strided(step - RIM_ROWS + d * half + s, n_row, step)][: min(n_row, SIDE - s * n_row)]
            for d in range(2)
            for s in range(half)
        ],
        axis=0,
    ).astype(BF16)
    outer = matmul(outer, qkv_w_ref[:, wide:]).astype(BF16).astype(F32)
    own = qkv_ref[...].astype(F32)
    keys_ext, values = (
        jnp.concatenate(
            [outer[:SIDE, at : at + wide], own[:, wide + at : 2 * wide + at], outer[SIDE:, at : at + wide]], axis=0
        )
        for at in (0, wide)
    )
    values_ext[...] = values
    tag_at = [(step - RIM_ROWS + d * half + SIDE // n_row) + step * (SIDE % n_row) for d in range(2)]
    before_tag, after_tag = (taken[at : at + 1] for at in tag_at)
    own_tag = slots_ref[2:3]
    lane = iota((1, LANES), 1)
    for w in range(windows):
        start = w * QUERY_WINDOW
        query = own[start : start + QUERY_WINDOW, :wide]
        split = jnp.concatenate([jnp.where(head_of == h, query, 0.0) for h in range(heads)], axis=0).astype(BF16)
        before_end = SIDE - start
        own_end = before_end + slab
        is_before, is_own = lane < before_end, lane < own_end
        tag = jnp.where(
            is_before,
            pltpu.roll(before_tag, (SIDE - slab - start) % LANES, 1),
            jnp.where(
                is_own, pltpu.roll(own_tag, before_end % LANES, 1), pltpu.roll(after_tag, own_end % LANES, 1)
            ),
        )
        offset = jnp.where(is_before, 0.0, jnp.where(is_own, 1.0 * rows, 2.0 * rows))
        valid = tag > 0
        key_slot = jnp.where(valid, tag - 1 + offset, -1.0)
        key_slots[w : w + 1] = key_slot
        product = matmul(split, keys_ext[start : start + KEYS].astype(BF16), NT) * (1 / math.sqrt(head_size))
        product = jnp.where(valid, product, -1e30)
        products[w] = product - jnp.max(product, axis=1, keepdims=True)
    for i in range(rows):
        update = matmul(normalize(sums[i], 0).astype(BF16), out_w_ref[...], TN)
        fresh = (pair_ref[i].astype(F32) + gate_ref[i * cols : (i + 1) * cols] * update).astype(BF16)
        pair_new[i] = fresh
        padded[i, :SUBLANES] = jnp.zeros((SUBLANES, channels), F32)
        padded[i, SUBLANES : SUBLANES + cols] = fresh.astype(F32)
        padded[i, SUBLANES + cols :] = jnp.zeros((BAND_PAD, channels), F32)
    pair_copy = pltpu.make_async_copy(pair_new, pair_out, sems.at[0])
    atom_copy = pltpu.make_async_copy(atom_new, atom_out, sems.at[1])
    token_copy = pltpu.make_async_copy(token_new, token_out, sems.at[2])
    pair_copy.start()

    @pl.when(me >= 0)
    def _():
        band = [padded[i, pl.ds(SUBLANES + (me - 1) * rows, BAND_PAD)] for i in range(rows)]
        band = normalize(jnp.concatenate(band, axis=0), 1).astype(BF16)
        bias_rows = matmul(bias_w_ref[...], band, NT).astype(BF16).astype(F32)
        query_hot = query_hot_ref[...]
        flat = query_hot.shape[1]
        slot = (iota((flat, KEYS), 0) % BAND_PAD).astype(F32)
        mixed = []
        for w in range(windows):
            start = w * QUERY_WINDOW
            key_hot = (slot == key_slots[w : w + 1]).astype(BF16)
            hot = query_hot[start : start + QUERY_WINDOW]
            hot_bias = jnp.concatenate([hot * bias_rows[h : h + 1] for h in range(heads)], axis=0).astype(BF16)
            powers = jnp.exp(products[w] + matmul(hot_bias, key_hot))
            blend = matmul(powers.astype(BF16), values_ext[start : start + KEYS].astype(BF16))
            blend = blend / jnp.sum(powers, axis=1, keepdims=True)
            total = jnp.zeros((QUERY_WINDOW, wide), F32)
            for h in range(heads):
                total = jnp.where(head_of == h, blend[h * QUERY_WINDOW : (h + 1) * QUERY_WINDOW], total)
            mixed.append(total)
        attended = jnp.concatenate(mixed, axis=0).astype(BF16)
        mixture = matmul(attended, attn_wide_ref[...])
        middle = act_ref[...].astype(F32) + mixture[:, :wide]
        shift = mixture[:, wide : 2 * wide] + mixture[:, 2 * wide : 3 * wide] + mixture[:, 3 * wide :]
        centred = middle - (act_mean_ref[...] + shift)
        spread = jnp.mean(centred * centred, axis=1, keepdims=True)
        expanded = matmul((centred * lax.rsqrt(spread + EPSILON)).astype(BF16), ffn_in_ref[...])
        hidden = ffn_out_ref.shape[0]
        inner = (jax.nn.silu(expanded[:, :hidden]) * expanded[:, hidden:]).astype(BF16)
        final = ((middle + matmul(inner, ffn_out_ref[...])) * live_ref[...]).astype(BF16)
        atom_new[...] = final
        atom_copy.start()
        features = jnp.maximum(matmul(final, agg_ref[...]), 0.0).astype(BF16).astype(F32)
        for b in range(features.shape[1] // LANES):
            block = features[:, b * LANES : (b + 1) * LANES]
            totals = [jnp.sum(block * member_ref[t], axis=0, keepdims=True) for t in range(rows)]
            token_new[:, b * LANES : (b + 1) * LANES] = (
                jnp.concatenate(totals, axis=0) / counts_ref[:rows]
            ).astype(BF16)
        token_copy.start()

    pair_copy.wait()
    atom_copy.wait()
    token_copy.wait()


def in_vmem(count):
    return [pl.BlockSpec(memory_space=pltpu.VMEM)] * count


def in_hbm(arrays):
    return [pltpu.with_memory_space_constraint(a, pltpu.HBM) for a in arrays]


def cost(flops, nbytes, exps=0):
    return pl.CostEstimate(flops=flops, bytes_accessed=nbytes, transcendentals=exps)


def exchange(blocks, n_row):
    grouped = blocks.reshape(n_row, -1, RIM_ROWS, LANES)
    return lax.all_to_all(grouped, "row", split_axis=0, concat_axis=0, tiled=True).reshape(blocks.shape)


def by_kernels(
    pair, token_mask, tri_in_weight, tri_gate_weight, tri_out_weight, atom_act, atom_cond, atom_token, atom_mask,
    ada_weight, qkv_weight, bias_weight, attn_out_weight, ffn_in_weight, ffn_out_weight, agg_weight,
):
    n_row = lax.axis_size("row")
    rows, cols, channels = pair.shape
    slab, wide = atom_act.shape
    width = rows * cols
    part = channels // n_row
    mask = token_mask.reshape(1, -1)
    token = atom_token.reshape(1, -1)
    alive = atom_mask.reshape(1, -1)
    sent = n_row * (2 * part * rows + RIM_ROWS)
    back_rows = n_row * (part * rows + RIM_ROWS)
    sources = (pair, atom_act, bias_weight.T, tri_in_weight, atom_cond, ada_weight, mask, token, alive)
    kept = 3
    pair, atom_act, bias_rows, terms, normed, inputs, slots = pl.pallas_call(
        functools.partial(send_kernel, n_row),
        out_shape=(
            *(jax.ShapeDtypeStruct(a.shape, a.dtype) for a in sources[:kept]),
            jax.ShapeDtypeStruct((sent, LANES), BF16),
            jax.ShapeDtypeStruct((width, channels), BF16),
            jax.ShapeDtypeStruct((slab, wide), BF16),
            jax.ShapeDtypeStruct((SUBLANES, LANES), F32),
        ),
        in_specs=[pl.BlockSpec(memory_space=pltpu.HBM)] * len(sources),
        out_specs=tuple(in_vmem(kept + 4)),
        scratch_shapes=[
            *(pltpu.VMEM(a.shape, a.dtype) for a in sources[kept:]),
            pltpu.VMEM((sent, LANES), F32),
            pltpu.SemaphoreType.DMA((len(sources),)),
        ],
        cost_estimate=cost(8 * width * channels * channels, 1 << 20, 2 * width * channels),
        compiler_params=LIMIT,
        name="send",
    )(*in_hbm(sources))
    got = exchange(terms, n_row)
    sums, gate = pl.pallas_call(
        functools.partial(triangle_kernel, n_row, rows),
        out_shape=(
            jax.ShapeDtypeStruct((back_rows, LANES), BF16),
            jax.ShapeDtypeStruct((width, channels), F32),
        ),
        in_specs=in_vmem(3),
        out_specs=tuple(in_vmem(2)),
        scratch_shapes=[
            pltpu.VMEM((sent, LANES), F32),
            pltpu.VMEM((part, cols, cols), F32),
            pltpu.VMEM((back_rows, LANES), F32),
        ],
        cost_estimate=cost(2 * width * width, 1 << 19),
        compiler_params=LIMIT,
        name="triangle",
    )(got, normed, tri_gate_weight)
    back = exchange(sums, n_row)
    token_shape = (rows, agg_weight.shape[1])
    return pl.pallas_call(
        functools.partial(finish_kernel, n_row),
        out_shape=(
            jax.ShapeDtypeStruct(pair.shape, BF16),
            jax.ShapeDtypeStruct(atom_act.shape, BF16),
            jax.ShapeDtypeStruct(token_shape, BF16),
        ),
        in_specs=in_vmem(13),
        out_specs=(pl.BlockSpec(memory_space=pltpu.HBM),) * 3,
        scratch_shapes=[
            pltpu.VMEM((back_rows, LANES), F32),
            pltpu.VMEM(pair.shape, BF16),
            pltpu.VMEM(atom_act.shape, BF16),
            pltpu.VMEM(token_shape, BF16),
            pltpu.VMEM((rows, SUBLANES + cols + BAND_PAD, channels), F32),
            pltpu.VMEM((slab // QUERY_WINDOW, bias_weight.shape[1] * QUERY_WINDOW, KEYS), F32),
            pltpu.VMEM((slab + 2 * SIDE, wide), F32),
            pltpu.VMEM((SUBLANES, LANES), F32),
            pltpu.VMEM((slab, 3 * wide), BF16),
            pltpu.VMEM((slab, rows * BAND_PAD), F32),
            pltpu.VMEM((slab, wide), F32),
            pltpu.VMEM((rows, slab, LANES), F32),
            pltpu.VMEM((SUBLANES, LANES), F32),
            pltpu.VMEM((slab, wide), F32),
            pltpu.VMEM((wide, 4 * wide), BF16),
            pltpu.SemaphoreType.DMA((3,)),
        ],
        cost_estimate=cost(4 * width * channels * channels, 1 << 20),
        compiler_params=LIMIT,
        name="finish",
    )(
        back, pair, tri_out_weight, atom_act, slots, bias_rows, gate, inputs, qkv_weight, attn_out_weight,
        ffn_in_weight, ffn_out_weight, agg_weight,
    )


def kernels_fit(mesh, args):
    pair, atom_act, bias_weight = args[0], args[5], args[11]
    n_row = mesh.shape["row"]
    parts = mesh.shape["groups"] * n_row
    cols, channels = pair.shape[1:]
    rows = pair.shape[0] // parts
    slab = atom_act.shape[0] // parts
    wide = atom_act.shape[1]
    return (
        mesh.shape["col"] == 1
        and cols == channels == wide == LANES
        and cols == n_row * rows
        and channels % n_row == 0
        and n_row % SUBLANES == 0
        and SIDE < RIM_ROWS // 2 * n_row
        and 3 * rows <= BAND_PAD
        and rows <= SUBLANES
        and slab // QUERY_WINDOW <= SUBLANES
        and SIDE <= slab <= LANES
        and slab % QUERY_WINDOW == 0
        and slab - QUERY_WINDOW <= SIDE
        and wide % bias_weight.shape[1] == 0
    )


def solution(mesh):
    in_specs = (
        P(("groups", "row"), "col", None),
        P("groups"),
        P(),
        P(),
        P(),
        P(("groups", "row"), None),
        P(("groups", "row"), None),
        P(("groups", "row")),
        P(("groups", "row")),
        P(),
        P(),
        P(),
        P(),
        P(),
        P(),
        P(),
    )
    out_specs = (
        P(("groups", "row"), "col", None),
        P(("groups", "row"), None),
        P(("groups", "row"), None),
    )

    def layer(*args):
        body = by_kernels if kernels_fit(mesh, args) else per_device
        return jax.shard_map(body, mesh=mesh, in_specs=in_specs, out_specs=out_specs, check_vma=False)(*args)

    return layer
```

```python
import functools
import math

import jax
import jax.numpy as jnp
from jax import lax
from jax.experimental import pallas as pl
from jax.experimental.pallas import tpu as pltpu
from jax.sharding import PartitionSpec as P

QUERY_WINDOW = 32
KEYS = 128


EPSILON = 1e-05


def extended(shard, sides, width):
    for axis, dim in sides:
        size, length = (lax.axis_size(axis), shard.shape[dim])
        up = [(i, (i + 1) % size) for i in range(size - 1)]
        down = [(j, i) for i, j in up]
        last = lax.slice_in_dim(shard, length - width, length, axis=dim)
        first = lax.slice_in_dim(shard, 0, width, axis=dim)
        before = lax.ppermute(last, axis, up)
        after = lax.ppermute(first, axis, down)
        shard = jnp.concatenate([before, shard, after], axis=dim)
    return shard


def layer_norm(values, along):
    average = jnp.mean(values, axis=along, keepdims=True)
    centred = values - average
    spread = jnp.mean(centred * centred, axis=along, keepdims=True)
    return centred / jnp.sqrt(spread + EPSILON)


def per_device(
    pair,
    token_mask,
    tri_in_weight,
    tri_gate_weight,
    tri_out_weight,
    atom_act,
    atom_cond,
    atom_token,
    atom_mask,
    ada_weight,
    qkv_weight,
    bias_weight,
    attn_out_weight,
    ffn_in_weight,
    ffn_out_weight,
    agg_weight,
):
    tok_rows = pair.shape[0]
    col_count = pair.shape[1]
    channels = pair.shape[2]
    row_index = lax.axis_index("row")
    col_index = lax.axis_index("col")
    pair_float = pair.astype(jnp.float32)
    pair_norm = layer_norm(pair_float, 2).astype(jnp.bfloat16)
    row_live = lax.dynamic_slice_in_dim(token_mask, row_index * tok_rows, tok_rows, 0).astype(
        jnp.float32
    )
    col_live = lax.dynamic_slice_in_dim(token_mask, col_index * col_count, col_count, 0).astype(
        jnp.float32
    )
    pair_live = row_live[:, None] * col_live[None, :]
    left_terms = jnp.einsum(
        "ijd,de->eij",
        pair_norm,
        tri_in_weight[:, : 2 * channels],
        preferred_element_type=jnp.float32,
    )
    left = (jax.nn.sigmoid(left_terms[channels:]) * left_terms[:channels] * pair_live).astype(
        jnp.bfloat16
    )
    right_terms = jnp.einsum(
        "ijd,de->eij",
        pair_norm,
        tri_in_weight[:, 2 * channels :],
        preferred_element_type=jnp.float32,
    )
    right = (jax.nn.sigmoid(right_terms[channels:]) * right_terms[:channels] * pair_live).astype(
        jnp.bfloat16
    )
    tri_gate = jax.nn.sigmoid(
        jnp.einsum("ijd,de->ije", pair_norm, tri_gate_weight, preferred_element_type=jnp.float32)
    )
    left_owned, right_owned = (
        lax.all_to_all(left, "row", split_axis=0, concat_axis=1, tiled=True),
        lax.all_to_all(right, "row", split_axis=0, concat_axis=1, tiled=True),
    )
    left_full, right_rows = (
        lax.all_gather(left_owned, "col", axis=2, tiled=True),
        lax.all_gather(right_owned, "col", axis=2, tiled=True),
    )
    right_used = lax.dynamic_slice_in_dim(right_rows, col_index * col_count, col_count, 1)
    tri_sum = jnp.einsum(
        "cik,cjk->cij", left_full, right_used, preferred_element_type=jnp.float32
    ).astype(jnp.bfloat16)
    merged = lax.all_to_all(tri_sum, "row", split_axis=1, concat_axis=0, tiled=True)
    tri_norm = layer_norm(merged.astype(jnp.float32), 0).astype(jnp.bfloat16)
    update = jnp.einsum("dij,de->ije", tri_norm, tri_out_weight, preferred_element_type=jnp.float32)
    pair_out = (pair_float + tri_gate * update).astype(jnp.bfloat16)
    band_width = 3 * tok_rows
    targets = (row_index - 1) * tok_rows + jnp.arange(band_width, dtype=jnp.int32)
    columns = col_index * col_count + jnp.arange(col_count, dtype=jnp.int32)
    selector = (columns[:, None] == targets[None, :]).astype(jnp.bfloat16)
    band_part = jnp.einsum("ijd,jb->ibd", pair_out, selector, preferred_element_type=jnp.float32)
    band = lax.psum(band_part.astype(jnp.bfloat16), "col").astype(jnp.float32)
    band_norm = layer_norm(band, 2).astype(jnp.bfloat16)
    bias_table = jnp.einsum(
        "ibd,dh->ibh", band_norm, bias_weight, preferred_element_type=jnp.float32
    ).astype(jnp.bfloat16)
    slab = atom_act.shape[0]
    window_width = atom_act.shape[1]
    heads = bias_weight.shape[1]
    head_size = window_width // heads
    side = (KEYS - QUERY_WINDOW) // 2
    windows = slab // QUERY_WINDOW
    local_token = atom_token - row_index * tok_rows
    live = atom_mask.astype(jnp.float32)
    token_tag = ((local_token + 1) * atom_mask).astype(jnp.bfloat16)
    ada = jnp.dot(atom_cond, ada_weight, preferred_element_type=jnp.float32)
    atom_inputs = (
        jax.nn.sigmoid(ada[:, :window_width]) * layer_norm(atom_act.astype(jnp.float32), 1)
        + ada[:, window_width:]
    ).astype(jnp.bfloat16)
    projected = jnp.dot(atom_inputs, qkv_weight, preferred_element_type=jnp.float32).astype(
        jnp.bfloat16
    )
    queries = projected[:, :window_width]
    ext_pairs, ext_tag = (
        extended(projected[:, window_width:], (("row", 0),), side),
        extended(token_tag, (("row", 0),), side),
    )
    ext_rows = slab + 2 * side
    ext_position = jnp.arange(ext_rows, dtype=jnp.int32)
    offset = jnp.where(
        ext_position < side, 0, jnp.where(ext_position < side + slab, tok_rows, 2 * tok_rows)
    )
    tag_value = ext_tag.astype(jnp.int32)
    key_valid = tag_value > 0
    band_index = tag_value - 1 + offset
    band_slots = jnp.arange(band_width, dtype=jnp.int32)
    key_onehot = ((band_index[:, None] == band_slots[None, :]) & key_valid[:, None]).astype(
        jnp.bfloat16
    )
    query_onehot = (local_token[:, None] == jnp.arange(tok_rows, dtype=jnp.int32)[None, :]).astype(
        jnp.bfloat16
    )
    query_bias = jnp.einsum(
        "lt,tbh->lbh", query_onehot, bias_table, preferred_element_type=jnp.float32
    ).astype(jnp.bfloat16)
    query_bias = query_bias.reshape(windows, QUERY_WINDOW, band_width, heads)
    key_index = (
        jnp.arange(windows, dtype=jnp.int32)[:, None] * QUERY_WINDOW
        + jnp.arange(KEYS, dtype=jnp.int32)[None, :]
    )
    window_pairs = ext_pairs[key_index]
    window_onehot = key_onehot[key_index]
    window_valid = key_valid[key_index]
    window_bias = jnp.einsum(
        "wlbh,wmb->whlm", query_bias, window_onehot, preferred_element_type=jnp.float32
    )
    query_heads = queries.reshape(windows, QUERY_WINDOW, heads, head_size)
    key_heads = window_pairs[..., :window_width].reshape(windows, KEYS, heads, head_size)
    value_heads = window_pairs[..., window_width:].reshape(windows, KEYS, heads, head_size)
    logit_scores = (
        jnp.einsum("wlhd,wmhd->whlm", query_heads, key_heads, preferred_element_type=jnp.float32)
        / math.sqrt(head_size)
        + window_bias
    )
    logit_scores = jnp.where(window_valid[:, None, None, :], logit_scores, -1e30)
    attn_weights = jax.nn.softmax(logit_scores, axis=-1).astype(jnp.bfloat16)
    attended = (
        jnp.einsum("whlm,wmhd->wlhd", attn_weights, value_heads, preferred_element_type=jnp.float32)
        .reshape(slab, window_width)
        .astype(jnp.bfloat16)
    )
    atom_mid = atom_act.astype(jnp.float32) + jnp.dot(
        attended, attn_out_weight, preferred_element_type=jnp.float32
    )
    atom_norm = layer_norm(atom_mid, 1).astype(jnp.bfloat16)
    expanded = jnp.dot(atom_norm, ffn_in_weight, preferred_element_type=jnp.float32)
    hidden_width = ffn_out_weight.shape[0]
    inner = (jax.nn.silu(expanded[:, :hidden_width]) * expanded[:, hidden_width:]).astype(
        jnp.bfloat16
    )
    atom_out = (
        (atom_mid + jnp.dot(inner, ffn_out_weight, preferred_element_type=jnp.float32))
        * live[:, None]
    ).astype(jnp.bfloat16)
    features = jax.nn.relu(
        jnp.dot(atom_out, agg_weight, preferred_element_type=jnp.float32)
    ).astype(jnp.bfloat16)
    live_onehot = query_onehot * atom_mask.astype(jnp.bfloat16)[:, None]
    token_sums = jnp.einsum("at,ac->tc", live_onehot, features, preferred_element_type=jnp.float32)
    token_counts = jnp.sum(live_onehot.astype(jnp.float32), axis=0)
    token_out = (token_sums / token_counts[:, None]).astype(jnp.bfloat16)
    return (pair_out, atom_out, token_out)


LANES = 128
SUBLANES = 8
SIDE = (KEYS - QUERY_WINDOW) // 2
RIM_ROWS = 4
BAND_PAD = 2 * SUBLANES
LIMIT = pltpu.CompilerParams(vmem_limit_bytes=8 << 20)
F32 = jnp.float32
BF16 = jnp.bfloat16
NT = (((1,), (1,)), ((), ()))
TN = (((0,), (0,)), ((), ()))
TT = (((0,), (1,)), ((), ()))


def matmul(a, b, dims=(((1,), (0,)), ((), ()))):
    return lax.dot_general(a, b, dims, preferred_element_type=F32)


def normalize(values, axis):
    average = jnp.mean(values, axis=axis, keepdims=True)
    centred = values - average
    spread = jnp.mean(centred * centred, axis=axis, keepdims=True)
    return centred * lax.rsqrt(spread + EPSILON)


def iota(shape, dim):
    return lax.broadcasted_iota(jnp.int32, shape, dim)


def column_of(row, size):
    eye = iota((size, size), 0) == iota((size, size), 1)
    return jnp.sum(jnp.where(eye, row, 0.0), axis=1, keepdims=True)


def pad_lanes(row):
    return jnp.concatenate([row, jnp.zeros((row.shape[0], LANES - row.shape[1]), row.dtype)], axis=1)


def strided(first, count, step):
    return pl.ds(first, count, stride=step)


def send_kernel(
    n_row, pair_hbm, act_hbm, bias_w_hbm, in_w_hbm, cond_hbm, ada_w_hbm, mask_hbm, token_hbm, alive_hbm,
    pair_ref, act_ref, bias_w_ref, out_ref, normed_ref, inputs_ref, slots_ref,
    in_w_ref, cond_ref, ada_w_ref, mask_ref, token_ref, alive_ref, staged, sems,
):
    sources = (pair_hbm, cond_hbm, act_hbm, mask_hbm, token_hbm, alive_hbm, bias_w_hbm, ada_w_hbm, in_w_hbm)
    places = (pair_ref, cond_ref, act_ref, mask_ref, token_ref, alive_ref, bias_w_ref, ada_w_ref, in_w_ref)
    loads = [pltpu.make_async_copy(a, b, sems.at[i]) for i, (a, b) in enumerate(zip(sources, places))]
    for load in loads:
        load.start()
    loads[0].wait()
    me = lax.axis_index("row")
    rows, cols, channels = pair_ref.shape
    part = channels // n_row
    width = rows * cols
    step = 2 * part * rows + RIM_ROWS
    normed = normalize(pair_ref[...].reshape(width, channels).astype(F32), 1).astype(BF16)
    normed_ref[...] = normed
    for load in loads[1:]:
        load.wait()
    live = mask_ref[...].astype(F32)
    lane = iota(live.shape, 1)
    both = jnp.concatenate(
        [live * jnp.sum(jnp.where(lane == me * rows + i, live, 0.0), axis=1, keepdims=True) for i in range(rows)],
        axis=1,
    )
    for side in range(2):
        first = 2 * side * channels
        value = matmul(in_w_ref[:, first : first + channels], normed, TT)
        gate = matmul(in_w_ref[:, first + channels : first + 2 * channels], normed, TT)
        term = jax.nn.sigmoid(gate) * value * both
        for q in range(part):
            for i in range(rows):
                staged[strided((side * part + q) * rows + i, n_row, step)] = term[
                    q * n_row : (q + 1) * n_row, i * cols : (i + 1) * cols
                ]
    act = act_ref[...].astype(F32)
    ada = matmul(cond_ref[...], ada_w_ref[...])
    slab, wide = act.shape
    inputs = (jax.nn.sigmoid(ada[:, :wide]) * normalize(act, 1) + ada[:, wide:]).astype(BF16)
    inputs_ref[...] = inputs
    inputs = inputs.astype(F32)
    token = token_ref[...] - me * rows
    alive = alive_ref[...]
    tag = pad_lanes(((token + 1) * alive).astype(F32))
    slots_ref[...] = jnp.zeros(slots_ref.shape, F32)
    slots_ref[0:1] = pad_lanes(token.astype(F32))
    slots_ref[1:2] = pad_lanes(alive.astype(F32))
    slots_ref[2:3] = tag
    tags = jnp.broadcast_to(tag, (2 * n_row - SIDE, LANES))
    for d, rim in enumerate((inputs[slab - SIDE :], inputs[:SIDE])):
        block = jnp.concatenate([rim, tags], axis=0)
        for s in range(RIM_ROWS // 2):
            staged[strided(step - RIM_ROWS + d * (RIM_ROWS // 2) + s, n_row, step)] = block[
                s * n_row : (s + 1) * n_row
            ]
    out_ref[...] = staged[...].astype(BF16)


def tables(inputs_ref, qkv_w_ref, slots_ref, act_ref, attn_w_ref, rows):
    slab, wide = inputs_ref.shape
    token = slots_ref[0:1, :slab]
    alive = slots_ref[1:2, :slab]
    own = matmul(inputs_ref[...], qkv_w_ref[...]).astype(BF16).astype(F32)
    token_col = column_of(token, slab)
    live_col = column_of(alive, slab)
    query_hot = (token_col == (iota((slab, rows * BAND_PAD), 1) // BAND_PAD).astype(F32)).astype(F32)
    members = [jnp.broadcast_to(jnp.where(token_col == t, live_col, 0.0), (slab, LANES)) for t in range(rows)]
    counts = jnp.sum(jnp.where(iota((SUBLANES, slab), 0).astype(F32) == token, alive, 0.0), axis=1, keepdims=True)
    act_mean = jnp.mean(act_ref[...].astype(F32), axis=1, keepdims=True)
    attn_w = attn_w_ref[...]
    pieces = [attn_w]
    rest = jnp.broadcast_to(jnp.mean(attn_w.astype(F32), axis=1, keepdims=True), attn_w.shape)
    for _ in range(3):
        pieces.append(rest.astype(BF16))
        rest = rest - pieces[-1].astype(F32)
    attn_wide = jnp.concatenate(pieces, axis=1)
    return own, query_hot, live_col, members, jnp.maximum(counts, 1.0), act_mean, attn_wide


def triangle_kernel(n_row, rows, got_ref, normed_ref, gate_w_ref, out_ref, gate_ref, taken, right_terms, staged):
    gate_ref[...] = jax.nn.sigmoid(matmul(normed_ref[...], gate_w_ref[...]))
    taken[...] = got_ref[...].astype(F32)
    step = got_ref.shape[0] // n_row
    part = right_terms.shape[0]
    out_step = part * rows + RIM_ROWS
    for q in range(part):
        left = jnp.concatenate(
            [taken[strided(q * rows + i, n_row, step)] for i in range(rows)], axis=0
        ).astype(BF16)
        for j in range(rows):
            right_terms[q, strided(j, n_row, rows)] = taken[strided((part + q) * rows + j, n_row, step)]
        summed = matmul(left, right_terms[q].astype(BF16), NT)
        for i in range(rows):
            staged[strided(q * rows + i, n_row, out_step)] = summed[i * n_row : (i + 1) * n_row]
    nothing = jnp.zeros((1, LANES), F32)
    for s in range(RIM_ROWS):
        rim = taken[strided(step - RIM_ROWS + s, n_row, step)]
        if s < RIM_ROWS // 2:
            rim = jnp.concatenate([nothing, rim[:-1]], axis=0)
        else:
            rim = jnp.concatenate([rim[1:], nothing], axis=0)
        staged[strided(out_step - RIM_ROWS + s, n_row, out_step)] = rim
    out_ref[...] = staged[...].astype(BF16)


def finish_kernel(
    n_row, got_ref, pair_ref, out_w_ref, act_ref, slots_ref, bias_w_ref, gate_ref, inputs_ref, qkv_w_ref, attn_w_ref,
    ffn_in_ref, ffn_out_ref, agg_ref,
    pair_out, atom_out, token_out, taken, pair_new, atom_new, token_new, padded, sems,
):
    me = lax.axis_index("row")
    rows, cols, channels = pair_ref.shape
    part = channels // n_row
    step = part * rows + RIM_ROWS
    half = RIM_ROWS // 2
    slab, wide = act_ref.shape
    heads = bias_w_ref.shape[0]
    head_size = wide // heads
    taken[...] = got_ref[...].astype(F32)
    for i in range(rows):
        sums = jnp.concatenate([taken[strided(q * rows + i, n_row, step)] for q in range(part)], axis=0)
        update = matmul(normalize(sums, 0).astype(BF16), out_w_ref[...], TN)
        fresh = (pair_ref[i].astype(F32) + gate_ref[i * cols : (i + 1) * cols] * update).astype(BF16)
        pair_new[i] = fresh
        padded[i, :SUBLANES] = jnp.zeros((SUBLANES, channels), F32)
        padded[i, SUBLANES : SUBLANES + cols] = fresh.astype(F32)
        padded[i, SUBLANES + cols :] = jnp.zeros((BAND_PAD, channels), F32)
    pair_copy = pltpu.make_async_copy(pair_new, pair_out, sems.at[0])
    atom_copy = pltpu.make_async_copy(atom_new, atom_out, sems.at[1])
    token_copy = pltpu.make_async_copy(token_new, token_out, sems.at[2])
    pair_copy.start()

    @pl.when(me >= 0)
    def _():
        band = [padded[i, pl.ds(SUBLANES + (me - 1) * rows, BAND_PAD)] for i in range(rows)]
        band = normalize(jnp.concatenate(band, axis=0), 1).astype(BF16)
        bias_rows = matmul(bias_w_ref[...], band, NT).astype(BF16).astype(F32)
        own, query_hot, live_col, members, counts, act_mean, attn_wide = tables(
            inputs_ref, qkv_w_ref, slots_ref, act_ref, attn_w_ref, rows
        )
        outer = jnp.concatenate(
            [
                taken[strided(step - RIM_ROWS + d * half + s, n_row, step)][: min(n_row, SIDE - s * n_row)]
                for d in range(2)
                for s in range(half)
            ],
            axis=0,
        ).astype(BF16)
        outer = matmul(outer, qkv_w_ref[:, wide:]).astype(BF16).astype(F32)
        keys_ext, values_ext = (
            jnp.concatenate(
                [outer[:SIDE, at : at + wide], own[:, wide + at : 2 * wide + at], outer[SIDE:, at : at + wide]], axis=0
            ).astype(BF16)
            for at in (0, wide)
        )
        tag_at = [(step - RIM_ROWS + d * half + SIDE // n_row) + step * (SIDE % n_row) for d in range(2)]
        before_tag, after_tag = (taken[at : at + 1] for at in tag_at)
        own_tag = slots_ref[2:3]
        lane = iota((1, LANES), 1)
        flat = query_hot.shape[1]
        slot = (iota((flat, KEYS), 0) % BAND_PAD).astype(F32)
        head_of = iota((QUERY_WINDOW, wide), 1) // head_size
        mixed = []
        for w in range(slab // QUERY_WINDOW):
            start = w * QUERY_WINDOW
            before_end = SIDE - start
            own_end = before_end + slab
            is_before, is_own = lane < before_end, lane < own_end
            tag = jnp.where(
                is_before,
                pltpu.roll(before_tag, (SIDE - slab - start) % LANES, 1),
                jnp.where(
                    is_own, pltpu.roll(own_tag, before_end % LANES, 1), pltpu.roll(after_tag, own_end % LANES, 1)
                ),
            )
            offset = jnp.where(is_before, 0.0, jnp.where(is_own, 1.0 * rows, 2.0 * rows))
            valid = tag > 0
            key_slot = jnp.where(valid, tag - 1 + offset, -1.0)
            key_hot = (slot == key_slot).astype(BF16)
            query = own[start : start + QUERY_WINDOW, :wide]
            split = jnp.concatenate([jnp.where(head_of == h, query, 0.0) for h in range(heads)], axis=0).astype(BF16)
            product = matmul(split, keys_ext[start : start + KEYS], NT) * (1 / math.sqrt(head_size))
            product = jnp.where(valid, product, -1e30)
            product = product - jnp.max(product, axis=1, keepdims=True)
            hot = query_hot[start : start + QUERY_WINDOW]
            hot_bias = jnp.concatenate([hot * bias_rows[h : h + 1] for h in range(heads)], axis=0).astype(BF16)
            powers = jnp.exp(product + matmul(hot_bias, key_hot))
            blend = matmul(powers.astype(BF16), values_ext[start : start + KEYS])
            blend = blend / jnp.sum(powers, axis=1, keepdims=True)
            total = jnp.zeros((QUERY_WINDOW, wide), F32)
            for h in range(heads):
                total = jnp.where(head_of == h, blend[h * QUERY_WINDOW : (h + 1) * QUERY_WINDOW], total)
            mixed.append(total)
        attended = jnp.concatenate(mixed, axis=0).astype(BF16)
        mixture = matmul(attended, attn_wide)
        middle = act_ref[...].astype(F32) + mixture[:, :wide]
        shift = mixture[:, wide : 2 * wide] + mixture[:, 2 * wide : 3 * wide] + mixture[:, 3 * wide :]
        centred = middle - (act_mean + shift)
        spread = jnp.mean(centred * centred, axis=1, keepdims=True)
        expanded = matmul((centred * lax.rsqrt(spread + EPSILON)).astype(BF16), ffn_in_ref[...])
        hidden = ffn_out_ref.shape[0]
        inner = (jax.nn.silu(expanded[:, :hidden]) * expanded[:, hidden:]).astype(BF16)
        final = ((middle + matmul(inner, ffn_out_ref[...])) * live_col).astype(BF16)
        atom_new[...] = final
        atom_copy.start()
        features = jnp.maximum(matmul(final, agg_ref[...]), 0.0).astype(BF16).astype(F32)
        for b in range(features.shape[1] // LANES):
            block = features[:, b * LANES : (b + 1) * LANES]
            totals = [jnp.sum(block * members[t], axis=0, keepdims=True) for t in range(rows)]
            token_new[:, b * LANES : (b + 1) * LANES] = (
                jnp.concatenate(totals, axis=0) / counts[:rows]
            ).astype(BF16)
        token_copy.start()

    pair_copy.wait()
    atom_copy.wait()
    token_copy.wait()


def in_vmem(count):
    return [pl.BlockSpec(memory_space=pltpu.VMEM)] * count


def in_hbm(arrays):
    return [pltpu.with_memory_space_constraint(a, pltpu.HBM) for a in arrays]


def cost(flops, nbytes, exps=0):
    return pl.CostEstimate(flops=flops, bytes_accessed=nbytes, transcendentals=exps)


def exchange(blocks, n_row):
    grouped = blocks.reshape(n_row, -1, RIM_ROWS, LANES)
    return lax.all_to_all(grouped, "row", split_axis=0, concat_axis=0, tiled=True).reshape(blocks.shape)


def by_kernels(
    pair, token_mask, tri_in_weight, tri_gate_weight, tri_out_weight, atom_act, atom_cond, atom_token, atom_mask,
    ada_weight, qkv_weight, bias_weight, attn_out_weight, ffn_in_weight, ffn_out_weight, agg_weight,
):
    n_row = lax.axis_size("row")
    rows, cols, channels = pair.shape
    slab, wide = atom_act.shape
    width = rows * cols
    part = channels // n_row
    mask = token_mask.reshape(1, -1)
    token = atom_token.reshape(1, -1)
    alive = atom_mask.reshape(1, -1)
    sent = n_row * (2 * part * rows + RIM_ROWS)
    back_rows = n_row * (part * rows + RIM_ROWS)
    sources = (pair, atom_act, bias_weight.T, tri_in_weight, atom_cond, ada_weight, mask, token, alive)
    kept = 3
    pair, atom_act, bias_rows, terms, normed, inputs, slots = pl.pallas_call(
        functools.partial(send_kernel, n_row),
        out_shape=(
            *(jax.ShapeDtypeStruct(a.shape, a.dtype) for a in sources[:kept]),
            jax.ShapeDtypeStruct((sent, LANES), BF16),
            jax.ShapeDtypeStruct((width, channels), BF16),
            jax.ShapeDtypeStruct((slab, wide), BF16),
            jax.ShapeDtypeStruct((SUBLANES, LANES), F32),
        ),
        in_specs=[pl.BlockSpec(memory_space=pltpu.HBM)] * len(sources),
        out_specs=tuple(in_vmem(kept + 4)),
        scratch_shapes=[
            *(pltpu.VMEM(a.shape, a.dtype) for a in sources[kept:]),
            pltpu.VMEM((sent, LANES), F32),
            pltpu.SemaphoreType.DMA((len(sources),)),
        ],
        cost_estimate=cost(8 * width * channels * channels, 1 << 20, 2 * width * channels),
        compiler_params=LIMIT,
        name="send",
    )(*in_hbm(sources))
    got = exchange(terms, n_row)
    sums, gate = pl.pallas_call(
        functools.partial(triangle_kernel, n_row, rows),
        out_shape=(
            jax.ShapeDtypeStruct((back_rows, LANES), BF16),
            jax.ShapeDtypeStruct((width, channels), F32),
        ),
        in_specs=in_vmem(3),
        out_specs=tuple(in_vmem(2)),
        scratch_shapes=[
            pltpu.VMEM((sent, LANES), F32),
            pltpu.VMEM((part, cols, cols), F32),
            pltpu.VMEM((back_rows, LANES), F32),
        ],
        cost_estimate=cost(2 * width * width, 1 << 19),
        compiler_params=LIMIT,
        name="triangle",
    )(got, normed, tri_gate_weight)
    back = exchange(sums, n_row)
    token_shape = (rows, agg_weight.shape[1])
    return pl.pallas_call(
        functools.partial(finish_kernel, n_row),
        out_shape=(
            jax.ShapeDtypeStruct(pair.shape, BF16),
            jax.ShapeDtypeStruct(atom_act.shape, BF16),
            jax.ShapeDtypeStruct(token_shape, BF16),
        ),
        in_specs=in_vmem(13),
        out_specs=(pl.BlockSpec(memory_space=pltpu.HBM),) * 3,
        scratch_shapes=[
            pltpu.VMEM((back_rows, LANES), F32),
            pltpu.VMEM(pair.shape, BF16),
            pltpu.VMEM(atom_act.shape, BF16),
            pltpu.VMEM(token_shape, BF16),
            pltpu.VMEM((rows, SUBLANES + cols + BAND_PAD, channels), F32),
            pltpu.SemaphoreType.DMA((3,)),
        ],
        cost_estimate=cost(4 * width * channels * channels, 1 << 20),
        compiler_params=LIMIT,
        name="finish",
    )(
        back, pair, tri_out_weight, atom_act, slots, bias_rows, gate, inputs, qkv_weight, attn_out_weight,
        ffn_in_weight, ffn_out_weight, agg_weight,
    )


def kernels_fit(mesh, args):
    pair, atom_act, bias_weight = args[0], args[5], args[11]
    n_row = mesh.shape["row"]
    parts = mesh.shape["groups"] * n_row
    cols, channels = pair.shape[1:]
    rows = pair.shape[0] // parts
    slab = atom_act.shape[0] // parts
    wide = atom_act.shape[1]
    return (
        mesh.shape["col"] == 1
        and cols == channels == wide == LANES
        and cols == n_row * rows
        and channels % n_row == 0
        and n_row % SUBLANES == 0
        and SIDE < RIM_ROWS // 2 * n_row
        and 3 * rows <= BAND_PAD
        and rows <= SUBLANES
        and slab // QUERY_WINDOW <= SUBLANES
        and SIDE <= slab <= LANES
        and slab % QUERY_WINDOW == 0
        and slab - QUERY_WINDOW <= SIDE
        and wide % bias_weight.shape[1] == 0
    )


def solution(mesh):
    in_specs = (
        P(("groups", "row"), "col", None),
        P("groups"),
        P(),
        P(),
        P(),
        P(("groups", "row"), None),
        P(("groups", "row"), None),
        P(("groups", "row")),
        P(("groups", "row")),
        P(),
        P(),
        P(),
        P(),
        P(),
        P(),
        P(),
    )
    out_specs = (
        P(("groups", "row"), "col", None),
        P(("groups", "row"), None),
        P(("groups", "row"), None),
    )

    def layer(*args):
        body = by_kernels if kernels_fit(mesh, args) else per_device
        return jax.shard_map(body, mesh=mesh, in_specs=in_specs, out_specs=out_specs, check_vma=False)(*args)

    return layer
```

```python
import functools
import math

import jax
import jax.numpy as jnp
from jax import lax
from jax.experimental import pallas as pl
from jax.experimental.pallas import tpu as pltpu
from jax.sharding import PartitionSpec as P

QUERY_WINDOW = 32
KEYS = 128


EPSILON = 1e-05


def extended(shard, sides, width):
    for axis, dim in sides:
        size, length = (lax.axis_size(axis), shard.shape[dim])
        up = [(i, (i + 1) % size) for i in range(size - 1)]
        down = [(j, i) for i, j in up]
        last = lax.slice_in_dim(shard, length - width, length, axis=dim)
        first = lax.slice_in_dim(shard, 0, width, axis=dim)
        before = lax.ppermute(last, axis, up)
        after = lax.ppermute(first, axis, down)
        shard = jnp.concatenate([before, shard, after], axis=dim)
    return shard


def layer_norm(values, along):
    average = jnp.mean(values, axis=along, keepdims=True)
    centred = values - average
    spread = jnp.mean(centred * centred, axis=along, keepdims=True)
    return centred / jnp.sqrt(spread + EPSILON)


def per_device(
    pair,
    token_mask,
    tri_in_weight,
    tri_gate_weight,
    tri_out_weight,
    atom_act,
    atom_cond,
    atom_token,
    atom_mask,
    ada_weight,
    qkv_weight,
    bias_weight,
    attn_out_weight,
    ffn_in_weight,
    ffn_out_weight,
    agg_weight,
):
    tok_rows = pair.shape[0]
    col_count = pair.shape[1]
    channels = pair.shape[2]
    row_index = lax.axis_index("row")
    col_index = lax.axis_index("col")
    pair_float = pair.astype(jnp.float32)
    pair_norm = layer_norm(pair_float, 2).astype(jnp.bfloat16)
    row_live = lax.dynamic_slice_in_dim(token_mask, row_index * tok_rows, tok_rows, 0).astype(
        jnp.float32
    )
    col_live = lax.dynamic_slice_in_dim(token_mask, col_index * col_count, col_count, 0).astype(
        jnp.float32
    )
    pair_live = row_live[:, None] * col_live[None, :]
    left_terms = jnp.einsum(
        "ijd,de->eij",
        pair_norm,
        tri_in_weight[:, : 2 * channels],
        preferred_element_type=jnp.float32,
    )
    left = (jax.nn.sigmoid(left_terms[channels:]) * left_terms[:channels] * pair_live).astype(
        jnp.bfloat16
    )
    right_terms = jnp.einsum(
        "ijd,de->eij",
        pair_norm,
        tri_in_weight[:, 2 * channels :],
        preferred_element_type=jnp.float32,
    )
    right = (jax.nn.sigmoid(right_terms[channels:]) * right_terms[:channels] * pair_live).astype(
        jnp.bfloat16
    )
    tri_gate = jax.nn.sigmoid(
        jnp.einsum("ijd,de->ije", pair_norm, tri_gate_weight, preferred_element_type=jnp.float32)
    )
    left_owned, right_owned = (
        lax.all_to_all(left, "row", split_axis=0, concat_axis=1, tiled=True),
        lax.all_to_all(right, "row", split_axis=0, concat_axis=1, tiled=True),
    )
    left_full, right_rows = (
        lax.all_gather(left_owned, "col", axis=2, tiled=True),
        lax.all_gather(right_owned, "col", axis=2, tiled=True),
    )
    right_used = lax.dynamic_slice_in_dim(right_rows, col_index * col_count, col_count, 1)
    tri_sum = jnp.einsum(
        "cik,cjk->cij", left_full, right_used, preferred_element_type=jnp.float32
    ).astype(jnp.bfloat16)
    merged = lax.all_to_all(tri_sum, "row", split_axis=1, concat_axis=0, tiled=True)
    tri_norm = layer_norm(merged.astype(jnp.float32), 0).astype(jnp.bfloat16)
    update = jnp.einsum("dij,de->ije", tri_norm, tri_out_weight, preferred_element_type=jnp.float32)
    pair_out = (pair_float + tri_gate * update).astype(jnp.bfloat16)
    band_width = 3 * tok_rows
    targets = (row_index - 1) * tok_rows + jnp.arange(band_width, dtype=jnp.int32)
    columns = col_index * col_count + jnp.arange(col_count, dtype=jnp.int32)
    selector = (columns[:, None] == targets[None, :]).astype(jnp.bfloat16)
    band_part = jnp.einsum("ijd,jb->ibd", pair_out, selector, preferred_element_type=jnp.float32)
    band = lax.psum(band_part.astype(jnp.bfloat16), "col").astype(jnp.float32)
    band_norm = layer_norm(band, 2).astype(jnp.bfloat16)
    bias_table = jnp.einsum(
        "ibd,dh->ibh", band_norm, bias_weight, preferred_element_type=jnp.float32
    ).astype(jnp.bfloat16)
    slab = atom_act.shape[0]
    window_width = atom_act.shape[1]
    heads = bias_weight.shape[1]
    head_size = window_width // heads
    side = (KEYS - QUERY_WINDOW) // 2
    windows = slab // QUERY_WINDOW
    local_token = atom_token - row_index * tok_rows
    live = atom_mask.astype(jnp.float32)
    token_tag = ((local_token + 1) * atom_mask).astype(jnp.bfloat16)
    ada = jnp.dot(atom_cond, ada_weight, preferred_element_type=jnp.float32)
    atom_inputs = (
        jax.nn.sigmoid(ada[:, :window_width]) * layer_norm(atom_act.astype(jnp.float32), 1)
        + ada[:, window_width:]
    ).astype(jnp.bfloat16)
    projected = jnp.dot(atom_inputs, qkv_weight, preferred_element_type=jnp.float32).astype(
        jnp.bfloat16
    )
    queries = projected[:, :window_width]
    ext_pairs, ext_tag = (
        extended(projected[:, window_width:], (("row", 0),), side),
        extended(token_tag, (("row", 0),), side),
    )
    ext_rows = slab + 2 * side
    ext_position = jnp.arange(ext_rows, dtype=jnp.int32)
    offset = jnp.where(
        ext_position < side, 0, jnp.where(ext_position < side + slab, tok_rows, 2 * tok_rows)
    )
    tag_value = ext_tag.astype(jnp.int32)
    key_valid = tag_value > 0
    band_index = tag_value - 1 + offset
    band_slots = jnp.arange(band_width, dtype=jnp.int32)
    key_onehot = ((band_index[:, None] == band_slots[None, :]) & key_valid[:, None]).astype(
        jnp.bfloat16
    )
    query_onehot = (local_token[:, None] == jnp.arange(tok_rows, dtype=jnp.int32)[None, :]).astype(
        jnp.bfloat16
    )
    query_bias = jnp.einsum(
        "lt,tbh->lbh", query_onehot, bias_table, preferred_element_type=jnp.float32
    ).astype(jnp.bfloat16)
    query_bias = query_bias.reshape(windows, QUERY_WINDOW, band_width, heads)
    key_index = (
        jnp.arange(windows, dtype=jnp.int32)[:, None] * QUERY_WINDOW
        + jnp.arange(KEYS, dtype=jnp.int32)[None, :]
    )
    window_pairs = ext_pairs[key_index]
    window_onehot = key_onehot[key_index]
    window_valid = key_valid[key_index]
    window_bias = jnp.einsum(
        "wlbh,wmb->whlm", query_bias, window_onehot, preferred_element_type=jnp.float32
    )
    query_heads = queries.reshape(windows, QUERY_WINDOW, heads, head_size)
    key_heads = window_pairs[..., :window_width].reshape(windows, KEYS, heads, head_size)
    value_heads = window_pairs[..., window_width:].reshape(windows, KEYS, heads, head_size)
    logit_scores = (
        jnp.einsum("wlhd,wmhd->whlm", query_heads, key_heads, preferred_element_type=jnp.float32)
        / math.sqrt(head_size)
        + window_bias
    )
    logit_scores = jnp.where(window_valid[:, None, None, :], logit_scores, -1e30)
    attn_weights = jax.nn.softmax(logit_scores, axis=-1).astype(jnp.bfloat16)
    attended = (
        jnp.einsum("whlm,wmhd->wlhd", attn_weights, value_heads, preferred_element_type=jnp.float32)
        .reshape(slab, window_width)
        .astype(jnp.bfloat16)
    )
    atom_mid = atom_act.astype(jnp.float32) + jnp.dot(
        attended, attn_out_weight, preferred_element_type=jnp.float32
    )
    atom_norm = layer_norm(atom_mid, 1).astype(jnp.bfloat16)
    expanded = jnp.dot(atom_norm, ffn_in_weight, preferred_element_type=jnp.float32)
    hidden_width = ffn_out_weight.shape[0]
    inner = (jax.nn.silu(expanded[:, :hidden_width]) * expanded[:, hidden_width:]).astype(
        jnp.bfloat16
    )
    atom_out = (
        (atom_mid + jnp.dot(inner, ffn_out_weight, preferred_element_type=jnp.float32))
        * live[:, None]
    ).astype(jnp.bfloat16)
    features = jax.nn.relu(
        jnp.dot(atom_out, agg_weight, preferred_element_type=jnp.float32)
    ).astype(jnp.bfloat16)
    live_onehot = query_onehot * atom_mask.astype(jnp.bfloat16)[:, None]
    token_sums = jnp.einsum("at,ac->tc", live_onehot, features, preferred_element_type=jnp.float32)
    token_counts = jnp.sum(live_onehot.astype(jnp.float32), axis=0)
    token_out = (token_sums / token_counts[:, None]).astype(jnp.bfloat16)
    return (pair_out, atom_out, token_out)


LANES = 128
SUBLANES = 8
SIDE = (KEYS - QUERY_WINDOW) // 2
RIM_ROWS = 4
BAND_PAD = 2 * SUBLANES
LIMIT = pltpu.CompilerParams(vmem_limit_bytes=8 << 20)
F32 = jnp.float32
BF16 = jnp.bfloat16
NT = (((1,), (1,)), ((), ()))
TN = (((0,), (0,)), ((), ()))
TT = (((0,), (1,)), ((), ()))


def matmul(a, b, dims=(((1,), (0,)), ((), ()))):
    return lax.dot_general(a, b, dims, preferred_element_type=F32)


def normalize(values, axis):
    average = jnp.mean(values, axis=axis, keepdims=True)
    centred = values - average
    spread = jnp.mean(centred * centred, axis=axis, keepdims=True)
    return centred * lax.rsqrt(spread + EPSILON)


def iota(shape, dim):
    return lax.broadcasted_iota(jnp.int32, shape, dim)


def column_of(row, size):
    eye = iota((size, size), 0) == iota((size, size), 1)
    return jnp.sum(jnp.where(eye, row, 0.0), axis=1, keepdims=True)


def pad_lanes(row):
    return jnp.concatenate([row, jnp.zeros((row.shape[0], LANES - row.shape[1]), row.dtype)], axis=1)


def strided(first, count, step):
    return pl.ds(first, count, stride=step)


def send_kernel(
    n_row, pair_hbm, act_hbm, bias_w_hbm, in_w_hbm, cond_hbm, ada_w_hbm, mask_hbm, token_hbm, alive_hbm,
    pair_ref, act_ref, bias_w_ref, out_ref, normed_ref, inputs_ref, slots_ref,
    in_w_ref, cond_ref, ada_w_ref, mask_ref, token_ref, alive_ref, staged, sems,
):
    sources = (pair_hbm, cond_hbm, act_hbm, mask_hbm, token_hbm, alive_hbm, bias_w_hbm, ada_w_hbm, in_w_hbm)
    places = (pair_ref, cond_ref, act_ref, mask_ref, token_ref, alive_ref, bias_w_ref, ada_w_ref, in_w_ref)
    loads = [pltpu.make_async_copy(a, b, sems.at[i]) for i, (a, b) in enumerate(zip(sources, places))]
    for load in loads:
        load.start()
    loads[0].wait()
    me = lax.axis_index("row")
    rows, cols, channels = pair_ref.shape
    part = channels // n_row
    width = rows * cols
    step = 2 * part * rows + RIM_ROWS
    normed = normalize(pair_ref[...].reshape(width, channels).astype(F32), 1).astype(BF16)
    normed_ref[...] = normed
    for load in loads[1:]:
        load.wait()
    live = mask_ref[...].astype(F32)
    lane = iota(live.shape, 1)
    both = jnp.concatenate(
        [live * jnp.sum(jnp.where(lane == me * rows + i, live, 0.0), axis=1, keepdims=True) for i in range(rows)],
        axis=1,
    )
    for side in range(2):
        first = 2 * side * channels
        value = matmul(in_w_ref[:, first : first + channels], normed, TT)
        gate = matmul(in_w_ref[:, first + channels : first + 2 * channels], normed, TT)
        term = jax.nn.sigmoid(gate) * value * both
        for q in range(part):
            for i in range(rows):
                staged[strided((side * part + q) * rows + i, n_row, step)] = term[
                    q * n_row : (q + 1) * n_row, i * cols : (i + 1) * cols
                ]
    act = act_ref[...].astype(F32)
    ada = matmul(cond_ref[...], ada_w_ref[...])
    slab, wide = act.shape
    inputs = (jax.nn.sigmoid(ada[:, :wide]) * normalize(act, 1) + ada[:, wide:]).astype(BF16)
    inputs_ref[...] = inputs
    inputs = inputs.astype(F32)
    token = token_ref[...] - me * rows
    alive = alive_ref[...]
    tag = pad_lanes(((token + 1) * alive).astype(F32))
    slots_ref[...] = jnp.zeros(slots_ref.shape, F32)
    slots_ref[0:1] = pad_lanes(token.astype(F32))
    slots_ref[1:2] = pad_lanes(alive.astype(F32))
    slots_ref[2:3] = tag
    tags = jnp.broadcast_to(tag, (2 * n_row - SIDE, LANES))
    for d, rim in enumerate((inputs[slab - SIDE :], inputs[:SIDE])):
        block = jnp.concatenate([rim, tags], axis=0)
        for s in range(RIM_ROWS // 2):
            staged[strided(step - RIM_ROWS + d * (RIM_ROWS // 2) + s, n_row, step)] = block[
                s * n_row : (s + 1) * n_row
            ]
    out_ref[...] = staged[...].astype(BF16)


def tables(inputs_ref, qkv_w_ref, slots_ref, act_ref, attn_w_ref, rows):
    slab, wide = inputs_ref.shape
    token = slots_ref[0:1, :slab]
    alive = slots_ref[1:2, :slab]
    own = matmul(inputs_ref[...], qkv_w_ref[...]).astype(BF16).astype(F32)
    token_col = column_of(token, slab)
    live_col = column_of(alive, slab)
    query_hot = (token_col == (iota((slab, rows * BAND_PAD), 1) // BAND_PAD).astype(F32)).astype(F32)
    members = [jnp.broadcast_to(jnp.where(token_col == t, live_col, 0.0), (slab, LANES)) for t in range(rows)]
    counts = jnp.sum(jnp.where(iota((SUBLANES, slab), 0).astype(F32) == token, alive, 0.0), axis=1, keepdims=True)
    act_mean = jnp.mean(act_ref[...].astype(F32), axis=1, keepdims=True)
    attn_w = attn_w_ref[...]
    pieces = [attn_w]
    rest = jnp.broadcast_to(jnp.mean(attn_w.astype(F32), axis=1, keepdims=True), attn_w.shape)
    for _ in range(3):
        pieces.append(rest.astype(BF16))
        rest = rest - pieces[-1].astype(F32)
    attn_wide = jnp.concatenate(pieces, axis=1)
    return own, query_hot, live_col, members, jnp.maximum(counts, 1.0), act_mean, attn_wide


def triangle_kernel(n_row, rows, got_ref, normed_ref, gate_w_ref, out_ref, gate_ref, taken, right_terms, staged):
    gate_ref[...] = jax.nn.sigmoid(matmul(normed_ref[...], gate_w_ref[...]))
    taken[...] = got_ref[...].astype(F32)
    step = got_ref.shape[0] // n_row
    part = right_terms.shape[0]
    out_step = part * rows + RIM_ROWS
    for q in range(part):
        left = jnp.concatenate(
            [taken[strided(q * rows + i, n_row, step)] for i in range(rows)], axis=0
        ).astype(BF16)
        for j in range(rows):
            right_terms[q, strided(j, n_row, rows)] = taken[strided((part + q) * rows + j, n_row, step)]
        summed = matmul(left, right_terms[q].astype(BF16), NT)
        for i in range(rows):
            staged[strided(q * rows + i, n_row, out_step)] = summed[i * n_row : (i + 1) * n_row]
    nothing = jnp.zeros((1, LANES), F32)
    for s in range(RIM_ROWS):
        rim = taken[strided(step - RIM_ROWS + s, n_row, step)]
        if s < RIM_ROWS // 2:
            rim = jnp.concatenate([nothing, rim[:-1]], axis=0)
        else:
            rim = jnp.concatenate([rim[1:], nothing], axis=0)
        staged[strided(out_step - RIM_ROWS + s, n_row, out_step)] = rim
    out_ref[...] = staged[...].astype(BF16)


def finish_kernel(
    n_row, got_ref, pair_ref, out_w_ref, act_ref, slots_ref, bias_w_ref, gate_ref, inputs_ref, qkv_w_ref, attn_w_ref,
    ffn_in_ref, ffn_out_ref, agg_ref,
    pair_out, atom_out, token_out, taken, pair_new, atom_new, token_new, padded, sems,
):
    me = lax.axis_index("row")
    rows, cols, channels = pair_ref.shape
    part = channels // n_row
    step = part * rows + RIM_ROWS
    half = RIM_ROWS // 2
    slab, wide = act_ref.shape
    heads = bias_w_ref.shape[0]
    head_size = wide // heads
    taken[...] = got_ref[...].astype(F32)
    for i in range(rows):
        sums = jnp.concatenate([taken[strided(q * rows + i, n_row, step)] for q in range(part)], axis=0)
        update = matmul(normalize(sums, 0).astype(BF16), out_w_ref[...], TN)
        fresh = (pair_ref[i].astype(F32) + gate_ref[i * cols : (i + 1) * cols] * update).astype(BF16)
        pair_new[i] = fresh
        padded[i, :SUBLANES] = jnp.zeros((SUBLANES, channels), F32)
        padded[i, SUBLANES : SUBLANES + cols] = fresh.astype(F32)
        padded[i, SUBLANES + cols :] = jnp.zeros((BAND_PAD, channels), F32)
    pair_copy = pltpu.make_async_copy(pair_new, pair_out, sems.at[0])
    atom_copy = pltpu.make_async_copy(atom_new, atom_out, sems.at[1])
    token_copy = pltpu.make_async_copy(token_new, token_out, sems.at[2])
    pair_copy.start()

    @pl.when(me >= 0)
    def _():
        band = [padded[i, pl.ds(SUBLANES + (me - 1) * rows, BAND_PAD)] for i in range(rows)]
        band = jnp.concatenate(band, axis=0)
        band = band - jnp.mean(band, axis=1, keepdims=True)
        squares = band * band
        high = squares.astype(BF16)
        low = (squares - high.astype(F32)).astype(BF16)
        share = jnp.full(bias_w_ref.shape, 1 / channels, BF16)
        spread = matmul(share, high, NT) + matmul(share, low, NT)
        bias_rows = matmul(bias_w_ref[...], band.astype(BF16), NT) * lax.rsqrt(spread + EPSILON)
        bias_rows = bias_rows.astype(BF16).astype(F32)
        own, query_hot, live_col, members, counts, act_mean, attn_wide = tables(
            inputs_ref, qkv_w_ref, slots_ref, act_ref, attn_w_ref, rows
        )
        outer = jnp.concatenate(
            [
                taken[strided(step - RIM_ROWS + d * half + s, n_row, step)][: min(n_row, SIDE - s * n_row)]
                for d in range(2)
                for s in range(half)
            ],
            axis=0,
        ).astype(BF16)
        outer = matmul(outer, qkv_w_ref[:, wide:]).astype(BF16).astype(F32)
        keys_ext, values_ext = (
            jnp.concatenate(
                [outer[:SIDE, at : at + wide], own[:, wide + at : 2 * wide + at], outer[SIDE:, at : at + wide]], axis=0
            ).astype(BF16)
            for at in (0, wide)
        )
        tag_at = [(step - RIM_ROWS + d * half + SIDE // n_row) + step * (SIDE % n_row) for d in range(2)]
        before_tag, after_tag = (taken[at : at + 1] for at in tag_at)
        own_tag = slots_ref[2:3]
        lane = iota((1, LANES), 1)
        flat = query_hot.shape[1]
        slot = (iota((flat, KEYS), 0) % BAND_PAD).astype(F32)
        head_of = iota((QUERY_WINDOW, wide), 1) // head_size
        mixed = []
        for w in range(slab // QUERY_WINDOW):
            start = w * QUERY_WINDOW
            before_end = SIDE - start
            own_end = before_end + slab
            is_before, is_own = lane < before_end, lane < own_end
            tag = jnp.where(
                is_before,
                pltpu.roll(before_tag, (SIDE - slab - start) % LANES, 1),
                jnp.where(
                    is_own, pltpu.roll(own_tag, before_end % LANES, 1), pltpu.roll(after_tag, own_end % LANES, 1)
                ),
            )
            offset = jnp.where(is_before, 0.0, jnp.where(is_own, 1.0 * rows, 2.0 * rows))
            valid = tag > 0
            key_slot = jnp.where(valid, tag - 1 + offset, -1.0)
            key_hot = (slot == key_slot).astype(BF16)
            query = own[start : start + QUERY_WINDOW, :wide]
            split = jnp.concatenate([jnp.where(head_of == h, query, 0.0) for h in range(heads)], axis=0).astype(BF16)
            product = matmul(split, keys_ext[start : start + KEYS], NT) * (1 / math.sqrt(head_size))
            product = jnp.where(valid, product, -1e30)
            product = product - jnp.max(product, axis=1, keepdims=True)
            hot = query_hot[start : start + QUERY_WINDOW]
            hot_bias = jnp.concatenate([hot * bias_rows[h : h + 1] for h in range(heads)], axis=0).astype(BF16)
            powers = jnp.exp(product + matmul(hot_bias, key_hot))
            blend = matmul(powers.astype(BF16), values_ext[start : start + KEYS])
            blend = blend / jnp.sum(powers, axis=1, keepdims=True)
            total = jnp.zeros((QUERY_WINDOW, wide), F32)
            for h in range(heads):
                total = jnp.where(head_of == h, blend[h * QUERY_WINDOW : (h + 1) * QUERY_WINDOW], total)
            mixed.append(total)
        attended = jnp.concatenate(mixed, axis=0).astype(BF16)
        mixture = matmul(attended, attn_wide)
        middle = act_ref[...].astype(F32) + mixture[:, :wide]
        shift = mixture[:, wide : 2 * wide] + mixture[:, 2 * wide : 3 * wide] + mixture[:, 3 * wide :]
        centred = middle - (act_mean + shift)
        spread = jnp.mean(centred * centred, axis=1, keepdims=True)
        expanded = matmul(centred.astype(BF16), ffn_in_ref[...]) * lax.rsqrt(spread + EPSILON)
        hidden = ffn_out_ref.shape[0]
        inner = (jax.nn.silu(expanded[:, :hidden]) * expanded[:, hidden:]).astype(BF16)
        final = ((middle + matmul(inner, ffn_out_ref[...])) * live_col).astype(BF16)
        atom_new[...] = final
        atom_copy.start()
        features = jnp.maximum(matmul(final, agg_ref[...]), 0.0).astype(BF16).astype(F32)
        for b in range(features.shape[1] // LANES):
            block = features[:, b * LANES : (b + 1) * LANES]
            totals = [jnp.sum(block * members[t], axis=0, keepdims=True) for t in range(rows)]
            token_new[:, b * LANES : (b + 1) * LANES] = (
                jnp.concatenate(totals, axis=0) / counts[:rows]
            ).astype(BF16)
        token_copy.start()

    pair_copy.wait()
    atom_copy.wait()
    token_copy.wait()


def in_vmem(count):
    return [pl.BlockSpec(memory_space=pltpu.VMEM)] * count


def in_hbm(arrays):
    return [pltpu.with_memory_space_constraint(a, pltpu.HBM) for a in arrays]


def cost(flops, nbytes, exps=0):
    return pl.CostEstimate(flops=flops, bytes_accessed=nbytes, transcendentals=exps)


def exchange(blocks, n_row):
    grouped = blocks.reshape(n_row, -1, RIM_ROWS, LANES)
    return lax.all_to_all(grouped, "row", split_axis=0, concat_axis=0, tiled=True).reshape(blocks.shape)


def by_kernels(
    pair, token_mask, tri_in_weight, tri_gate_weight, tri_out_weight, atom_act, atom_cond, atom_token, atom_mask,
    ada_weight, qkv_weight, bias_weight, attn_out_weight, ffn_in_weight, ffn_out_weight, agg_weight,
):
    n_row = lax.axis_size("row")
    rows, cols, channels = pair.shape
    slab, wide = atom_act.shape
    width = rows * cols
    part = channels // n_row
    mask = token_mask.reshape(1, -1)
    token = atom_token.reshape(1, -1)
    alive = atom_mask.reshape(1, -1)
    sent = n_row * (2 * part * rows + RIM_ROWS)
    back_rows = n_row * (part * rows + RIM_ROWS)
    sources = (pair, atom_act, bias_weight.T, tri_in_weight, atom_cond, ada_weight, mask, token, alive)
    kept = 3
    pair, atom_act, bias_rows, terms, normed, inputs, slots = pl.pallas_call(
        functools.partial(send_kernel, n_row),
        out_shape=(
            *(jax.ShapeDtypeStruct(a.shape, a.dtype) for a in sources[:kept]),
            jax.ShapeDtypeStruct((sent, LANES), BF16),
            jax.ShapeDtypeStruct((width, channels), BF16),
            jax.ShapeDtypeStruct((slab, wide), BF16),
            jax.ShapeDtypeStruct((SUBLANES, LANES), F32),
        ),
        in_specs=[pl.BlockSpec(memory_space=pltpu.HBM)] * len(sources),
        out_specs=tuple(in_vmem(kept + 4)),
        scratch_shapes=[
            *(pltpu.VMEM(a.shape, a.dtype) for a in sources[kept:]),
            pltpu.VMEM((sent, LANES), F32),
            pltpu.SemaphoreType.DMA((len(sources),)),
        ],
        cost_estimate=cost(8 * width * channels * channels, 1 << 20, 2 * width * channels),
        compiler_params=LIMIT,
        name="send",
    )(*in_hbm(sources))
    got = exchange(terms, n_row)
    sums, gate = pl.pallas_call(
        functools.partial(triangle_kernel, n_row, rows),
        out_shape=(
            jax.ShapeDtypeStruct((back_rows, LANES), BF16),
            jax.ShapeDtypeStruct((width, channels), F32),
        ),
        in_specs=in_vmem(3),
        out_specs=tuple(in_vmem(2)),
        scratch_shapes=[
            pltpu.VMEM((sent, LANES), F32),
            pltpu.VMEM((part, cols, cols), F32),
            pltpu.VMEM((back_rows, LANES), F32),
        ],
        cost_estimate=cost(2 * width * width, 1 << 19),
        compiler_params=LIMIT,
        name="triangle",
    )(got, normed, tri_gate_weight)
    back = exchange(sums, n_row)
    token_shape = (rows, agg_weight.shape[1])
    return pl.pallas_call(
        functools.partial(finish_kernel, n_row),
        out_shape=(
            jax.ShapeDtypeStruct(pair.shape, BF16),
            jax.ShapeDtypeStruct(atom_act.shape, BF16),
            jax.ShapeDtypeStruct(token_shape, BF16),
        ),
        in_specs=in_vmem(13),
        out_specs=(pl.BlockSpec(memory_space=pltpu.HBM),) * 3,
        scratch_shapes=[
            pltpu.VMEM((back_rows, LANES), F32),
            pltpu.VMEM(pair.shape, BF16),
            pltpu.VMEM(atom_act.shape, BF16),
            pltpu.VMEM(token_shape, BF16),
            pltpu.VMEM((rows, SUBLANES + cols + BAND_PAD, channels), F32),
            pltpu.SemaphoreType.DMA((3,)),
        ],
        cost_estimate=cost(4 * width * channels * channels, 1 << 20),
        compiler_params=LIMIT,
        name="finish",
    )(
        back, pair, tri_out_weight, atom_act, slots, bias_rows, gate, inputs, qkv_weight, attn_out_weight,
        ffn_in_weight, ffn_out_weight, agg_weight,
    )


def kernels_fit(mesh, args):
    pair, atom_act, bias_weight = args[0], args[5], args[11]
    n_row = mesh.shape["row"]
    parts = mesh.shape["groups"] * n_row
    cols, channels = pair.shape[1:]
    rows = pair.shape[0] // parts
    slab = atom_act.shape[0] // parts
    wide = atom_act.shape[1]
    return (
        mesh.shape["col"] == 1
        and cols == channels == wide == LANES
        and cols == n_row * rows
        and channels % n_row == 0
        and n_row % SUBLANES == 0
        and SIDE < RIM_ROWS // 2 * n_row
        and 3 * rows <= BAND_PAD
        and rows <= SUBLANES
        and slab // QUERY_WINDOW <= SUBLANES
        and SIDE <= slab <= LANES
        and slab % QUERY_WINDOW == 0
        and slab - QUERY_WINDOW <= SIDE
        and wide % bias_weight.shape[1] == 0
    )


def solution(mesh):
    in_specs = (
        P(("groups", "row"), "col", None),
        P("groups"),
        P(),
        P(),
        P(),
        P(("groups", "row"), None),
        P(("groups", "row"), None),
        P(("groups", "row")),
        P(("groups", "row")),
        P(),
        P(),
        P(),
        P(),
        P(),
        P(),
        P(),
    )
    out_specs = (
        P(("groups", "row"), "col", None),
        P(("groups", "row"), None),
        P(("groups", "row"), None),
    )

    def layer(*args):
        body = by_kernels if kernels_fit(mesh, args) else per_device
        return jax.shard_map(body, mesh=mesh, in_specs=in_specs, out_specs=out_specs, check_vma=False)(*args)

    return layer
```

```python
import functools
import math

import jax
import jax.numpy as jnp
from jax import lax
from jax.experimental import pallas as pl
from jax.experimental.pallas import tpu as pltpu
from jax.sharding import PartitionSpec as P

QUERY_WINDOW = 32
KEYS = 128


EPSILON = 1e-05


def extended(shard, sides, width):
    for axis, dim in sides:
        size, length = (lax.axis_size(axis), shard.shape[dim])
        up = [(i, (i + 1) % size) for i in range(size - 1)]
        down = [(j, i) for i, j in up]
        last = lax.slice_in_dim(shard, length - width, length, axis=dim)
        first = lax.slice_in_dim(shard, 0, width, axis=dim)
        before = lax.ppermute(last, axis, up)
        after = lax.ppermute(first, axis, down)
        shard = jnp.concatenate([before, shard, after], axis=dim)
    return shard


def layer_norm(values, along):
    average = jnp.mean(values, axis=along, keepdims=True)
    centred = values - average
    spread = jnp.mean(centred * centred, axis=along, keepdims=True)
    return centred / jnp.sqrt(spread + EPSILON)


def per_device(
    pair,
    token_mask,
    tri_in_weight,
    tri_gate_weight,
    tri_out_weight,
    atom_act,
    atom_cond,
    atom_token,
    atom_mask,
    ada_weight,
    qkv_weight,
    bias_weight,
    attn_out_weight,
    ffn_in_weight,
    ffn_out_weight,
    agg_weight,
):
    tok_rows = pair.shape[0]
    col_count = pair.shape[1]
    channels = pair.shape[2]
    row_index = lax.axis_index("row")
    col_index = lax.axis_index("col")
    pair_float = pair.astype(jnp.float32)
    pair_norm = layer_norm(pair_float, 2).astype(jnp.bfloat16)
    row_live = lax.dynamic_slice_in_dim(token_mask, row_index * tok_rows, tok_rows, 0).astype(
        jnp.float32
    )
    col_live = lax.dynamic_slice_in_dim(token_mask, col_index * col_count, col_count, 0).astype(
        jnp.float32
    )
    pair_live = row_live[:, None] * col_live[None, :]
    left_terms = jnp.einsum(
        "ijd,de->eij",
        pair_norm,
        tri_in_weight[:, : 2 * channels],
        preferred_element_type=jnp.float32,
    )
    left = (jax.nn.sigmoid(left_terms[channels:]) * left_terms[:channels] * pair_live).astype(
        jnp.bfloat16
    )
    right_terms = jnp.einsum(
        "ijd,de->eij",
        pair_norm,
        tri_in_weight[:, 2 * channels :],
        preferred_element_type=jnp.float32,
    )
    right = (jax.nn.sigmoid(right_terms[channels:]) * right_terms[:channels] * pair_live).astype(
        jnp.bfloat16
    )
    tri_gate = jax.nn.sigmoid(
        jnp.einsum("ijd,de->ije", pair_norm, tri_gate_weight, preferred_element_type=jnp.float32)
    )
    left_owned, right_owned = (
        lax.all_to_all(left, "row", split_axis=0, concat_axis=1, tiled=True),
        lax.all_to_all(right, "row", split_axis=0, concat_axis=1, tiled=True),
    )
    left_full, right_rows = (
        lax.all_gather(left_owned, "col", axis=2, tiled=True),
        lax.all_gather(right_owned, "col", axis=2, tiled=True),
    )
    right_used = lax.dynamic_slice_in_dim(right_rows, col_index * col_count, col_count, 1)
    tri_sum = jnp.einsum(
        "cik,cjk->cij", left_full, right_used, preferred_element_type=jnp.float32
    ).astype(jnp.bfloat16)
    merged = lax.all_to_all(tri_sum, "row", split_axis=1, concat_axis=0, tiled=True)
    tri_norm = layer_norm(merged.astype(jnp.float32), 0).astype(jnp.bfloat16)
    update = jnp.einsum("dij,de->ije", tri_norm, tri_out_weight, preferred_element_type=jnp.float32)
    pair_out = (pair_float + tri_gate * update).astype(jnp.bfloat16)
    band_width = 3 * tok_rows
    targets = (row_index - 1) * tok_rows + jnp.arange(band_width, dtype=jnp.int32)
    columns = col_index * col_count + jnp.arange(col_count, dtype=jnp.int32)
    selector = (columns[:, None] == targets[None, :]).astype(jnp.bfloat16)
    band_part = jnp.einsum("ijd,jb->ibd", pair_out, selector, preferred_element_type=jnp.float32)
    band = lax.psum(band_part.astype(jnp.bfloat16), "col").astype(jnp.float32)
    band_norm = layer_norm(band, 2).astype(jnp.bfloat16)
    bias_table = jnp.einsum(
        "ibd,dh->ibh", band_norm, bias_weight, preferred_element_type=jnp.float32
    ).astype(jnp.bfloat16)
    slab = atom_act.shape[0]
    window_width = atom_act.shape[1]
    heads = bias_weight.shape[1]
    head_size = window_width // heads
    side = (KEYS - QUERY_WINDOW) // 2
    windows = slab // QUERY_WINDOW
    local_token = atom_token - row_index * tok_rows
    live = atom_mask.astype(jnp.float32)
    token_tag = ((local_token + 1) * atom_mask).astype(jnp.bfloat16)
    ada = jnp.dot(atom_cond, ada_weight, preferred_element_type=jnp.float32)
    atom_inputs = (
        jax.nn.sigmoid(ada[:, :window_width]) * layer_norm(atom_act.astype(jnp.float32), 1)
        + ada[:, window_width:]
    ).astype(jnp.bfloat16)
    projected = jnp.dot(atom_inputs, qkv_weight, preferred_element_type=jnp.float32).astype(
        jnp.bfloat16
    )
    queries = projected[:, :window_width]
    ext_pairs, ext_tag = (
        extended(projected[:, window_width:], (("row", 0),), side),
        extended(token_tag, (("row", 0),), side),
    )
    ext_rows = slab + 2 * side
    ext_position = jnp.arange(ext_rows, dtype=jnp.int32)
    offset = jnp.where(
        ext_position < side, 0, jnp.where(ext_position < side + slab, tok_rows, 2 * tok_rows)
    )
    tag_value = ext_tag.astype(jnp.int32)
    key_valid = tag_value > 0
    band_index = tag_value - 1 + offset
    band_slots = jnp.arange(band_width, dtype=jnp.int32)
    key_onehot = ((band_index[:, None] == band_slots[None, :]) & key_valid[:, None]).astype(
        jnp.bfloat16
    )
    query_onehot = (local_token[:, None] == jnp.arange(tok_rows, dtype=jnp.int32)[None, :]).astype(
        jnp.bfloat16
    )
    query_bias = jnp.einsum(
        "lt,tbh->lbh", query_onehot, bias_table, preferred_element_type=jnp.float32
    ).astype(jnp.bfloat16)
    query_bias = query_bias.reshape(windows, QUERY_WINDOW, band_width, heads)
    key_index = (
        jnp.arange(windows, dtype=jnp.int32)[:, None] * QUERY_WINDOW
        + jnp.arange(KEYS, dtype=jnp.int32)[None, :]
    )
    window_pairs = ext_pairs[key_index]
    window_onehot = key_onehot[key_index]
    window_valid = key_valid[key_index]
    window_bias = jnp.einsum(
        "wlbh,wmb->whlm", query_bias, window_onehot, preferred_element_type=jnp.float32
    )
    query_heads = queries.reshape(windows, QUERY_WINDOW, heads, head_size)
    key_heads = window_pairs[..., :window_width].reshape(windows, KEYS, heads, head_size)
    value_heads = window_pairs[..., window_width:].reshape(windows, KEYS, heads, head_size)
    logit_scores = (
        jnp.einsum("wlhd,wmhd->whlm", query_heads, key_heads, preferred_element_type=jnp.float32)
        / math.sqrt(head_size)
        + window_bias
    )
    logit_scores = jnp.where(window_valid[:, None, None, :], logit_scores, -1e30)
    attn_weights = jax.nn.softmax(logit_scores, axis=-1).astype(jnp.bfloat16)
    attended = (
        jnp.einsum("whlm,wmhd->wlhd", attn_weights, value_heads, preferred_element_type=jnp.float32)
        .reshape(slab, window_width)
        .astype(jnp.bfloat16)
    )
    atom_mid = atom_act.astype(jnp.float32) + jnp.dot(
        attended, attn_out_weight, preferred_element_type=jnp.float32
    )
    atom_norm = layer_norm(atom_mid, 1).astype(jnp.bfloat16)
    expanded = jnp.dot(atom_norm, ffn_in_weight, preferred_element_type=jnp.float32)
    hidden_width = ffn_out_weight.shape[0]
    inner = (jax.nn.silu(expanded[:, :hidden_width]) * expanded[:, hidden_width:]).astype(
        jnp.bfloat16
    )
    atom_out = (
        (atom_mid + jnp.dot(inner, ffn_out_weight, preferred_element_type=jnp.float32))
        * live[:, None]
    ).astype(jnp.bfloat16)
    features = jax.nn.relu(
        jnp.dot(atom_out, agg_weight, preferred_element_type=jnp.float32)
    ).astype(jnp.bfloat16)
    live_onehot = query_onehot * atom_mask.astype(jnp.bfloat16)[:, None]
    token_sums = jnp.einsum("at,ac->tc", live_onehot, features, preferred_element_type=jnp.float32)
    token_counts = jnp.sum(live_onehot.astype(jnp.float32), axis=0)
    token_out = (token_sums / token_counts[:, None]).astype(jnp.bfloat16)
    return (pair_out, atom_out, token_out)


LANES = 128
SUBLANES = 8
SIDE = (KEYS - QUERY_WINDOW) // 2
RIM_ROWS = 4
BAND_PAD = 2 * SUBLANES
LIMIT = pltpu.CompilerParams(vmem_limit_bytes=8 << 20)
F32 = jnp.float32
BF16 = jnp.bfloat16
NT = (((1,), (1,)), ((), ()))
TN = (((0,), (0,)), ((), ()))
TT = (((0,), (1,)), ((), ()))


def matmul(a, b, dims=(((1,), (0,)), ((), ()))):
    return lax.dot_general(a, b, dims, preferred_element_type=F32)


def normalize(values, axis):
    average = jnp.mean(values, axis=axis, keepdims=True)
    centred = values - average
    spread = jnp.mean(centred * centred, axis=axis, keepdims=True)
    return centred * lax.rsqrt(spread + EPSILON)


def iota(shape, dim):
    return lax.broadcasted_iota(jnp.int32, shape, dim)


def column_of(row, size):
    eye = iota((size, size), 0) == iota((size, size), 1)
    return jnp.sum(jnp.where(eye, row, 0.0), axis=1, keepdims=True)


def pad_lanes(row):
    return jnp.concatenate([row, jnp.zeros((row.shape[0], LANES - row.shape[1]), row.dtype)], axis=1)


def strided(first, count, step):
    return pl.ds(first, count, stride=step)


def send_kernel(
    n_row, pair_hbm, act_hbm, bias_w_hbm, in_w_hbm, cond_hbm, ada_w_hbm, mask_hbm, token_hbm, alive_hbm,
    pair_ref, act_ref, bias_w_ref, out_ref, normed_ref, inputs_ref, slots_ref,
    in_w_ref, cond_ref, ada_w_ref, mask_ref, token_ref, alive_ref, staged, sems,
):
    sources = (pair_hbm, cond_hbm, act_hbm, mask_hbm, token_hbm, alive_hbm, bias_w_hbm, ada_w_hbm, in_w_hbm)
    places = (pair_ref, cond_ref, act_ref, mask_ref, token_ref, alive_ref, bias_w_ref, ada_w_ref, in_w_ref)
    loads = [pltpu.make_async_copy(a, b, sems.at[i]) for i, (a, b) in enumerate(zip(sources, places))]
    for load in loads:
        load.start()
    loads[0].wait()
    me = lax.axis_index("row")
    rows, cols, channels = pair_ref.shape
    part = channels // n_row
    width = rows * cols
    step = 2 * part * rows + RIM_ROWS
    normed = normalize(pair_ref[...].reshape(width, channels).astype(F32), 1).astype(BF16)
    normed_ref[...] = normed
    for load in loads[1:]:
        load.wait()
    live = mask_ref[...].astype(F32)
    lane = iota(live.shape, 1)
    both = jnp.concatenate(
        [live * jnp.sum(jnp.where(lane == me * rows + i, live, 0.0), axis=1, keepdims=True) for i in range(rows)],
        axis=1,
    )
    for side in range(2):
        first = 2 * side * channels
        value = matmul(in_w_ref[:, first : first + channels], normed, TT)
        gate = matmul(in_w_ref[:, first + channels : first + 2 * channels], normed, TT)
        term = jax.nn.sigmoid(gate) * value * both
        for q in range(part):
            for i in range(rows):
                staged[strided((side * part + q) * rows + i, n_row, step)] = term[
                    q * n_row : (q + 1) * n_row, i * cols : (i + 1) * cols
                ]
    act = act_ref[...].astype(F32)
    ada = matmul(cond_ref[...], ada_w_ref[...])
    slab, wide = act.shape
    inputs = (jax.nn.sigmoid(ada[:, :wide]) * normalize(act, 1) + ada[:, wide:]).astype(BF16)
    inputs_ref[...] = inputs
    inputs = inputs.astype(F32)
    token = token_ref[...] - me * rows
    alive = alive_ref[...]
    tag = pad_lanes(((token + 1) * alive).astype(F32))
    slots_ref[...] = jnp.zeros(slots_ref.shape, F32)
    slots_ref[0:1] = pad_lanes(token.astype(F32))
    slots_ref[1:2] = pad_lanes(alive.astype(F32))
    slots_ref[2:3] = tag
    tags = jnp.broadcast_to(tag, (2 * n_row - SIDE, LANES))
    for d, rim in enumerate((inputs[slab - SIDE :], inputs[:SIDE])):
        block = jnp.concatenate([rim, tags], axis=0)
        for s in range(RIM_ROWS // 2):
            staged[strided(step - RIM_ROWS + d * (RIM_ROWS // 2) + s, n_row, step)] = block[
                s * n_row : (s + 1) * n_row
            ]
    out_ref[...] = staged[...].astype(BF16)


def tables(inputs_ref, qkv_w_ref, slots_ref, act_ref, attn_w_ref, rows):
    slab, wide = inputs_ref.shape
    token = slots_ref[0:1, :slab]
    alive = slots_ref[1:2, :slab]
    own = matmul(inputs_ref[...], qkv_w_ref[...]).astype(BF16).astype(F32)
    token_col = column_of(token, slab)
    live_col = column_of(alive, slab)
    query_hot = (token_col == (iota((slab, rows * BAND_PAD), 1) // BAND_PAD).astype(F32)).astype(F32)
    members = [jnp.broadcast_to(jnp.where(token_col == t, live_col, 0.0), (slab, LANES)) for t in range(rows)]
    counts = jnp.sum(jnp.where(iota((SUBLANES, slab), 0).astype(F32) == token, alive, 0.0), axis=1, keepdims=True)
    act_mean = jnp.mean(act_ref[...].astype(F32), axis=1, keepdims=True)
    attn_w = attn_w_ref[...]
    pieces = [attn_w]
    rest = jnp.broadcast_to(jnp.mean(attn_w.astype(F32), axis=1, keepdims=True), attn_w.shape)
    for _ in range(3):
        pieces.append(rest.astype(BF16))
        rest = rest - pieces[-1].astype(F32)
    attn_wide = jnp.concatenate(pieces, axis=1)
    return own, query_hot, live_col, members, jnp.maximum(counts, 1.0), act_mean, attn_wide


def triangle_kernel(n_row, rows, got_ref, normed_ref, gate_w_ref, out_ref, gate_ref, taken, right_terms, staged):
    gate_ref[...] = jax.nn.sigmoid(matmul(normed_ref[...], gate_w_ref[...]))
    taken[...] = got_ref[...].astype(F32)
    step = got_ref.shape[0] // n_row
    part = right_terms.shape[0]
    out_step = part * rows + RIM_ROWS
    for q in range(part):
        left = jnp.concatenate(
            [taken[strided(q * rows + i, n_row, step)] for i in range(rows)], axis=0
        ).astype(BF16)
        for j in range(rows):
            right_terms[q, strided(j, n_row, rows)] = taken[strided((part + q) * rows + j, n_row, step)]
        summed = matmul(left, right_terms[q].astype(BF16), NT)
        for i in range(rows):
            staged[strided(q * rows + i, n_row, out_step)] = summed[i * n_row : (i + 1) * n_row]
    nothing = jnp.zeros((1, LANES), F32)
    for s in range(RIM_ROWS):
        rim = taken[strided(step - RIM_ROWS + s, n_row, step)]
        if s < RIM_ROWS // 2:
            rim = jnp.concatenate([nothing, rim[:-1]], axis=0)
        else:
            rim = jnp.concatenate([rim[1:], nothing], axis=0)
        staged[strided(out_step - RIM_ROWS + s, n_row, out_step)] = rim
    out_ref[...] = staged[...].astype(BF16)


def finish_kernel(
    n_row, got_ref, pair_ref, out_w_ref, act_ref, slots_ref, bias_w_ref, gate_ref, inputs_ref, qkv_w_ref, attn_w_ref,
    ffn_in_ref, ffn_out_ref, agg_ref,
    pair_out, atom_out, token_out, taken, pair_new, atom_new, token_new, padded, sems,
):
    me = lax.axis_index("row")
    rows, cols, channels = pair_ref.shape
    part = channels // n_row
    step = part * rows + RIM_ROWS
    half = RIM_ROWS // 2
    slab, wide = act_ref.shape
    heads = bias_w_ref.shape[0]
    head_size = wide // heads
    taken[...] = got_ref[...].astype(F32)
    for i in range(rows):
        sums = jnp.concatenate([taken[strided(q * rows + i, n_row, step)] for q in range(part)], axis=0)
        update = matmul(normalize(sums, 0).astype(BF16), out_w_ref[...], TN)
        fresh = (pair_ref[i].astype(F32) + gate_ref[i * cols : (i + 1) * cols] * update).astype(BF16)
        pair_new[i] = fresh
        padded[i, :SUBLANES] = jnp.zeros((SUBLANES, channels), F32)
        padded[i, SUBLANES : SUBLANES + cols] = fresh.astype(F32)
        padded[i, SUBLANES + cols :] = jnp.zeros((BAND_PAD, channels), F32)
    pair_copy = pltpu.make_async_copy(pair_new, pair_out, sems.at[0])
    atom_copy = pltpu.make_async_copy(atom_new, atom_out, sems.at[1])
    token_copy = pltpu.make_async_copy(token_new, token_out, sems.at[2])
    pair_copy.start()

    @pl.when(me >= 0)
    def _():
        band = [padded[i, pl.ds(SUBLANES + (me - 1) * rows, BAND_PAD)] for i in range(rows)]
        band = normalize(jnp.concatenate(band, axis=0), 1).astype(BF16)
        bias_rows = matmul(bias_w_ref[...], band, NT).astype(BF16).astype(F32)
        own, query_hot, live_col, members, counts, act_mean, attn_wide = tables(
            inputs_ref, qkv_w_ref, slots_ref, act_ref, attn_w_ref, rows
        )
        outer = jnp.concatenate(
            [
                taken[strided(step - RIM_ROWS + d * half + s, n_row, step)][: min(n_row, SIDE - s * n_row)]
                for d in range(2)
                for s in range(half)
            ],
            axis=0,
        ).astype(BF16)
        outer = matmul(outer, qkv_w_ref[:, wide:]).astype(BF16).astype(F32)
        keys_ext, values_ext = (
            jnp.concatenate(
                [outer[:SIDE, at : at + wide], own[:, wide + at : 2 * wide + at], outer[SIDE:, at : at + wide]], axis=0
            ).astype(BF16)
            for at in (0, wide)
        )
        tag_at = [(step - RIM_ROWS + d * half + SIDE // n_row) + step * (SIDE % n_row) for d in range(2)]
        before_tag, after_tag = (taken[at : at + 1] for at in tag_at)
        own_tag = slots_ref[2:3]
        lane = iota((1, LANES), 1)
        flat = query_hot.shape[1]
        slot = (iota((flat, KEYS), 0) % BAND_PAD).astype(F32)
        head_of = iota((QUERY_WINDOW, wide), 1) // head_size
        mixed = []
        for w in range(slab // QUERY_WINDOW):
            start = w * QUERY_WINDOW
            before_end = SIDE - start
            own_end = before_end + slab
            is_before, is_own = lane < before_end, lane < own_end
            tag = jnp.where(
                is_before,
                pltpu.roll(before_tag, (SIDE - slab - start) % LANES, 1),
                jnp.where(
                    is_own, pltpu.roll(own_tag, before_end % LANES, 1), pltpu.roll(after_tag, own_end % LANES, 1)
                ),
            )
            offset = jnp.where(is_before, 0.0, jnp.where(is_own, 1.0 * rows, 2.0 * rows))
            valid = tag > 0
            key_slot = jnp.where(valid, tag - 1 + offset, -1.0)
            key_hot = (slot == key_slot).astype(BF16)
            query = own[start : start + QUERY_WINDOW, :wide]
            split = jnp.concatenate([jnp.where(head_of == h, query, 0.0) for h in range(heads)], axis=0).astype(BF16)
            product = matmul(split, keys_ext[start : start + KEYS], NT) * (1 / math.sqrt(head_size))
            product = jnp.where(valid, product, -1e30)
            product = product - jnp.max(product, axis=1, keepdims=True)
            hot = query_hot[start : start + QUERY_WINDOW]
            hot_bias = jnp.concatenate([hot * bias_rows[h : h + 1] for h in range(heads)], axis=0).astype(BF16)
            powers = jnp.exp(product + matmul(hot_bias, key_hot))
            blend = matmul(powers.astype(BF16), values_ext[start : start + KEYS])
            blend = blend / jnp.sum(powers, axis=1, keepdims=True)
            total = jnp.zeros((QUERY_WINDOW, wide), F32)
            for h in range(heads):
                total = jnp.where(head_of == h, blend[h * QUERY_WINDOW : (h + 1) * QUERY_WINDOW], total)
            mixed.append(total)
        attended = jnp.concatenate(mixed, axis=0).astype(BF16)
        mixture = matmul(attended, attn_wide)
        middle = act_ref[...].astype(F32) + mixture[:, :wide]
        shift = mixture[:, wide : 2 * wide] + mixture[:, 2 * wide : 3 * wide] + mixture[:, 3 * wide :]
        centred = middle - (act_mean + shift)
        spread = jnp.mean(centred * centred, axis=1, keepdims=True)
        expanded = matmul(centred.astype(BF16), ffn_in_ref[...]) * lax.rsqrt(spread + EPSILON)
        hidden = ffn_out_ref.shape[0]
        inner = (jax.nn.silu(expanded[:, :hidden]) * expanded[:, hidden:]).astype(BF16)
        final = ((middle + matmul(inner, ffn_out_ref[...])) * live_col).astype(BF16)
        atom_new[...] = final
        atom_copy.start()
        features = jnp.maximum(matmul(final, agg_ref[...]), 0.0).astype(BF16).astype(F32)
        for b in range(features.shape[1] // LANES):
            block = features[:, b * LANES : (b + 1) * LANES]
            totals = [jnp.sum(block * members[t], axis=0, keepdims=True) for t in range(rows)]
            token_new[:, b * LANES : (b + 1) * LANES] = (
                jnp.concatenate(totals, axis=0) / counts[:rows]
            ).astype(BF16)
        token_copy.start()

    pair_copy.wait()
    atom_copy.wait()
    token_copy.wait()


def in_vmem(count):
    return [pl.BlockSpec(memory_space=pltpu.VMEM)] * count


def in_hbm(arrays):
    return [pltpu.with_memory_space_constraint(a, pltpu.HBM) for a in arrays]


def cost(flops, nbytes, exps=0):
    return pl.CostEstimate(flops=flops, bytes_accessed=nbytes, transcendentals=exps)


def exchange(blocks, n_row):
    grouped = blocks.reshape(n_row, -1, RIM_ROWS, LANES)
    return lax.all_to_all(grouped, "row", split_axis=0, concat_axis=0, tiled=True).reshape(blocks.shape)


def by_kernels(
    pair, token_mask, tri_in_weight, tri_gate_weight, tri_out_weight, atom_act, atom_cond, atom_token, atom_mask,
    ada_weight, qkv_weight, bias_weight, attn_out_weight, ffn_in_weight, ffn_out_weight, agg_weight,
):
    n_row = lax.axis_size("row")
    rows, cols, channels = pair.shape
    slab, wide = atom_act.shape
    width = rows * cols
    part = channels // n_row
    mask = token_mask.reshape(1, -1)
    token = atom_token.reshape(1, -1)
    alive = atom_mask.reshape(1, -1)
    sent = n_row * (2 * part * rows + RIM_ROWS)
    back_rows = n_row * (part * rows + RIM_ROWS)
    sources = (pair, atom_act, bias_weight.T, tri_in_weight, atom_cond, ada_weight, mask, token, alive)
    kept = 3
    pair, atom_act, bias_rows, terms, normed, inputs, slots = pl.pallas_call(
        functools.partial(send_kernel, n_row),
        out_shape=(
            *(jax.ShapeDtypeStruct(a.shape, a.dtype) for a in sources[:kept]),
            jax.ShapeDtypeStruct((sent, LANES), BF16),
            jax.ShapeDtypeStruct((width, channels), BF16),
            jax.ShapeDtypeStruct((slab, wide), BF16),
            jax.ShapeDtypeStruct((SUBLANES, LANES), F32),
        ),
        in_specs=[pl.BlockSpec(memory_space=pltpu.HBM)] * len(sources),
        out_specs=tuple(in_vmem(kept + 4)),
        scratch_shapes=[
            *(pltpu.VMEM(a.shape, a.dtype) for a in sources[kept:]),
            pltpu.VMEM((sent, LANES), F32),
            pltpu.SemaphoreType.DMA((len(sources),)),
        ],
        cost_estimate=cost(8 * width * channels * channels, 1 << 20, 2 * width * channels),
        compiler_params=LIMIT,
        name="send",
    )(*in_hbm(sources))
    got = exchange(terms, n_row)
    sums, gate = pl.pallas_call(
        functools.partial(triangle_kernel, n_row, rows),
        out_shape=(
            jax.ShapeDtypeStruct((back_rows, LANES), BF16),
            jax.ShapeDtypeStruct((width, channels), F32),
        ),
        in_specs=in_vmem(3),
        out_specs=tuple(in_vmem(2)),
        scratch_shapes=[
            pltpu.VMEM((sent, LANES), F32),
            pltpu.VMEM((part, cols, cols), F32),
            pltpu.VMEM((back_rows, LANES), F32),
        ],
        cost_estimate=cost(2 * width * width, 1 << 19),
        compiler_params=LIMIT,
        name="triangle",
    )(got, normed, tri_gate_weight)
    back = exchange(sums, n_row)
    token_shape = (rows, agg_weight.shape[1])
    return pl.pallas_call(
        functools.partial(finish_kernel, n_row),
        out_shape=(
            jax.ShapeDtypeStruct(pair.shape, BF16),
            jax.ShapeDtypeStruct(atom_act.shape, BF16),
            jax.ShapeDtypeStruct(token_shape, BF16),
        ),
        in_specs=in_vmem(13),
        out_specs=(pl.BlockSpec(memory_space=pltpu.HBM),) * 3,
        scratch_shapes=[
            pltpu.VMEM((back_rows, LANES), F32),
            pltpu.VMEM(pair.shape, BF16),
            pltpu.VMEM(atom_act.shape, BF16),
            pltpu.VMEM(token_shape, BF16),
            pltpu.VMEM((rows, SUBLANES + cols + BAND_PAD, channels), F32),
            pltpu.SemaphoreType.DMA((3,)),
        ],
        cost_estimate=cost(4 * width * channels * channels, 1 << 20),
        compiler_params=LIMIT,
        name="finish",
    )(
        back, pair, tri_out_weight, atom_act, slots, bias_rows, gate, inputs, qkv_weight, attn_out_weight,
        ffn_in_weight, ffn_out_weight, agg_weight,
    )


def kernels_fit(mesh, args):
    pair, atom_act, bias_weight = args[0], args[5], args[11]
    n_row = mesh.shape["row"]
    parts = mesh.shape["groups"] * n_row
    cols, channels = pair.shape[1:]
    rows = pair.shape[0] // parts
    slab = atom_act.shape[0] // parts
    wide = atom_act.shape[1]
    return (
        mesh.shape["col"] == 1
        and cols == channels == wide == LANES
        and cols == n_row * rows
        and channels % n_row == 0
        and n_row % SUBLANES == 0
        and SIDE < RIM_ROWS // 2 * n_row
        and 3 * rows <= BAND_PAD
        and rows <= SUBLANES
        and slab // QUERY_WINDOW <= SUBLANES
        and SIDE <= slab <= LANES
        and slab % QUERY_WINDOW == 0
        and slab - QUERY_WINDOW <= SIDE
        and wide % bias_weight.shape[1] == 0
    )


def solution(mesh):
    in_specs = (
        P(("groups", "row"), "col", None),
        P("groups"),
        P(),
        P(),
        P(),
        P(("groups", "row"), None),
        P(("groups", "row"), None),
        P(("groups", "row")),
        P(("groups", "row")),
        P(),
        P(),
        P(),
        P(),
        P(),
        P(),
        P(),
    )
    out_specs = (
        P(("groups", "row"), "col", None),
        P(("groups", "row"), None),
        P(("groups", "row"), None),
    )

    def layer(*args):
        body = by_kernels if kernels_fit(mesh, args) else per_device
        return jax.shard_map(body, mesh=mesh, in_specs=in_specs, out_specs=out_specs, check_vma=False)(*args)

    return layer
```
